32 devices in a mesh: dp: 8 (over z, y), upd: 4 (over x, core).
Axes of the slice: x: 2, y: 2, z: 4, core: 2. Of those that a mesh axis runs over, the one named last changes fastest.
Arguments:
- inputs: bfloat16 [256, 128, 768], P(('dp', 'upd')), may hold values from -6 to 6
- memory: bfloat16 [256, 256, 768], P(('dp', 'upd')), may hold values from -6 to 6
- cotangent: bfloat16 [256, 128, 768], P(('dp', 'upd')), may hold values from -6 to 6
- lengths: int32 [256], P(('dp', 'upd')), may hold values from 1 to 128, as said below
- memory_len: int32 [256], P(('dp', 'upd')), may hold values from 64 to 225, as said below
- square_master: float32 [8, 768, 768], P(None, ('dp', 'upd')), may hold values from -0.21875 to 0.21875
- tall_master: float32 [2, 3072, 768], P(None, ('dp', 'upd'))
- square_momentum: float32 [8, 768, 768], P(None, ('dp', 'upd'))
- tall_momentum: float32 [2, 3072, 768], P(None, ('dp', 'upd'))
- vectors: bfloat16 [17, 768], replicated, may hold values from -1.5 to 1.5
- feed_vectors: bfloat16 [3, 3072], replicated, may hold values from -1.5 to 1.5
- head_scale: bfloat16 [12], replicated, may hold values from 0.25 to 1.75
- relative: bfloat16 [12, 128], replicated, may hold values from -4 to 4
Outputs:
- output: bfloat16 [256, 128, 768], P(('dp', 'upd'))
- input_gradient: bfloat16 [256, 128, 768], P(('dp', 'upd'))
- memory_gradient: bfloat16 [256, 256, 768], P(('dp', 'upd'))
- square_state: float32 [8, 768, 768], P(None, ('dp', 'upd'))
- tall_state: float32 [2, 3072, 768], P(None, ('dp', 'upd'))
- square_weight: float32 [8, 768, 768], P(None, ('dp', 'upd'))
- tall_weight: float32 [2, 3072, 768], P(None, ('dp', 'upd'))
- vector_gradient: float32 [17, 768], P(None, ('dp', 'upd'))
- feed_gradient: float32 [3, 3072], P(None, ('dp', 'upd'))
- scale_gradient: float32 [12], replicated
- bias_gradient: float32 [12, 128], replicated
The draws below stay inside these ranges and needn't reach their ends.
Inputs may be any that keep to these rules, and one draw needn't show every extreme that they name: `lengths`: positions at or past an item's count are padding; some item has exactly 128. `memory_len`: each item has 64 or 225 real memory rows, the first ones; both occur.
All inputs are finite; a program needn't handle non-finite values.
Results may differ from the reference program's by a relative error of at most 0.02.
Values may be sent and summed in bfloat16 or wider, within the bound.
A program may use at most 384 MiB of HBM per device.

```python
import jax
import jax.numpy as jnp
from jax import lax

D = 768
FF = 3072
HEADS = 12
SEQ = 128
MEM = 256
MEM_SHORT = 64
MEM_LONG = 225
ITERS = 5
ITEMS_DEV = 8
ITEMS = 256


def draw_lengths(key, part):
    devices = ITEMS // ITEMS_DEV
    index = jnp.arange(ITEMS)
    device = index // ITEMS_DEV
    low_end = SEQ // 3
    center = low_end + (SEQ - low_end) * device // max(devices - 1, 1)
    jitter = jax.random.randint(key, (ITEMS,), -(SEQ // 8), SEQ // 8 + 1)
    drawn = jnp.clip(center + jitter, 1, SEQ)
    return jnp.where(index == ITEMS - 1, SEQ, drawn).astype(jnp.int32)


def draw_memory_len(key, part):
    index = jnp.arange(ITEMS)
    coin = jax.random.randint(key, (ITEMS,), 0, 2)
    coin = jnp.where(index == 0, 1, jnp.where(index == 1, 0, coin))
    return jnp.where(coin == 1, MEM_LONG, MEM_SHORT).astype(jnp.int32)


def draw_tall_master(key, part):
    values = jnp.clip(jax.random.normal(key, (2, FF, D), jnp.float32), -5.0, 5.0)
    scales = jnp.array([D ** (-0.5), FF ** (-0.5)], jnp.float32)
    return values * scales[:, None, None]


def momentum_size():
    return 0.5 * (1.5 * ITEMS / SEQ) ** 0.5


def draw_square_momentum(key, part):
    return momentum_size() * jnp.clip(jax.random.normal(key, (8, D, D), jnp.float32), -5.0, 5.0)


def draw_tall_momentum(key, part):
    return momentum_size() * jnp.clip(jax.random.normal(key, (2, FF, D), jnp.float32), -5.0, 5.0)


def mixed_rows(key, rows, width, gain_rows):
    first, second = jax.random.split(key)
    gains = jnp.clip(1.0 + 0.15 * jax.random.normal(first, (rows, width), jnp.float32), 0.5, 1.5)
    shifts = jnp.clip(0.3 * jax.random.normal(second, (rows, width), jnp.float32), -1.5, 1.5)
    return jnp.where(gain_rows[:, None] == 1, gains, shifts)


def draw_vectors(key, part):
    gain_rows = jnp.array([1, 0, 0, 0, 0, 1, 0, 1, 0, 0, 0, 0, 1, 0, 1, 0, 0], jnp.int32)
    return mixed_rows(key, 17, D, gain_rows).astype(jnp.bfloat16)


def draw_feed_vectors(key, part):
    gain_rows = jnp.array([0, 1, 0], jnp.int32)
    return mixed_rows(key, 3, FF, gain_rows).astype(jnp.bfloat16)


def strengthened(values, own_key, source, target, blocks, factor):
    def block_of(axis_at):
        return (jnp.arange(values.shape[axis_at]) // (values.shape[axis_at] // blocks)).reshape((-1,) + (1,) * (values.ndim - 1 - axis_at))

    first = jax.random.permutation(own_key, blocks)[block_of(target)]
    second = (block_of(target) + blocks // 2) % blocks
    return jnp.where((block_of(source) == first) | (block_of(source) == second), factor * values, values)


def block_levels(rng, shape, pieces, low, high):
    loudness, own = 1.0, jax.random.fold_in(rng, 6)
    for position, shards_of in pieces:
        draws = jnp.exp(jax.random.uniform(jax.random.fold_in(own, position), (shards_of,), jnp.float32, low / len(pieces), high / len(pieces)))
        loudness = loudness * jnp.repeat(draws, shape[position] // shards_of).reshape([-1 if axis == position else 1 for axis in range(len(shape))])
    return loudness


def noise(stream_key, shape, scale, limit, shards=(), held_as=jnp.bfloat16):
    values = jax.random.normal(stream_key, shape, jnp.float32) * scale
    if len(shards) > 0:
        values = block_levels(stream_key, shape, shards, -0.22, 0.18) * values
    return jnp.clip(values, min=-limit, max=limit).astype(held_as)


def heavy_noise(key, shape, scale, limit, cuts, heavy, held_as=jnp.bfloat16):
    values = scale * jax.random.normal(key, shape, jnp.float32)
    if cuts:
        values = values * block_levels(key, shape, cuts, -0.22, 0.18)
    return jnp.clip(strengthened(values, jax.random.fold_in(key, 3), *heavy), -limit, limit).astype(held_as)


def setup_inputs(seed: int = 0) -> dict:
    key_of = jax.random.split(jax.random.key(seed), 14)
    inputs = noise(key_of[0], (ITEMS, SEQ, D), 1.0, 6.0, ((0, 32),))
    memory = noise(key_of[1], (ITEMS, MEM, D), 1.0, 6.0, ((0, 32),))
    cotangent = heavy_noise(key_of[2], (ITEMS, SEQ, D), 1.0, 6.0, ((0, 32),), (0, 2, 32, 2.75))
    lengths = draw_lengths(jax.random.fold_in(key_of[13], 71), 0)
    memory_len = draw_memory_len(jax.random.fold_in(key_of[13], 71), 0)
    square_master = noise(key_of[5], (8, D, D), D ** -0.5, 0.21875, ((1, 32),), jnp.float32)
    tall_master = draw_tall_master(jax.random.fold_in(key_of[13], 71), 0)
    square_momentum = draw_square_momentum(jax.random.fold_in(key_of[13], 71), 0)
    tall_momentum = draw_tall_momentum(jax.random.fold_in(key_of[13], 71), 0)
    vectors = draw_vectors(jax.random.fold_in(key_of[13], 71), 0)
    feed_vectors = draw_feed_vectors(jax.random.fold_in(key_of[13], 71), 0)
    head_scale = jnp.clip(1.0 + 0.15 * jax.random.normal(key_of[11], (HEADS,), jnp.float32), 0.25, 1.75).astype(jnp.bfloat16)
    relative = noise(key_of[12], (HEADS, SEQ), 1.0, 4.0)
    return {"inputs": inputs, "memory": memory, "cotangent": cotangent, "lengths": lengths, "memory_len": memory_len, "square_master": square_master, "tall_master": tall_master, "square_momentum": square_momentum, "tall_momentum": tall_momentum, "vectors": vectors, "feed_vectors": feed_vectors, "head_scale": head_scale, "relative": relative}


@jax.custom_vjp
def low(v):
    return lax.optimization_barrier(v.astype(jnp.bfloat16)).astype(jnp.float32)

@jax.custom_vjp
def low_back(v):
    return v

def low_keep(v):
    return (low(v), None)

def low_pass(kept, grad):
    return (grad,)

def back_keep(v):
    return (v, None)

def back_low(kept, grad):
    return (low(grad),)
low.defvjp(low_keep, low_pass)
low_back.defvjp(back_keep, back_low)
NORM_EPSILON = 1e-05
FLOOR_EPSILON = 1e-07
FIRST_TERM = 3.4445
SECOND_TERM = -4.775
THIRD_TERM = 2.0315
MOMENTUM_DECAY = 0.95
LEARN_RATE = 0.8
WEIGHT_DECAY = 0.01
NEGATIVE_LARGE = -1e+30

def product(left, right):
    return jnp.matmul(left, right, precision=lax.Precision.HIGHEST)

def norm_rows(values, gain, shift):
    center = values - lax.optimization_barrier(jnp.mean(values, axis=-1, keepdims=True))
    spread = lax.optimization_barrier(jnp.mean(center * center, axis=-1, keepdims=True))
    return center * lax.rsqrt(spread + NORM_EPSILON) * gain + shift

def attend(query, keys, values, allowed, bias):
    scores = jnp.einsum('bqhe,bkhe->bhqk', query, keys, precision=lax.Precision.HIGHEST) + bias
    scores = jnp.where(allowed, low_back(scores), NEGATIVE_LARGE)
    weights = jnp.exp(scores - lax.optimization_barrier(jnp.max(scores, axis=-1, keepdims=True)))
    weights = low(weights / lax.optimization_barrier(jnp.sum(weights, axis=-1, keepdims=True)))
    return low_back(jnp.einsum('bhqk,bkhe->bqhe', weights, values, precision=lax.Precision.HIGHEST))

def split_heads(values, head_count):
    return values.reshape(values.shape[0], values.shape[1], head_count, values.shape[2] // head_count)

def layer_block(inputs, memory, memory_len, square, tall, vectors, feed_vectors, head_scale, relative):
    item_count, query_count, model_width = inputs.shape
    head_count = head_scale.shape[0]
    memory_slots = memory.shape[1]
    normed = low(norm_rows(inputs, vectors[0], vectors[1]))
    query = low_back(low((product(normed, square[0]) + vectors[2]) * 0.125))
    keys = low_back(low(product(normed, square[1])))
    values = low_back(low(product(normed, square[2]) + vectors[3]))
    query_index = jnp.arange(query_count).astype(jnp.int32)[:, None]
    key_index = jnp.arange(query_count).astype(jnp.int32)[None, :]
    distance = jnp.clip(query_index - key_index, 0, query_count - 1).astype(jnp.int32)
    bias = relative[:, distance][None]
    mixed = attend(split_heads(query, head_count), split_heads(keys, head_count), split_heads(values, head_count), (query_index >= key_index)[None, None], bias)
    mixed = (mixed * head_scale[None, None, :, None]).reshape(item_count, query_count, model_width)
    mixed = low(norm_rows(mixed, vectors[5], vectors[6]))
    hidden = inputs + low_back(product(mixed, square[3]) + vectors[4])
    normed = low(norm_rows(hidden, vectors[7], vectors[8]))
    query = low_back(low((product(normed, square[4]) + vectors[9]) * 0.125))
    keys = low_back(low(product(memory, square[5])))
    values = low_back(low(product(memory, square[6]) + vectors[10]))
    allowed = (jnp.arange(memory_slots).astype(jnp.int32)[None, :] < memory_len[:, None])[:, None, None, :]
    mixed = attend(split_heads(query, head_count), split_heads(keys, head_count), split_heads(values, head_count), allowed, 0.0)
    mixed = low(norm_rows(mixed.reshape(item_count, query_count, model_width), vectors[12], vectors[13]))
    hidden = hidden + low_back(product(mixed, square[7]) + vectors[11])
    normed = low(norm_rows(hidden, vectors[14], vectors[15]))
    inner = low_back(product(normed, tall[0].T) + feed_vectors[0])
    active = low(norm_rows(jax.nn.gelu(inner, approximate=False), feed_vectors[1], feed_vectors[2]))
    return hidden + low_back(product(active, tall[1]) + vectors[16])

def orthogonal(matrix):
    current = matrix * (1.0 / (jnp.sqrt(jnp.sum(matrix * matrix)) + FLOOR_EPSILON))
    for sweep in range(ITERS):
        gram = product(current.T, current)
        mixed = product(current, gram)
        current = FIRST_TERM * current + SECOND_TERM * mixed + THIRD_TERM * product(mixed, gram)
    return current

def reference(inputs, memory, cotangent, lengths, memory_len, square_master, tall_master, square_momentum, tall_momentum, vectors, feed_vectors, head_scale, relative):
    params = (square_master.astype(jnp.bfloat16).astype(jnp.float32), tall_master.astype(jnp.bfloat16).astype(jnp.float32), vectors.astype(jnp.float32), feed_vectors.astype(jnp.float32), head_scale.astype(jnp.float32), relative.astype(jnp.float32))
    groups = ITEMS // ITEMS_DEV

    def run_all(params, inputs_all, memory_all):

        def one_group(packed):
            group_in, group_memory, group_len = packed
            return layer_block(group_in, group_memory, group_len, *params)
        packed = (inputs_all.reshape(groups, ITEMS_DEV, SEQ, D), memory_all.reshape(groups, ITEMS_DEV, MEM, D), memory_len.reshape(groups, ITEMS_DEV))
        return lax.map(jax.checkpoint(one_group), packed).reshape(ITEMS, SEQ, D)
    output, pullback = jax.vjp(run_all, params, inputs.astype(jnp.float32), memory.astype(jnp.float32))
    valid = (jnp.arange(SEQ).astype(jnp.int32)[None, :] < lengths[:, None]).astype(jnp.float32)
    param_slopes, input_slope, memory_slope = pullback(cotangent.astype(jnp.float32) * valid[:, :, None])
    square_slope, tall_slope, vector_slope, feed_slope, scale_slope, bias_slope = param_slopes
    total = jnp.sum(lengths).astype(jnp.float32)
    factor = ITEMS / total
    square_state = MOMENTUM_DECAY * square_momentum + factor * square_slope
    tall_state = MOMENTUM_DECAY * tall_momentum + factor * tall_slope
    square_weight = square_master * (1.0 - LEARN_RATE * WEIGHT_DECAY) - LEARN_RATE * jax.vmap(orthogonal)(square_state)
    tall_weight = tall_master * (1.0 - LEARN_RATE * WEIGHT_DECAY) - LEARN_RATE * max(1.0, FF / D) ** 0.5 * jax.vmap(orthogonal)(tall_state)
    return (output.astype(jnp.bfloat16), input_slope.astype(jnp.bfloat16), memory_slope.astype(jnp.bfloat16), square_state, tall_state, square_weight, tall_weight, factor * vector_slope, factor * feed_slope, factor * scale_slope, factor * bias_slope)
```

```python
import jax
import jax.numpy as jnp
from jax import lax
from jax.sharding import Mesh, PartitionSpec as P

D = 768
FF = 3072
ITERS = 5


NORM_EPSILON = 1e-05
FLOOR_EPSILON = 1e-07
FIRST_TERM = 3.4445
SECOND_TERM = -4.775
THIRD_TERM = 2.0315
MOMENTUM_DECAY = 0.95
LEARN_RATE = 0.8
WEIGHT_DECAY = 0.01
NEGATIVE_LARGE = -1e30


def plain_round(values):
    return lax.optimization_barrier(values.astype(jnp.bfloat16)).astype(jnp.float32)


def same_value(values):
    return values


def value_keep(values):
    return (plain_round(values), None)


def value_pass(kept, slope):
    return (slope,)


def gradient_keep(values):
    return (values, None)


def gradient_round(kept, slope):
    return (plain_round(slope),)


def round_value(values):
    wrapped = jax.custom_vjp(plain_round)
    wrapped.defvjp(value_keep, value_pass)
    return wrapped(values)


def round_gradient(values):
    wrapped = jax.custom_vjp(same_value)
    wrapped.defvjp(gradient_keep, gradient_round)
    return wrapped(values)


def norm_rows(values, gain, shift):
    center = values - jnp.mean(values, axis=-1, keepdims=True)
    spread = jnp.mean(center * center, axis=-1, keepdims=True)
    return center * lax.rsqrt(spread + NORM_EPSILON) * gain + shift


def attend(query, keys, values, allowed, bias):
    scores = jnp.einsum("bqhe,bkhe->bhqk", query, keys) + bias
    scores = jnp.where(allowed, round_gradient(scores), NEGATIVE_LARGE)
    weights = jnp.exp(scores - jnp.max(scores, axis=-1, keepdims=True))
    weights = round_value(weights / jnp.sum(weights, axis=-1, keepdims=True))
    return round_gradient(jnp.einsum("bhqk,bkhe->bqhe", weights, values))


def split_heads(values, head_count):
    return values.reshape(
        values.shape[0], values.shape[1], head_count, values.shape[2] // head_count
    )


def layer_block(
    inputs, memory, memory_len, square, tall, vectors, feed_vectors, head_scale, relative
):
    item_count, query_count, model_width = inputs.shape
    head_count = head_scale.shape[0]
    memory_slots = memory.shape[1]
    normed = round_value(norm_rows(inputs, vectors[0], vectors[1]))
    query = round_gradient(round_value((jnp.matmul(normed, square[0]) + vectors[2]) * 0.125))
    keys = round_gradient(round_value(jnp.matmul(normed, square[1])))
    values = round_gradient(round_value(jnp.matmul(normed, square[2]) + vectors[3]))
    query_index = jnp.arange(query_count)[:, None]
    key_index = jnp.arange(query_count)[None, :]
    distance = jnp.clip(query_index - key_index, 0, query_count - 1)
    position_table = (distance[:, :, None] == jnp.arange(query_count)[None, None, :]).astype(
        jnp.float32
    )
    bias = jnp.einsum("hd,qkd->hqk", relative, position_table)[None]
    mixed = attend(
        split_heads(query, head_count),
        split_heads(keys, head_count),
        split_heads(values, head_count),
        (query_index >= key_index)[None, None],
        bias,
    )
    mixed = (mixed * head_scale[None, None, :, None]).reshape(item_count, query_count, model_width)
    mixed = round_value(norm_rows(mixed, vectors[5], vectors[6]))
    hidden = inputs + round_gradient(jnp.matmul(mixed, square[3]) + vectors[4])
    normed = round_value(norm_rows(hidden, vectors[7], vectors[8]))
    query = round_gradient(round_value((jnp.matmul(normed, square[4]) + vectors[9]) * 0.125))
    keys = round_gradient(round_value(jnp.matmul(memory, square[5])))
    values = round_gradient(round_value(jnp.matmul(memory, square[6]) + vectors[10]))
    allowed = (jnp.arange(memory_slots)[None, :] < memory_len[:, None])[:, None, None, :]
    mixed = attend(
        split_heads(query, head_count),
        split_heads(keys, head_count),
        split_heads(values, head_count),
        allowed,
        0.0,
    )
    mixed = round_value(
        norm_rows(mixed.reshape(item_count, query_count, model_width), vectors[12], vectors[13])
    )
    hidden = hidden + round_gradient(jnp.matmul(mixed, square[7]) + vectors[11])
    normed = round_value(norm_rows(hidden, vectors[14], vectors[15]))
    inner = round_gradient(jnp.matmul(normed, tall[0].T) + feed_vectors[0])
    active = round_value(
        norm_rows(jax.nn.gelu(inner, approximate=False), feed_vectors[1], feed_vectors[2])
    )
    return hidden + round_gradient(jnp.matmul(active, tall[1]) + vectors[16])


AXES = ("tall", "square", "row")


def matmul3(left, right):
    return jnp.matmul(left, right, precision=lax.Precision.HIGH)


def to_owner_rows(square_state, tall_state, count):
    rows = square_state.shape[1]
    group = count // 16
    if rows % group == 0:
        piece = rows // group
        pieces = jnp.concatenate(
            [
                square_state.reshape(8 * group, piece, D),
                tall_state.reshape(8 * group, piece, D),
            ],
            axis=0,
        ).astype(jnp.bfloat16)
        return lax.all_to_all(pieces, AXES, 0, 0, tiled=True).reshape(count * piece, D)
    square_all = lax.all_gather(square_state.astype(jnp.bfloat16), AXES, axis=1, tiled=True)
    tall_all = lax.all_gather(tall_state.astype(jnp.bfloat16), AXES, axis=1, tiled=True)
    joined = jnp.concatenate([square_all.reshape(-1, D), tall_all.reshape(-1, D)], axis=0)
    own = joined.shape[0] // count
    return lax.dynamic_slice_in_dim(joined, lax.axis_index(AXES) * own, own, axis=0)


def from_owner_rows(rows_out, count, square_rows, tall_rows):
    group = count // 16
    rows_out = rows_out.astype(jnp.bfloat16)
    if square_rows % group == 0:
        piece = square_rows // group
        back = lax.all_to_all(rows_out.reshape(count, piece, D), AXES, 0, 0, tiled=True)
        return (
            back[: 8 * group].reshape(8, square_rows, D),
            back[8 * group :].reshape(2, tall_rows, D),
        )
    joined = lax.all_gather(rows_out, AXES, axis=0, tiled=True)
    square_all = joined[: 8 * square_rows * count].reshape(8, square_rows * count, D)
    tall_all = joined[8 * square_rows * count :].reshape(2, tall_rows * count, D)
    index = lax.axis_index(AXES)
    return (
        lax.dynamic_slice_in_dim(square_all, index * square_rows, square_rows, axis=1),
        lax.dynamic_slice_in_dim(tall_all, index * tall_rows, tall_rows, axis=1),
    )


def orthogonal_rows(rows_in):
    rows_in = rows_in.astype(jnp.float32)
    gram = lax.psum(
        jnp.einsum("rd,re->de", rows_in, rows_in, precision=lax.Precision.HIGHEST), "row"
    )
    is_tall = lax.axis_index("tall") >= 2
    wide = lax.psum(jnp.where(is_tall, gram, 0.0), "square")
    gram = jnp.where(is_tall, wide, gram)
    eye = (jnp.arange(D)[:, None] == jnp.arange(D)[None, :]).astype(jnp.float32)
    scale = 1.0 / (jnp.sqrt(jnp.sum(gram * eye)) + FLOOR_EPSILON)
    gram = gram * (scale * scale)
    current = rows_in * scale

    for sweep in range(ITERS):
        poly = FIRST_TERM * eye + SECOND_TERM * gram + THIRD_TERM * matmul3(gram, gram)
        current = matmul3(current, poly)
        if sweep < ITERS - 1:
            gram = matmul3(matmul3(gram, poly), poly)
    return current


def local(
    inputs,
    memory,
    cotangent,
    lengths,
    memory_len,
    square_master,
    tall_master,
    square_momentum,
    tall_momentum,
    vectors,
    feed_vectors,
    head_scale,
    relative,
):
    count = lax.axis_size(AXES)
    index = lax.axis_index(AXES)
    square_copy, tall_copy = (
        lax.all_gather(square_master.astype(jnp.bfloat16), AXES, axis=1, tiled=True),
        lax.all_gather(tall_master.astype(jnp.bfloat16), AXES, axis=1, tiled=True),
    )
    params = (
        square_copy.astype(jnp.float32),
        tall_copy.astype(jnp.float32),
        vectors.astype(jnp.float32),
        feed_vectors.astype(jnp.float32),
        head_scale.astype(jnp.float32),
        relative.astype(jnp.float32),
    )

    def forward(params, inputs_full, memory_full):
        return layer_block(inputs_full, memory_full, memory_len, *params)

    output, pullback = jax.vjp(
        forward, params, inputs.astype(jnp.float32), memory.astype(jnp.float32)
    )
    valid = (jnp.arange(inputs.shape[1])[None, :] < lengths[:, None]).astype(jnp.float32)
    param_slopes, input_slope, memory_slope = pullback(
        cotangent.astype(jnp.float32) * valid[:, :, None]
    )
    square_slope, tall_slope, vector_slope, feed_slope, scale_slope, bias_slope = param_slopes
    tall_sum = lax.psum_scatter(
        tall_slope.astype(jnp.bfloat16), AXES, scatter_dimension=1, tiled=True
    ).astype(jnp.float32)
    square_sum = lax.psum_scatter(
        square_slope.astype(jnp.bfloat16), AXES, scatter_dimension=1, tiled=True
    ).astype(jnp.float32)
    small = [
        jnp.sum(lengths).astype(jnp.float32).reshape(1),
        scale_slope.reshape(-1),
        bias_slope.reshape(-1),
        vector_slope.reshape(-1),
        feed_slope.reshape(-1),
    ]
    sizes = [piece.shape[0] for piece in small]
    summed = lax.psum(jnp.concatenate(small), AXES)
    starts = [sum(sizes[:i]) for i in range(len(sizes) + 1)]
    total, scale_sum, bias_sum, vector_sum, feed_sum = (
        summed[starts[i] : starts[i + 1]] for i in range(len(sizes))
    )
    factor = inputs.shape[0] * count / total[0]
    bias_sum = bias_sum.reshape(bias_slope.shape)
    width = vector_slope.shape[1] // count
    vector_sum = lax.dynamic_slice_in_dim(
        vector_sum.reshape(vector_slope.shape), index * width, width, axis=1
    )
    width = feed_slope.shape[1] // count
    feed_sum = lax.dynamic_slice_in_dim(
        feed_sum.reshape(feed_slope.shape), index * width, width, axis=1
    )
    square_state = MOMENTUM_DECAY * square_momentum + factor * square_sum
    tall_state = MOMENTUM_DECAY * tall_momentum + factor * tall_sum
    rows_out = orthogonal_rows(to_owner_rows(square_state, tall_state, count))
    square, tall = from_owner_rows(
        rows_out, count, square_state.shape[1], tall_state.shape[1]
    )
    square, tall = square.astype(jnp.float32), tall.astype(jnp.float32)
    square_weight = square_master * (1.0 - LEARN_RATE * WEIGHT_DECAY) - LEARN_RATE * square
    tall_weight = (
        tall_master * (1.0 - LEARN_RATE * WEIGHT_DECAY)
        - LEARN_RATE * max(1.0, FF / D) ** 0.5 * tall
    )
    return (
        output.astype(jnp.bfloat16),
        input_slope.astype(jnp.bfloat16),
        memory_slope.astype(jnp.bfloat16),
        square_state,
        tall_state,
        square_weight,
        tall_weight,
        factor * vector_sum,
        factor * feed_sum,
        factor * scale_sum,
        factor * bias_sum,
    )


def solution(mesh):
    count = mesh.devices.size
    grouped = Mesh(mesh.devices.reshape(4, 4, count // 16), AXES)
    placed = (
        P(AXES, None, None),
        P(AXES, None, None),
        P(AXES, None, None),
        P(AXES),
        P(AXES),
        P(None, AXES, None),
        P(None, AXES, None),
        P(None, AXES, None),
        P(None, AXES, None),
        P(),
        P(),
        P(),
        P(),
    )
    return jax.shard_map(
        local,
        mesh=grouped,
        in_specs=placed,
        out_specs=(
            P(AXES, None, None),
            P(AXES, None, None),
            P(AXES, None, None),
            P(None, AXES, None),
            P(None, AXES, None),
            P(None, AXES, None),
            P(None, AXES, None),
            P(None, AXES),
            P(None, AXES),
            P(),
            P(),
        ),
        check_vma=False,
    )
```

```python
import functools

import jax
import jax.numpy as jnp
from jax import lax
from jax.experimental import pallas as pl
from jax.experimental.pallas import tpu as pltpu
from jax.sharding import Mesh, PartitionSpec as P

D = 768
FF = 3072
ITERS = 5


NORM_EPSILON = 1e-05
FLOOR_EPSILON = 1e-07
FIRST_TERM = 3.4445
SECOND_TERM = -4.775
THIRD_TERM = 2.0315
MOMENTUM_DECAY = 0.95
LEARN_RATE = 0.8
WEIGHT_DECAY = 0.01
NEGATIVE_LARGE = -1e30


def plain_round(values):
    return lax.optimization_barrier(values.astype(jnp.bfloat16)).astype(jnp.float32)


def same_value(values):
    return values


def value_keep(values):
    return (plain_round(values), None)


def value_pass(kept, slope):
    return (slope,)


def gradient_keep(values):
    return (values, None)


def gradient_round(kept, slope):
    return (plain_round(slope),)


def round_value(values):
    wrapped = jax.custom_vjp(plain_round)
    wrapped.defvjp(value_keep, value_pass)
    return wrapped(values)


def round_gradient(values):
    wrapped = jax.custom_vjp(same_value)
    wrapped.defvjp(gradient_keep, gradient_round)
    return wrapped(values)


def norm_rows(values, gain, shift):
    center = values - jnp.mean(values, axis=-1, keepdims=True)
    spread = jnp.mean(center * center, axis=-1, keepdims=True)
    return center * lax.rsqrt(spread + NORM_EPSILON) * gain + shift


def attend(query, keys, values, allowed, bias):
    scores = jnp.einsum("bqhe,bkhe->bhqk", query, keys) + bias
    scores = jnp.where(allowed, round_gradient(scores), NEGATIVE_LARGE)
    weights = jnp.exp(scores - jnp.max(scores, axis=-1, keepdims=True))
    weights = round_value(weights / jnp.sum(weights, axis=-1, keepdims=True))
    return round_gradient(jnp.einsum("bhqk,bkhe->bqhe", weights, values))


def split_heads(values, head_count):
    return values.reshape(
        values.shape[0], values.shape[1], head_count, values.shape[2] // head_count
    )


def attention_block(inputs, memory, memory_len, square, vectors, head_scale, relative):
    item_count, query_count, model_width = inputs.shape
    head_count = head_scale.shape[0]
    memory_slots = memory.shape[1]
    normed = round_value(norm_rows(inputs, vectors[0], vectors[1]))
    query = round_gradient(round_value((jnp.matmul(normed, square[0]) + vectors[2]) * 0.125))
    keys = round_gradient(round_value(jnp.matmul(normed, square[1])))
    values = round_gradient(round_value(jnp.matmul(normed, square[2]) + vectors[3]))
    query_index = jnp.arange(query_count)[:, None]
    key_index = jnp.arange(query_count)[None, :]
    distance = jnp.clip(query_index - key_index, 0, query_count - 1)
    position_table = (distance[:, :, None] == jnp.arange(query_count)[None, None, :]).astype(
        jnp.float32
    )
    bias = jnp.einsum("hd,qkd->hqk", relative, position_table)[None]
    mixed = attend(
        split_heads(query, head_count),
        split_heads(keys, head_count),
        split_heads(values, head_count),
        (query_index >= key_index)[None, None],
        bias,
    )
    mixed = (mixed * head_scale[None, None, :, None]).reshape(item_count, query_count, model_width)
    mixed = round_value(norm_rows(mixed, vectors[5], vectors[6]))
    hidden = inputs + round_gradient(jnp.matmul(mixed, square[3]) + vectors[4])
    normed = round_value(norm_rows(hidden, vectors[7], vectors[8]))
    query = round_gradient(round_value((jnp.matmul(normed, square[4]) + vectors[9]) * 0.125))
    keys = round_gradient(round_value(jnp.matmul(memory, square[5])))
    values = round_gradient(round_value(jnp.matmul(memory, square[6]) + vectors[10]))
    allowed = (jnp.arange(memory_slots)[None, :] < memory_len[:, None])[:, None, None, :]
    mixed = attend(
        split_heads(query, head_count),
        split_heads(keys, head_count),
        split_heads(values, head_count),
        allowed,
        0.0,
    )
    mixed = round_value(
        norm_rows(mixed.reshape(item_count, query_count, model_width), vectors[12], vectors[13])
    )
    return hidden + round_gradient(jnp.matmul(mixed, square[7]) + vectors[11])


def feed_block(hidden, tall, vectors, feed_vectors):
    normed = round_value(norm_rows(hidden, vectors[14], vectors[15]))
    inner = round_gradient(jnp.matmul(normed, tall[0].T) + feed_vectors[0])
    active = round_value(
        norm_rows(jax.nn.gelu(inner, approximate=False), feed_vectors[1], feed_vectors[2])
    )
    return hidden + round_gradient(jnp.matmul(active, tall[1]) + vectors[16])


AXES = ("tall", "square", "row")
MESH = pl.DeviceIdType.MESH


def place():
    z, plane, core = lax.axis_index("tall"), lax.axis_index("square"), lax.axis_index("row")
    return z, lax.div(plane, 2), lax.rem(plane, 2), core


def device(z, y, x, core):
    return (z, y * 2 + x, core)


def greet(partners):
    barrier = pltpu.get_barrier_semaphore()
    for partner in partners:
        pl.semaphore_signal(barrier, inc=1, device_id=partner, device_id_type=MESH)
    pl.semaphore_wait(barrier, len(partners))


def reduce_kernel(groups, has_small, *refs):
    n = len(groups)
    ins, refs = refs[:n], refs[n:]
    if has_small:
        small, refs = refs[0], refs[1:]
    outs, refs = refs[:n], refs[n:]
    if has_small:
        small_out, refs = refs[0], refs[1:]
    z, y, x, core = place()
    other = 1 - core
    sibling = device(z, y, x, other)
    across = {"x": device(z, y, 1 - x, core), "y": device(z, 1 - y, x, core)}
    along = [device(lax.rem(z + k, 4), y, x, core) for k in (1, 2, 3)]
    greet([sibling, across["x"], across["y"]] + along)
    mine = core * 384
    theirs = other * 384

    if has_small:
        held, total, refs = refs[0], refs[1], refs[2:]
        small_send, small_recv, refs = refs[0], refs[1], refs[2:]

        def small_copies(stage):
            source = small if stage == 0 else total.at[stage - 1]
            if stage < 3:
                partner = (sibling, across["x"], across["y"])[stage]
                return [
                    pltpu.make_async_remote_copy(
                        source, held.at[stage], small_send.at[stage], small_recv.at[stage],
                        device_id=partner, device_id_type=MESH,
                    )
                ]
            return [
                pltpu.make_async_remote_copy(
                    source, held.at[3 + z], small_send.at[3 + k], small_recv.at[3 + k],
                    device_id=along[k], device_id_type=MESH,
                )
                for k in range(3)
            ]

        for copy in small_copies(0):
            copy.start()

        def small_step(stage):
            for copy in small_copies(stage):
                copy.wait_recv()
            if stage < 3:
                own = small if stage == 0 else total.at[stage - 1]
                total[stage] = own[...] + held[stage]
                if stage == 2:
                    held[3 + z] = total[2]
                for copy in small_copies(stage + 1):
                    copy.start()
            else:
                small_out[...] = ((held[3] + held[4]) + held[5]) + held[6]
    else:
        def small_step(stage):
            pass

    plans = []
    for g, (pieces, rows, width, by_column) in enumerate(groups):
        r0, r1, r2, r3, f3, r4, send, recv = refs[8 * g : 8 * g + 8]
        plans.append((pieces, rows, width, by_column, ins[g], outs[g], r0, r1, r2, r3, f3, r4, send, recv))

    def where(plan, order, i):
        pieces, by_column, width = plan[0], plan[3], plan[2]
        j = i + order * (pieces // 2)
        if by_column:
            return j, order, pl.multiple_of(i * width, 128)
        return j, j, 0

    def copies(plan, stage, order, i):
        pieces, rows, width, by_column, src, out, r0, r1, r2, r3, f3, r4, send, recv = plan
        j, matrix, column = where(plan, order, i)
        first = "xy"[order]

        def make(source, target, slot, partner):
            return pltpu.make_async_remote_copy(
                source, target, send.at[slot, j], recv.at[slot, j],
                device_id=partner, device_id_type=MESH,
            )

        if stage == 0:
            lanes = pl.ds(pl.multiple_of(theirs + column, 128), width)
            return [make(src.at[matrix, :, :, :, :, lanes], r0.at[j], 0, sibling)]
        if stage == 1:
            part = r0.at[j, :, :, 1 - x] if order == 0 else r0.at[j, :, 1 - y]
            return [make(part, r1.at[j], 1, across[first])]
        if stage == 2:
            return [
                make(r1.at[j, lax.rem(z + k + 1, 4)], r2.at[j, k], 2 + k, along[k])
                for k in range(3)
            ]
        if stage == 3:
            part = r2.at[j, 0, 1 - y] if order == 0 else r2.at[j, 0, 1 - x]
            return [make(part, r3.at[j], 5, across["yx"[order]])]
        share = rows // 2
        return [make(f3.at[j, pl.ds(pl.multiple_of(other * share, 8), share)], r4.at[j], 6, sibling)]

    f32 = jnp.float32

    def add(plan, stage, order, i):
        pieces, rows, width, by_column, src, out, r0, r1, r2, r3, f3, r4, send, recv = plan
        j, matrix, column = where(plan, order, i)
        if stage == 0:
            lanes = pl.ds(pl.multiple_of(mine + column, 128), width)

            @pl.loop(0, 16)
            def _(block):
                a, b, d = lax.div(block, 4), lax.rem(lax.div(block, 2), 2), lax.rem(block, 2)
                r0[j, a, b, d] = (
                    r0[j, a, b, d].astype(f32) + src[matrix, a, b, d, :, lanes].astype(f32)
                ).astype(jnp.bfloat16)
        elif stage == 1:
            @pl.loop(0, 8)
            def _(block):
                a, b = lax.div(block, 2), lax.rem(block, 2)
                own = r0[j, a, b, x] if order == 0 else r0[j, a, y, b]
                r1[j, a, b] = (r1[j, a, b].astype(f32) + own.astype(f32)).astype(jnp.bfloat16)
        elif stage == 2:
            for b in range(2):
                r2[j, 0, b] = (
                    (r2[j, 0, b].astype(f32) + r2[j, 1, b].astype(f32))
                    + (r2[j, 2, b].astype(f32) + r1[j, z, b].astype(f32))
                ).astype(jnp.bfloat16)
        elif stage == 3:
            own = r2[j, 0, y] if order == 0 else r2[j, 0, x]
            f3[j] = r3[j].astype(f32) + own.astype(f32)
        else:
            share = rows // 2
            lanes = pl.ds(pl.multiple_of(mine + column, 128), width)
            out[matrix, :, lanes] = f3[j, pl.ds(pl.multiple_of(core * share, 8), share)]
            lanes = pl.ds(pl.multiple_of(theirs + column, 128), width)
            out[matrix, :, lanes] = r4[j]

    def each(plan, body):
        @pl.loop(0, plan[0] // 2)
        def _(i):
            for order in range(2):
                body(order, i)

    def start(plan, stage):
        def body(order, i):
            for copy in copies(plan, stage, order, i):
                copy.start()

        each(plan, body)

    def step(plan, stage):
        def body(order, i):
            for copy in copies(plan, stage, order, i):
                copy.wait_recv()
            add(plan, stage, order, i)
            if stage < 4:
                for copy in copies(plan, stage + 1, order, i):
                    copy.start()

        each(plan, body)

    def finish(plan, stage):
        def body(order, i):
            for copy in copies(plan, stage, order, i):
                copy.wait_send()

        each(plan, body)

    for plan in plans:
        start(plan, 0)
    for stage in range(5):
        if stage < 4:
            small_step(stage)
        for plan in plans:
            step(plan, stage)
    for stage in range(5):
        for plan in plans:
            finish(plan, stage)
    if has_small:
        for stage in range(4):
            for copy in small_copies(stage):
                copy.wait_send()


def reduce_scatter(arrays, small, collective_id):
    groups, views, outs, scratch = [], [], [], []
    bf16, f32 = jnp.bfloat16, jnp.float32
    if small is not None:
        scratch += [
            pltpu.VMEM((7,) + small.shape, f32),
            pltpu.VMEM((3,) + small.shape, f32),
            pltpu.SemaphoreType.DMA((6,)),
            pltpu.SemaphoreType.DMA((6,)),
        ]
    for array in arrays:
        matrices, height, width_all = array.shape
        rows = height // 16
        by_column = matrices == 2
        pieces, width = (6, 128) if by_column else (matrices, 384)
        groups.append((pieces, rows, width, by_column))
        views.append(array.reshape(matrices, 4, 2, 2, rows, width_all))
        outs.append(jax.ShapeDtypeStruct((matrices, rows // 2, width_all), f32))
        scratch += [
            pltpu.VMEM((pieces, 4, 2, 2, rows, width), bf16),
            pltpu.VMEM((pieces, 4, 2, rows, width), bf16),
            pltpu.VMEM((pieces, 3, 2, rows, width), bf16),
            pltpu.VMEM((pieces, rows, width), bf16),
            pltpu.VMEM((pieces, rows, width), f32),
            pltpu.VMEM((pieces, rows // 2, width), f32),
            pltpu.SemaphoreType.DMA((7, pieces)),
            pltpu.SemaphoreType.DMA((7, pieces)),
        ]
    if small is not None:
        views.append(small)
        outs.append(jax.ShapeDtypeStruct(small.shape, f32))
    vmem = pl.BlockSpec(memory_space=pltpu.VMEM)
    return pl.pallas_call(
        functools.partial(reduce_kernel, tuple(groups), small is not None),
        out_shape=tuple(outs),
        in_specs=[vmem] * len(views),
        out_specs=tuple([vmem] * len(outs)),
        scratch_shapes=scratch,
        compiler_params=pltpu.CompilerParams(
            collective_id=collective_id, has_side_effects=True, vmem_limit_bytes=60 << 20
        ),
    )(*views)


def gram_kernel(gram, out, other_sum, half_a, half_b, final, send, recv):
    z, y, x, core = place()
    sibling = device(z, y, x, 1 - core)
    x_side, y_side = device(z, y, 1 - x, core), device(z, 1 - y, x, core)
    greet([sibling, x_side, y_side])
    side = gram.shape[0] // 2
    rows = pl.ds(pl.multiple_of(core * side, 8), side)
    rest = pl.ds(pl.multiple_of((1 - core) * side, 8), side)

    def send_to(source, target, slot, partner):
        return pltpu.make_async_remote_copy(
            source, target, send.at[slot], recv.at[slot], device_id=partner, device_id_type=MESH
        )

    first = send_to(gram.at[rest], other_sum.at[rest], 0, sibling)
    second = send_to(gram.at[rows], other_sum.at[rows], 1, sibling)
    first.start()
    second.start()
    mine = send_to(gram.at[rows], other_sum.at[rows], 0, sibling)
    mine.wait_recv()
    out[rows] = gram[rows] + other_sum[rows]
    theirs = send_to(gram.at[rest], other_sum.at[rest], 1, sibling)
    theirs.wait_recv()

    @pl.when(z < 2)
    def _():
        out[rest] = gram[rest] + other_sum[rest]

    @pl.when(z >= 2)
    def _():
        def pair(one, two):
            step = send_to(out.at[rows], half_a, 2, one)
            step.start()
            step.wait_recv()
            step.wait_send()
            half_b[...] = out[rows] + half_a[...]
            step = send_to(half_b, final, 3, two)
            step.start()
            step.wait_recv()
            out[rows] = half_b[...] + final[...]
            step.wait_send()

        @pl.when(core == 0)
        def _():
            pair(x_side, y_side)

        @pl.when(core == 1)
        def _():
            pair(y_side, x_side)

        last = send_to(out.at[rows], out.at[rows], 4, sibling)
        last.start()
        arrive = send_to(out.at[rest], out.at[rest], 4, sibling)
        arrive.wait_recv()
        last.wait_send()

    first.wait_send()
    second.wait_send()


def gram_sum(gram, collective_id):
    f32 = jnp.float32
    side = gram.shape[0] // 2
    vmem = pl.BlockSpec(memory_space=pltpu.VMEM)
    return pl.pallas_call(
        gram_kernel,
        out_shape=jax.ShapeDtypeStruct(gram.shape, f32),
        in_specs=[vmem],
        out_specs=vmem,
        scratch_shapes=[
            pltpu.VMEM(gram.shape, f32),
            pltpu.VMEM((side, gram.shape[1]), f32),
            pltpu.VMEM((side, gram.shape[1]), f32),
            pltpu.VMEM((side, gram.shape[1]), f32),
            pltpu.SemaphoreType.DMA((5,)),
            pltpu.SemaphoreType.DMA((5,)),
        ],
        compiler_params=pltpu.CompilerParams(
            collective_id=collective_id, has_side_effects=True, vmem_limit_bytes=32 << 20
        ),
    )(gram)


def matmul3(left, right):
    return jnp.matmul(left, right, precision=lax.Precision.HIGH)


def to_owner_rows(square_state, tall_state, count):
    rows = square_state.shape[1]
    group = count // 16
    if rows % group == 0:
        piece = rows // group
        pieces = jnp.concatenate(
            [
                square_state.reshape(8 * group, piece, D),
                tall_state.reshape(8 * group, piece, D),
            ],
            axis=0,
        ).astype(jnp.bfloat16)
        return lax.all_to_all(pieces, AXES, 0, 0, tiled=True).reshape(count * piece, D)
    square_all = lax.all_gather(square_state.astype(jnp.bfloat16), AXES, axis=1, tiled=True)
    tall_all = lax.all_gather(tall_state.astype(jnp.bfloat16), AXES, axis=1, tiled=True)
    joined = jnp.concatenate([square_all.reshape(-1, D), tall_all.reshape(-1, D)], axis=0)
    own = joined.shape[0] // count
    return lax.dynamic_slice_in_dim(joined, lax.axis_index(AXES) * own, own, axis=0)


def from_owner_rows(rows_out, count, square_rows, tall_rows):
    group = count // 16
    rows_out = rows_out.astype(jnp.bfloat16)
    if square_rows % group == 0:
        piece = square_rows // group
        back = lax.all_to_all(rows_out.reshape(count, piece, D), AXES, 0, 0, tiled=True)
        return (
            back[: 8 * group].reshape(8, square_rows, D),
            back[8 * group :].reshape(2, tall_rows, D),
        )
    joined = lax.all_gather(rows_out, AXES, axis=0, tiled=True)
    square_all = joined[: 8 * square_rows * count].reshape(8, square_rows * count, D)
    tall_all = joined[8 * square_rows * count :].reshape(2, tall_rows * count, D)
    index = lax.axis_index(AXES)
    return (
        lax.dynamic_slice_in_dim(square_all, index * square_rows, square_rows, axis=1),
        lax.dynamic_slice_in_dim(tall_all, index * tall_rows, tall_rows, axis=1),
    )


def orthogonal_rows(rows_in, kernels):
    rows_in = rows_in.astype(jnp.float32)
    gram = jnp.einsum("rd,re->de", rows_in, rows_in, precision=lax.Precision.HIGHEST)
    if kernels:
        gram = gram_sum(gram, 2)
    else:
        gram = lax.psum(gram, "row")
        is_tall = lax.axis_index("tall") >= 2
        gram = jnp.where(is_tall, lax.psum(jnp.where(is_tall, gram, 0.0), "square"), gram)
    eye = (jnp.arange(D)[:, None] == jnp.arange(D)[None, :]).astype(jnp.float32)
    scale = 1.0 / (jnp.sqrt(jnp.sum(gram * eye)) + FLOOR_EPSILON)
    gram = gram * (scale * scale)
    current = rows_in * scale

    for sweep in range(ITERS):
        poly = FIRST_TERM * eye + SECOND_TERM * gram + THIRD_TERM * matmul3(gram, gram)
        current = matmul3(current, poly)
        if sweep < ITERS - 1:
            gram = matmul3(matmul3(gram, poly), poly)
    return current


def local(
    inputs,
    memory,
    cotangent,
    lengths,
    memory_len,
    square_master,
    tall_master,
    square_momentum,
    tall_momentum,
    vectors,
    feed_vectors,
    head_scale,
    relative,
):
    count = lax.axis_size(AXES)
    kernels = count == 32
    index = lax.axis_index(AXES)
    square_copy, tall_copy = (
        lax.all_gather(square_master.astype(jnp.bfloat16), AXES, axis=1, tiled=True),
        lax.all_gather(tall_master.astype(jnp.bfloat16), AXES, axis=1, tiled=True),
    )
    params = (
        square_copy.astype(jnp.float32),
        tall_copy.astype(jnp.float32),
        vectors.astype(jnp.float32),
        feed_vectors.astype(jnp.float32),
        head_scale.astype(jnp.float32),
        relative.astype(jnp.float32),
    )

    square, tall, gains, feed_gains, scales, biases = params

    def attention(square, gains, scales, biases, inputs_full, memory_full):
        return attention_block(
            inputs_full, memory_full, memory_len, square, gains, scales, biases
        )

    hidden, attention_back = jax.vjp(
        attention,
        square,
        gains,
        scales,
        biases,
        inputs.astype(jnp.float32),
        memory.astype(jnp.float32),
    )
    output, feed_back = jax.vjp(feed_block, hidden, tall, gains, feed_gains)
    valid = (jnp.arange(inputs.shape[1])[None, :] < lengths[:, None]).astype(jnp.float32)
    hidden_slope, tall_slope, late_slope, feed_slope = feed_back(
        cotangent.astype(jnp.float32) * valid[:, :, None]
    )
    tall_slope, hidden_slope = lax.optimization_barrier(
        (tall_slope.astype(jnp.bfloat16), hidden_slope)
    )
    tall_sum = lax.psum_scatter(tall_slope, AXES, scatter_dimension=1, tiled=True).astype(
        jnp.float32
    )
    square_slope, vector_slope, scale_slope, bias_slope, input_slope, memory_slope = (
        attention_back(hidden_slope)
    )
    vector_slope = vector_slope + late_slope
    square_slope = square_slope.astype(jnp.bfloat16)
    small = [
        jnp.sum(lengths).astype(jnp.float32).reshape(1),
        scale_slope.reshape(-1),
        bias_slope.reshape(-1),
        vector_slope.reshape(-1),
        feed_slope.reshape(-1),
    ]
    sizes = [piece.shape[0] for piece in small]
    starts = [sum(sizes[:i]) for i in range(len(sizes) + 1)]
    if kernels:
        lines = -(-starts[-1] // 1024) * 8
        small.append(jnp.zeros((lines * 128 - starts[-1],), jnp.float32))
        square_sum, summed = reduce_scatter(
            [square_slope], jnp.concatenate(small).reshape(lines, 128), 1
        )
        summed = summed.reshape(-1)
    else:
        square_sum = lax.psum_scatter(
            square_slope, AXES, scatter_dimension=1, tiled=True
        ).astype(jnp.float32)
        summed = lax.psum(jnp.concatenate(small), AXES)
    total, scale_sum, bias_sum, vector_sum, feed_sum = (
        summed[starts[i] : starts[i + 1]] for i in range(len(sizes))
    )
    factor = inputs.shape[0] * count / total[0]
    bias_sum = bias_sum.reshape(bias_slope.shape)
    width = vector_slope.shape[1] // count
    vector_sum = lax.dynamic_slice_in_dim(
        vector_sum.reshape(vector_slope.shape), index * width, width, axis=1
    )
    width = feed_slope.shape[1] // count
    feed_sum = lax.dynamic_slice_in_dim(
        feed_sum.reshape(feed_slope.shape), index * width, width, axis=1
    )
    square_state = MOMENTUM_DECAY * square_momentum + factor * square_sum
    tall_state = MOMENTUM_DECAY * tall_momentum + factor * tall_sum
    rows_out = orthogonal_rows(to_owner_rows(square_state, tall_state, count), kernels)
    square, tall = from_owner_rows(
        rows_out, count, square_state.shape[1], tall_state.shape[1]
    )
    square, tall = square.astype(jnp.float32), tall.astype(jnp.float32)
    square_weight = square_master * (1.0 - LEARN_RATE * WEIGHT_DECAY) - LEARN_RATE * square
    tall_weight = (
        tall_master * (1.0 - LEARN_RATE * WEIGHT_DECAY)
        - LEARN_RATE * max(1.0, FF / D) ** 0.5 * tall
    )
    return (
        output.astype(jnp.bfloat16),
        input_slope.astype(jnp.bfloat16),
        memory_slope.astype(jnp.bfloat16),
        square_state,
        tall_state,
        square_weight,
        tall_weight,
        factor * vector_sum,
        factor * feed_sum,
        factor * scale_sum,
        factor * bias_sum,
    )


def solution(mesh):
    count = mesh.devices.size
    grouped = Mesh(mesh.devices.reshape(4, 4, count // 16), AXES)
    placed = (
        P(AXES, None, None),
        P(AXES, None, None),
        P(AXES, None, None),
        P(AXES),
        P(AXES),
        P(None, AXES, None),
        P(None, AXES, None),
        P(None, AXES, None),
        P(None, AXES, None),
        P(),
        P(),
        P(),
        P(),
    )
    return jax.shard_map(
        local,
        mesh=grouped,
        in_specs=placed,
        out_specs=(
            P(AXES, None, None),
            P(AXES, None, None),
            P(AXES, None, None),
            P(None, AXES, None),
            P(None, AXES, None),
            P(None, AXES, None),
            P(None, AXES, None),
            P(None, AXES),
            P(None, AXES),
            P(),
            P(),
        ),
        check_vma=False,
    )
```

```python
import functools

import jax
import jax.numpy as jnp
from jax import lax
from jax.experimental import pallas as pl
from jax.experimental.pallas import tpu as pltpu
from jax.sharding import Mesh, PartitionSpec as P

D = 768
FF = 3072
ITERS = 5


NORM_EPSILON = 1e-05
FLOOR_EPSILON = 1e-07
FIRST_TERM = 3.4445
SECOND_TERM = -4.775
THIRD_TERM = 2.0315
MOMENTUM_DECAY = 0.95
LEARN_RATE = 0.8
WEIGHT_DECAY = 0.01
NEGATIVE_LARGE = -1e30


F32, BF16 = jnp.float32, jnp.bfloat16
TOKENS = 256
SLOTS = 512
LANES = 128


def times(left, right):
    return jnp.dot(left, right, preferred_element_type=F32)


def times_back(left, right):
    return lax.dot_general(left, right, (((1,), (1,)), ((), ())), preferred_element_type=F32)


def times_down(left, right):
    return lax.dot_general(left, right, (((0,), (0,)), ((), ())), preferred_element_type=F32)


def standard(values):
    center = values - jnp.mean(values, axis=-1, keepdims=True)
    scale = lax.rsqrt(jnp.mean(center * center, axis=-1, keepdims=True) + NORM_EPSILON)
    return center * scale, scale


def norm(values, gain, shift):
    return standard(values)[0] * gain + shift


def norm_back(values, slope, gain):
    hat, scale = standard(values)
    inner = slope * gain
    back = scale * (
        inner
        - jnp.mean(inner, axis=-1, keepdims=True)
        - hat * jnp.mean(inner * hat, axis=-1, keepdims=True)
    )
    return back, down(slope * hat), down(slope)


def down(values):
    return jnp.sum(values, axis=0, keepdims=True)


def head_masks():
    lane = lax.broadcasted_iota(jnp.int32, (1, LANES), 1)
    even = jnp.where(lane < LANES // 2, 1.0, 0.0)
    return even.astype(BF16), (1.0 - even).astype(BF16)


def stacked(pair, masks):
    return jnp.concatenate([pair * masks[0], pair * masks[1]], axis=0)


def side_by_side(rows):
    half = rows.shape[0] // 2
    return jnp.concatenate([rows[:half], rows[half:]], axis=1)


def soften(scores):
    weights = jnp.exp(scores - jnp.max(scores, axis=-1, keepdims=True))
    return (weights * (1.0 / jnp.sum(weights, axis=-1, keepdims=True))).astype(BF16)


def soften_back(weights, slope):
    weights = weights.astype(F32)
    product = weights * slope
    return (product - weights * jnp.sum(product, axis=-1, keepdims=True)).astype(BF16)


def attention_kernel(
    memory_len, x_in, memory, w, vec, hs, bias,
    n1, q, k, v, p, o, m1, h1, n2, cq, ck, cv, pc, co, m2, h2,
):
    step = pl.program_id(0)
    masks = head_masks()
    x = x_in[...].astype(F32)
    n1[...] = norm(x, vec[0:1], vec[1:2]).astype(BF16)
    q[...] = ((times(n1[...], w[0]) + vec[2:3]) * 0.125).astype(BF16)
    k[...] = times(n1[...], w[1]).astype(BF16)
    v[...] = (times(n1[...], w[2]) + vec[3:4]).astype(BF16)
    items = TOKENS // 128

    @pl.loop(0, 6)
    def _(pair):
        lanes = pl.ds(pl.multiple_of(pair * LANES, LANES), LANES)
        for item in range(items):
            rows = slice(item * 128, item * 128 + 128)
            scores = times_back(stacked(q[rows, lanes], masks), k[rows, lanes]) + bias[pair]
            weights = soften(scores)
            p[item, pair] = weights
            o[rows, lanes] = times(side_by_side(weights), stacked(v[rows, lanes], masks))

    m1[...] = norm(o[...] * hs[...], vec[5:6], vec[6:7]).astype(BF16)
    h1[...] = x + (times(m1[...], w[3]) + vec[4:5])
    n2[...] = norm(h1[...], vec[7:8], vec[8:9]).astype(BF16)
    cq[...] = ((times(n2[...], w[4]) + vec[9:10]) * 0.125).astype(BF16)
    ck[...] = times(memory[...], w[5]).astype(BF16)
    cv[...] = (times(memory[...], w[6]) + vec[10:11]).astype(BF16)
    slots = SLOTS // items
    column = lax.broadcasted_iota(jnp.int32, (1, slots), 1)

    @pl.loop(0, 6)
    def _(pair):
        lanes = pl.ds(pl.multiple_of(pair * LANES, LANES), LANES)
        for item in range(items):
            rows = slice(item * 128, item * 128 + 128)
            keys = slice(item * slots, item * slots + slots)
            limit = memory_len[step * items + item]
            scores = times_back(stacked(cq[rows, lanes], masks), ck[keys, lanes])
            weights = soften(jnp.where(column < limit, scores, NEGATIVE_LARGE))
            pc[item, pair] = weights
            co[rows, lanes] = times(side_by_side(weights), stacked(cv[keys, lanes], masks))

    m2[...] = norm(co[...], vec[12:13], vec[13:14]).astype(BF16)
    h2[...] = h1[...] + (times(m2[...], w[7]) + vec[11:12])


def whole(shape):
    return pl.BlockSpec(shape, lambda *_: (0,) * len(shape), pipeline_mode=pl.Buffered(1))


def by_rows(rows, width):
    return pl.BlockSpec((rows, width), lambda i: (i, 0))


def by_items(items, *rest):
    return pl.BlockSpec((items,) + rest, lambda i: (i,) + (0,) * len(rest))


def attention_forward(inputs, memory, memory_len, square, vectors, head_row, bias):
    tokens, width = inputs.shape
    slots = memory.shape[0]
    steps = tokens // TOKENS
    items = TOKENS // 128
    shapes = [
        (BF16, "t"), (BF16, "t"), (BF16, "t"), (BF16, "t"), (BF16, "p"), (F32, "t"), (BF16, "t"), (F32, "t"),
        (BF16, "t"), (BF16, "t"), (BF16, "m"), (BF16, "m"), (BF16, "c"), (F32, "t"), (BF16, "t"), (F32, "t"),
    ]
    full = {"t": (tokens, width), "m": (slots, width), "p": (steps * items, 6, 256, 128), "c": (steps * items, 6, 256, SLOTS // items)}
    spec = {
        "t": by_rows(TOKENS, width), "m": by_rows(SLOTS, width),
        "p": by_items(items, 6, 256, 128), "c": by_items(items, 6, 256, SLOTS // items),
    }
    return pl.pallas_call(
        attention_kernel,
        grid=(steps,),
        out_shape=tuple(jax.ShapeDtypeStruct(full[kind], kept) for kept, kind in shapes),
        in_specs=[
            pl.BlockSpec(memory_space=pltpu.SMEM),
            spec["t"], spec["m"], whole(square.shape), whole(vectors.shape), whole(head_row.shape), whole(bias.shape),
        ],
        out_specs=tuple(spec[kind] for _, kind in shapes),
        compiler_params=pltpu.CompilerParams(vmem_limit_bytes=60 << 20),
        cost_estimate=pl.CostEstimate(flops=14_000_000_000, bytes_accessed=60_000_000, transcendentals=5_000_000),
    )(memory_len, inputs, memory, square, vectors, head_row, bias)


ROOT_HALF = 0.7071067811865476
INVERSE_ROOT = 0.3989422804014327
CHUNK = 512


def feed_kernel(
    lengths, h2_in, cot, tall, vec, feed,
    out, dh2, n3, r, du, dy, dvec, dfeed,
    u, g, dr, total,
):
    step = pl.program_id(0)
    items = TOKENS // 128
    width = tall.shape[1]
    chunks = width // CHUNK

    @pl.when(step == 0)
    def _():
        dvec[...] = jnp.zeros_like(dvec)
        dfeed[...] = jnp.zeros_like(dfeed)

    h2 = h2_in[...]
    n3[...] = norm(h2, vec[14:15], vec[15:16]).astype(BF16)

    def at(i):
        return pl.ds(pl.multiple_of(i * CHUNK, CHUNK), CHUNK)

    def first(i, total):
        some = at(i)
        inner = times_back(n3[...], tall[0, some]) + feed[0:1, some]
        bell = 0.5 + 0.5 * lax.erf(inner * ROOT_HALF)
        active = inner * bell
        g[:, some] = active
        u[:, some] = bell + inner * (jnp.exp(-0.5 * inner * inner) * INVERSE_ROOT)
        return total + jnp.sum(active, axis=-1, keepdims=True)

    zero = jnp.zeros((TOKENS, 1), F32)
    mean = lax.fori_loop(0, chunks, first, zero) * (1.0 / width)

    def second(i, total):
        center = g[:, at(i)] - mean
        return total + jnp.sum(center * center, axis=-1, keepdims=True)

    spread = lax.fori_loop(0, chunks, second, zero) * (1.0 / width)
    scale = lax.rsqrt(spread + NORM_EPSILON)
    row = lax.broadcasted_iota(jnp.int32, (128, 1), 0)
    valid = jnp.concatenate(
        [jnp.where(row < lengths[step * items + item], 1.0, 0.0) for item in range(items)], axis=0
    )
    dy32 = cot[...].astype(F32) * valid
    dy[...] = dy32.astype(BF16)
    total[...] = h2 + vec[16:17]

    def third(i, sums):
        some = at(i)
        hat = (g[:, some] - mean) * scale
        g[:, some] = hat
        gain = feed[1:2, some]
        active = (hat * gain + feed[2:3, some]).astype(BF16)
        r[:, some] = active
        total[...] += times(active, tall[1, some])
        slope = times_back(dy[...], tall[1, some])
        dfeed[1:2, some] += down(slope * hat)
        dfeed[2:3, some] += down(slope)
        inner = slope * gain
        dr[:, some] = inner
        return (
            sums[0] + jnp.sum(inner, axis=-1, keepdims=True),
            sums[1] + jnp.sum(inner * hat, axis=-1, keepdims=True),
        )

    one, two = lax.fori_loop(0, chunks, third, (zero, zero))
    out[...] = total[...].astype(BF16)
    one, two = one * (1.0 / width), two * (1.0 / width)
    dh2[...] = jnp.zeros_like(dh2)

    def fourth(i, carry):
        some = at(i)
        back = scale * (dr[:, some] - one - g[:, some] * two)
        slope = (back * u[:, some]).astype(BF16)
        du[:, some] = slope
        dfeed[0:1, some] += down(slope.astype(F32))
        dh2[...] += times(slope, tall[0, some])
        return carry

    lax.fori_loop(0, chunks, fourth, 0)
    back, gain_sum, shift_sum = norm_back(h2, dh2[...], vec[14:15])
    dvec[0:1] += gain_sum
    dvec[1:2] += shift_sum
    dvec[2:3] += down(dy32)
    dh2[...] = dy32 + back


def feed_both(hidden, cotangent, lengths, tall, vectors, feed_vectors):
    tokens, width = hidden.shape
    wide = tall.shape[1]
    steps = tokens // TOKENS
    some = by_rows(TOKENS, width)
    much = by_rows(TOKENS, wide)
    return pl.pallas_call(
        feed_kernel,
        grid=(steps,),
        out_shape=(
            jax.ShapeDtypeStruct((tokens, width), BF16),
            jax.ShapeDtypeStruct((tokens, width), F32),
            jax.ShapeDtypeStruct((tokens, width), BF16),
            jax.ShapeDtypeStruct((tokens, wide), BF16),
            jax.ShapeDtypeStruct((tokens, wide), BF16),
            jax.ShapeDtypeStruct((tokens, width), BF16),
            jax.ShapeDtypeStruct((3, width), F32),
            jax.ShapeDtypeStruct((3, wide), F32),
        ),
        in_specs=[
            pl.BlockSpec(memory_space=pltpu.SMEM),
            some, some, whole(tall.shape), whole(vectors.shape), whole(feed_vectors.shape),
        ],
        out_specs=(
            some, some, some, much, much, some,
            pl.BlockSpec((3, width), lambda i: (0, 0)),
            pl.BlockSpec((3, wide), lambda i: (0, 0)),
        ),
        scratch_shapes=[pltpu.VMEM((TOKENS, wide), F32)] * 3 + [pltpu.VMEM((TOKENS, width), F32)],
        compiler_params=pltpu.CompilerParams(vmem_limit_bytes=60 << 20),
        cost_estimate=pl.CostEstimate(flops=20_000_000_000, bytes_accessed=40_000_000, transcendentals=7_000_000),
    )(lengths, hidden, cotangent, tall, vectors, feed_vectors)


def attention_back_kernel(
    x_in, dh2, w, vec, hs,
    q, k, v, p, o, h1, cq, ck, cv, pc, co,
    dx, dmem, dy2, dcq, dck, dcv, dy1, dq, dk, dv, dvec, drel,
    do, dh1, dbias,
):
    step = pl.program_id(0)
    masks = head_masks()
    items = TOKENS // 128
    slots = SLOTS // items

    @pl.when(step == 0)
    def _():
        dvec[...] = jnp.zeros_like(dvec)
        dbias[...] = jnp.zeros_like(dbias)

    def note(row, value):
        dvec[row : row + 1] += value

    dy2[...] = dh2[...].astype(BF16)
    note(11, down(dy2[...].astype(F32)))
    back, gain_sum, shift_sum = norm_back(co[...], times_back(dy2[...], w[7]), vec[12:13])
    note(12, gain_sum)
    note(13, shift_sum)
    do[...] = back.astype(BF16)

    def through(pair, item, keys, query, key, value, weights, dquery, dkey, dvalue, with_bias):
        lanes = pl.ds(pl.multiple_of(pair * LANES, LANES), LANES)
        rows = slice(item * 128, item * 128 + 128)
        kept = weights[item, pair]
        grad = stacked(do[rows, lanes], masks)
        dvalue[keys, lanes] = times_down(kept, grad).astype(BF16)
        slope = soften_back(kept, times_back(grad, value[keys, lanes]))
        dquery[rows, lanes] = (
            times(side_by_side(slope), stacked(key[keys, lanes], masks)).astype(BF16) * 0.125
        ).astype(BF16)
        dkey[keys, lanes] = times_down(slope, stacked(query[rows, lanes], masks)).astype(BF16)
        if with_bias:
            dbias[pair] += slope.astype(F32)

    @pl.loop(0, 6)
    def _(pair):
        for item in range(items):
            keys = slice(item * slots, item * slots + slots)
            through(pair, item, keys, cq, ck, cv, pc, dcq, dck, dcv, False)

    note(9, down(dcq[...].astype(F32)))
    note(10, down(dcv[...].astype(F32)))
    dmem[...] = (times_back(dck[...], w[5]) + times_back(dcv[...], w[6])).astype(BF16)
    back, gain_sum, shift_sum = norm_back(h1[...], times_back(dcq[...], w[4]), vec[7:8])
    note(7, gain_sum)
    note(8, shift_sum)
    dh1[...] = dh2[...] + back
    dy1[...] = dh1[...].astype(BF16)
    note(4, down(dy1[...].astype(F32)))
    back, gain_sum, shift_sum = norm_back(o[...] * hs[...], times_back(dy1[...], w[3]), vec[5:6])
    note(5, gain_sum)
    note(6, shift_sum)
    note(17, down(back * o[...]))
    do[...] = (back * hs[...]).astype(BF16)

    @pl.loop(0, 6)
    def _(pair):
        for item in range(items):
            rows = slice(item * 128, item * 128 + 128)
            through(pair, item, rows, q, k, v, p, dq, dk, dv, True)

    note(2, down(dq[...].astype(F32)))
    note(3, down(dv[...].astype(F32)))
    slope = times_back(dq[...], w[0]) + times_back(dk[...], w[1]) + times_back(dv[...], w[2])
    back, gain_sum, shift_sum = norm_back(x_in[...].astype(F32), slope, vec[0:1])
    note(0, gain_sum)
    note(1, shift_sum)
    dx[...] = (dh1[...] + back).astype(BF16)

    @pl.when(step == pl.num_programs(0) - 1)
    def _():
        row = lax.broadcasted_iota(jnp.int32, (128, 128), 0)
        column = lax.broadcasted_iota(jnp.int32, (128, 128), 1)
        mirror = jnp.where(row + column == 127, 1.0, 0.0).astype(BF16)
        for head in range(12):
            part = dbias[head // 2, (head % 2) * 128 : (head % 2) * 128 + 128]
            high = part.astype(BF16)
            rest = part - high.astype(F32)
            middle = rest.astype(BF16)
            low = (rest - middle.astype(F32)).astype(BF16)
            flipped = times(high, mirror) + times(middle, mirror) + times(low, mirror)
            drel[head : head + 1] = down(pltpu.roll(flipped, 0, 1, stride=1, stride_axis=0))


def attention_backward(inputs, dh2, square, vectors, head_row, kept):
    tokens, width = inputs.shape
    q, k, v, p, o, h1, cq, ck, cv, pc, co = kept
    steps = tokens // TOKENS
    items = TOKENS // 128
    slots = ck.shape[0]
    t, m = by_rows(TOKENS, width), by_rows(SLOTS, width)
    ps, cs = by_items(items, 6, 256, 128), by_items(items, 6, 256, SLOTS // items)
    token = jax.ShapeDtypeStruct((tokens, width), BF16)
    slot = jax.ShapeDtypeStruct((slots, width), BF16)
    return pl.pallas_call(
        attention_back_kernel,
        grid=(steps,),
        out_shape=(
            token, slot, token, token, slot, slot, token, token, token, token,
            jax.ShapeDtypeStruct((18, width), F32),
            jax.ShapeDtypeStruct((12, 128), F32),
        ),
        in_specs=[
            t, t, whole(square.shape), whole(vectors.shape), whole(head_row.shape),
            t, t, t, ps, t, t, t, m, m, cs, t,
        ],
        out_specs=(
            t, m, t, t, m, m, t, t, t, t,
            pl.BlockSpec((18, width), lambda i: (0, 0)),
            pl.BlockSpec((12, 128), lambda i: (0, 0)),
        ),
        scratch_shapes=[
            pltpu.VMEM((TOKENS, width), BF16),
            pltpu.VMEM((TOKENS, width), F32),
            pltpu.VMEM((6, 256, 128), F32),
        ],
        compiler_params=pltpu.CompilerParams(vmem_limit_bytes=60 << 20),
        cost_estimate=pl.CostEstimate(flops=16_000_000_000, bytes_accessed=60_000_000, transcendentals=0),
    )(inputs, dh2, square, vectors, head_row, q, k, v, p, o, h1, cq, ck, cv, pc, co)


AXES = ("tall", "square", "row")
MESH = pl.DeviceIdType.MESH


def place():
    z, plane, core = lax.axis_index("tall"), lax.axis_index("square"), lax.axis_index("row")
    return z, lax.div(plane, 2), lax.rem(plane, 2), core


def device(z, y, x, core):
    return (z, y * 2 + x, core)


def greet(partners):
    barrier = pltpu.get_barrier_semaphore()
    for partner in partners:
        pl.semaphore_signal(barrier, inc=1, device_id=partner, device_id_type=MESH)
    pl.semaphore_wait(barrier, len(partners))


def reduce_kernel(groups, has_small, *refs):
    n = len(groups)
    ins, refs = refs[:n], refs[n:]
    if has_small:
        small, refs = refs[0], refs[1:]
    outs, refs = refs[:n], refs[n:]
    if has_small:
        small_out, refs = refs[0], refs[1:]
    z, y, x, core = place()
    other = 1 - core
    sibling = device(z, y, x, other)
    across = {"x": device(z, y, 1 - x, core), "y": device(z, 1 - y, x, core)}
    along = [device(lax.rem(z + k, 4), y, x, core) for k in (1, 2, 3)]
    greet([sibling, across["x"], across["y"]] + along)
    mine = core * 384
    theirs = other * 384

    if has_small:
        held, total, refs = refs[0], refs[1], refs[2:]
        small_send, small_recv, refs = refs[0], refs[1], refs[2:]

        def small_copies(stage):
            source = small if stage == 0 else total.at[stage - 1]
            if stage < 3:
                partner = (sibling, across["x"], across["y"])[stage]
                return [
                    pltpu.make_async_remote_copy(
                        source, held.at[stage], small_send.at[stage], small_recv.at[stage],
                        device_id=partner, device_id_type=MESH,
                    )
                ]
            return [
                pltpu.make_async_remote_copy(
                    source, held.at[3 + z], small_send.at[3 + k], small_recv.at[3 + k],
                    device_id=along[k], device_id_type=MESH,
                )
                for k in range(3)
            ]

        for copy in small_copies(0):
            copy.start()

        def small_step(stage):
            for copy in small_copies(stage):
                copy.wait_recv()
            if stage < 3:
                own = small if stage == 0 else total.at[stage - 1]
                total[stage] = own[...] + held[stage]
                if stage == 2:
                    held[3 + z] = total[2]
                for copy in small_copies(stage + 1):
                    copy.start()
            else:
                small_out[...] = ((held[3] + held[4]) + held[5]) + held[6]
    else:
        def small_step(stage):
            pass

    plans = []
    for g, (pieces, rows, width, by_column) in enumerate(groups):
        r0, r1, r2, r3, f3, r4, send, recv = refs[8 * g : 8 * g + 8]
        plans.append((pieces, rows, width, by_column, ins[g], outs[g], r0, r1, r2, r3, f3, r4, send, recv))

    def where(plan, order, i):
        pieces, by_column, width = plan[0], plan[3], plan[2]
        j = i + order * (pieces // 2)
        if by_column:
            return j, order, pl.multiple_of(i * width, 128)
        return j, j, 0

    def copies(plan, stage, order, i):
        pieces, rows, width, by_column, src, out, r0, r1, r2, r3, f3, r4, send, recv = plan
        j, matrix, column = where(plan, order, i)
        first = "xy"[order]

        def make(source, target, slot, partner):
            return pltpu.make_async_remote_copy(
                source, target, send.at[slot, j], recv.at[slot, j],
                device_id=partner, device_id_type=MESH,
            )

        if stage == 0:
            lanes = pl.ds(pl.multiple_of(theirs + column, 128), width)
            return [make(src.at[matrix, :, :, :, :, lanes], r0.at[j], 0, sibling)]
        if stage == 1:
            part = r0.at[j, :, :, 1 - x] if order == 0 else r0.at[j, :, 1 - y]
            return [make(part, r1.at[j], 1, across[first])]
        if stage == 2:
            return [
                make(r1.at[j, lax.rem(z + k + 1, 4)], r2.at[j, k], 2 + k, along[k])
                for k in range(3)
            ]
        if stage == 3:
            part = r2.at[j, 0, 1 - y] if order == 0 else r2.at[j, 0, 1 - x]
            return [make(part, r3.at[j], 5, across["yx"[order]])]
        share = rows // 2
        return [make(f3.at[j, pl.ds(pl.multiple_of(other * share, 8), share)], r4.at[j], 6, sibling)]

    f32 = jnp.float32

    def add(plan, stage, order, i):
        pieces, rows, width, by_column, src, out, r0, r1, r2, r3, f3, r4, send, recv = plan
        j, matrix, column = where(plan, order, i)
        if stage == 0:
            lanes = pl.ds(pl.multiple_of(mine + column, 128), width)

            @pl.loop(0, 16)
            def _(block):
                a, b, d = lax.div(block, 4), lax.rem(lax.div(block, 2), 2), lax.rem(block, 2)
                r0[j, a, b, d] = (
                    r0[j, a, b, d].astype(f32) + src[matrix, a, b, d, :, lanes].astype(f32)
                ).astype(jnp.bfloat16)
        elif stage == 1:
            @pl.loop(0, 8)
            def _(block):
                a, b = lax.div(block, 2), lax.rem(block, 2)
                own = r0[j, a, b, x] if order == 0 else r0[j, a, y, b]
                r1[j, a, b] = (r1[j, a, b].astype(f32) + own.astype(f32)).astype(jnp.bfloat16)
        elif stage == 2:
            for b in range(2):
                r2[j, 0, b] = (
                    (r2[j, 0, b].astype(f32) + r2[j, 1, b].astype(f32))
                    + (r2[j, 2, b].astype(f32) + r1[j, z, b].astype(f32))
                ).astype(jnp.bfloat16)
        elif stage == 3:
            own = r2[j, 0, y] if order == 0 else r2[j, 0, x]
            f3[j] = r3[j].astype(f32) + own.astype(f32)
        else:
            share = rows // 2
            lanes = pl.ds(pl.multiple_of(mine + column, 128), width)
            out[matrix, :, lanes] = f3[j, pl.ds(pl.multiple_of(core * share, 8), share)]
            lanes = pl.ds(pl.multiple_of(theirs + column, 128), width)
            out[matrix, :, lanes] = r4[j]

    def each(plan, body):
        @pl.loop(0, plan[0] // 2)
        def _(i):
            for order in range(2):
                body(order, i)

    def start(plan, stage):
        def body(order, i):
            for copy in copies(plan, stage, order, i):
                copy.start()

        each(plan, body)

    def step(plan, stage):
        def body(order, i):
            for copy in copies(plan, stage, order, i):
                copy.wait_recv()
            add(plan, stage, order, i)
            if stage < 4:
                for copy in copies(plan, stage + 1, order, i):
                    copy.start()

        each(plan, body)

    def finish(plan, stage):
        def body(order, i):
            for copy in copies(plan, stage, order, i):
                copy.wait_send()

        each(plan, body)

    for plan in plans:
        start(plan, 0)
    for stage in range(5):
        if stage < 4:
            small_step(stage)
        for plan in plans:
            step(plan, stage)
    for stage in range(5):
        for plan in plans:
            finish(plan, stage)
    if has_small:
        for stage in range(4):
            for copy in small_copies(stage):
                copy.wait_send()


def reduce_scatter(arrays, small, collective_id):
    groups, views, outs, scratch = [], [], [], []
    bf16, f32 = jnp.bfloat16, jnp.float32
    if small is not None:
        scratch += [
            pltpu.VMEM((7,) + small.shape, f32),
            pltpu.VMEM((3,) + small.shape, f32),
            pltpu.SemaphoreType.DMA((6,)),
            pltpu.SemaphoreType.DMA((6,)),
        ]
    for array in arrays:
        matrices, height, width_all = array.shape
        rows = height // 16
        by_column = matrices == 2
        pieces, width = (6, 128) if by_column else (matrices, 384)
        groups.append((pieces, rows, width, by_column))
        views.append(array.reshape(matrices, 4, 2, 2, rows, width_all))
        outs.append(jax.ShapeDtypeStruct((matrices, rows // 2, width_all), f32))
        scratch += [
            pltpu.VMEM((pieces, 4, 2, 2, rows, width), bf16),
            pltpu.VMEM((pieces, 4, 2, rows, width), bf16),
            pltpu.VMEM((pieces, 3, 2, rows, width), bf16),
            pltpu.VMEM((pieces, rows, width), bf16),
            pltpu.VMEM((pieces, rows, width), f32),
            pltpu.VMEM((pieces, rows // 2, width), f32),
            pltpu.SemaphoreType.DMA((7, pieces)),
            pltpu.SemaphoreType.DMA((7, pieces)),
        ]
    if small is not None:
        views.append(small)
        outs.append(jax.ShapeDtypeStruct(small.shape, f32))
    vmem = pl.BlockSpec(memory_space=pltpu.VMEM)
    return pl.pallas_call(
        functools.partial(reduce_kernel, tuple(groups), small is not None),
        out_shape=tuple(outs),
        in_specs=[vmem] * len(views),
        out_specs=tuple([vmem] * len(outs)),
        scratch_shapes=scratch,
        compiler_params=pltpu.CompilerParams(
            collective_id=collective_id, has_side_effects=True, vmem_limit_bytes=60 << 20
        ),
    )(*views)


def gram_kernel(gram, out, other_sum, half_a, half_b, final, send, recv):
    z, y, x, core = place()
    sibling = device(z, y, x, 1 - core)
    x_side, y_side = device(z, y, 1 - x, core), device(z, 1 - y, x, core)
    greet([sibling, x_side, y_side])
    side = gram.shape[0] // 2
    rows = pl.ds(pl.multiple_of(core * side, 8), side)
    rest = pl.ds(pl.multiple_of((1 - core) * side, 8), side)

    def send_to(source, target, slot, partner):
        return pltpu.make_async_remote_copy(
            source, target, send.at[slot], recv.at[slot], device_id=partner, device_id_type=MESH
        )

    first = send_to(gram.at[rest], other_sum.at[rest], 0, sibling)
    second = send_to(gram.at[rows], other_sum.at[rows], 1, sibling)
    first.start()
    second.start()
    mine = send_to(gram.at[rows], other_sum.at[rows], 0, sibling)
    mine.wait_recv()
    out[rows] = gram[rows] + other_sum[rows]
    theirs = send_to(gram.at[rest], other_sum.at[rest], 1, sibling)
    theirs.wait_recv()

    @pl.when(z < 2)
    def _():
        out[rest] = gram[rest] + other_sum[rest]

    @pl.when(z >= 2)
    def _():
        def pair(one, two):
            step = send_to(out.at[rows], half_a, 2, one)
            step.start()
            step.wait_recv()
            step.wait_send()
            half_b[...] = out[rows] + half_a[...]
            step = send_to(half_b, final, 3, two)
            step.start()
            step.wait_recv()
            out[rows] = half_b[...] + final[...]
            step.wait_send()

        @pl.when(core == 0)
        def _():
            pair(x_side, y_side)

        @pl.when(core == 1)
        def _():
            pair(y_side, x_side)

        last = send_to(out.at[rows], out.at[rows], 4, sibling)
        last.start()
        arrive = send_to(out.at[rest], out.at[rest], 4, sibling)
        arrive.wait_recv()
        last.wait_send()

    first.wait_send()
    second.wait_send()


def gram_sum(gram, collective_id):
    f32 = jnp.float32
    side = gram.shape[0] // 2
    vmem = pl.BlockSpec(memory_space=pltpu.VMEM)
    return pl.pallas_call(
        gram_kernel,
        out_shape=jax.ShapeDtypeStruct(gram.shape, f32),
        in_specs=[vmem],
        out_specs=vmem,
        scratch_shapes=[
            pltpu.VMEM(gram.shape, f32),
            pltpu.VMEM((side, gram.shape[1]), f32),
            pltpu.VMEM((side, gram.shape[1]), f32),
            pltpu.VMEM((side, gram.shape[1]), f32),
            pltpu.SemaphoreType.DMA((5,)),
            pltpu.SemaphoreType.DMA((5,)),
        ],
        compiler_params=pltpu.CompilerParams(
            collective_id=collective_id, has_side_effects=True, vmem_limit_bytes=32 << 20
        ),
    )(gram)


def matmul3(left, right):
    return jnp.matmul(left, right, precision=lax.Precision.HIGH)


def to_owner_rows(square_state, tall_state, count):
    rows = square_state.shape[1]
    group = count // 16
    if rows % group == 0:
        piece = rows // group
        pieces = jnp.concatenate(
            [
                square_state.reshape(8 * group, piece, D),
                tall_state.reshape(8 * group, piece, D),
            ],
            axis=0,
        ).astype(jnp.bfloat16)
        return lax.all_to_all(pieces, AXES, 0, 0, tiled=True).reshape(count * piece, D)
    square_all = lax.all_gather(square_state.astype(jnp.bfloat16), AXES, axis=1, tiled=True)
    tall_all = lax.all_gather(tall_state.astype(jnp.bfloat16), AXES, axis=1, tiled=True)
    joined = jnp.concatenate([square_all.reshape(-1, D), tall_all.reshape(-1, D)], axis=0)
    own = joined.shape[0] // count
    return lax.dynamic_slice_in_dim(joined, lax.axis_index(AXES) * own, own, axis=0)


def from_owner_rows(rows_out, count, square_rows, tall_rows):
    group = count // 16
    rows_out = rows_out.astype(jnp.bfloat16)
    if square_rows % group == 0:
        piece = square_rows // group
        back = lax.all_to_all(rows_out.reshape(count, piece, D), AXES, 0, 0, tiled=True)
        return (
            back[: 8 * group].reshape(8, square_rows, D),
            back[8 * group :].reshape(2, tall_rows, D),
        )
    joined = lax.all_gather(rows_out, AXES, axis=0, tiled=True)
    square_all = joined[: 8 * square_rows * count].reshape(8, square_rows * count, D)
    tall_all = joined[8 * square_rows * count :].reshape(2, tall_rows * count, D)
    index = lax.axis_index(AXES)
    return (
        lax.dynamic_slice_in_dim(square_all, index * square_rows, square_rows, axis=1),
        lax.dynamic_slice_in_dim(tall_all, index * tall_rows, tall_rows, axis=1),
    )


def orthogonal_rows(rows_in, kernels):
    rows_in = rows_in.astype(jnp.float32)
    gram = jnp.einsum("rd,re->de", rows_in, rows_in, precision=lax.Precision.HIGHEST)
    if kernels:
        gram = gram_sum(gram, 2)
    else:
        gram = lax.psum(gram, "row")
        is_tall = lax.axis_index("tall") >= 2
        gram = jnp.where(is_tall, lax.psum(jnp.where(is_tall, gram, 0.0), "square"), gram)
    eye = (jnp.arange(D)[:, None] == jnp.arange(D)[None, :]).astype(jnp.float32)
    scale = 1.0 / (jnp.sqrt(jnp.sum(gram * eye)) + FLOOR_EPSILON)
    gram = gram * (scale * scale)
    current = rows_in * scale

    for sweep in range(ITERS):
        poly = FIRST_TERM * eye + SECOND_TERM * gram + THIRD_TERM * matmul3(gram, gram)
        current = matmul3(current, poly)
        if sweep < ITERS - 1:
            gram = matmul3(matmul3(gram, poly), poly)
    return current


def local(
    inputs,
    memory,
    cotangent,
    lengths,
    memory_len,
    square_master,
    tall_master,
    square_momentum,
    tall_momentum,
    vectors,
    feed_vectors,
    head_scale,
    relative,
):
    count = lax.axis_size(AXES)
    kernels = count == 32
    index = lax.axis_index(AXES)
    square_copy, tall_copy = (
        lax.all_gather(square_master.astype(jnp.bfloat16), AXES, axis=1, tiled=True),
        lax.all_gather(tall_master.astype(jnp.bfloat16), AXES, axis=1, tiled=True),
    )
    width = inputs.shape[2]
    vec, feed = vectors.astype(F32), feed_vectors.astype(F32)
    head_row = jnp.repeat(head_scale.astype(F32), width // head_scale.shape[0])[None]
    at = jnp.arange(inputs.shape[1])
    distance = at[:, None] - at[None, :]
    table = (jnp.maximum(distance, 0)[:, :, None] == at[None, None, :]).astype(BF16)
    bias = jnp.einsum("hd,qkd->hqk", relative, table, preferred_element_type=F32)
    bias = jnp.where(distance >= 0, bias, NEGATIVE_LARGE).reshape(6, 256, 128)
    flat_in, flat_memory = inputs.reshape(-1, width), memory.reshape(-1, width)
    n1, q, k, v, p, o, m1, h1, n2, cq, ck, cv, pc, co, m2, h2 = attention_forward(
        flat_in, flat_memory, memory_len, square_copy, vec, head_row, bias
    )
    output, dh2, n3, r, du, dy, late_slope, feed_slope = feed_both(
        h2, cotangent.reshape(-1, width), lengths, tall_copy, vec, feed
    )

    def weight_slope(left, right):
        return lax.dot_general(
            left, right, (((0,), (0,)), ((), ())), preferred_element_type=F32
        ).astype(BF16)

    tall_slope = jnp.stack([weight_slope(du, n3), weight_slope(r, dy)])
    tall_slope, dh2 = lax.optimization_barrier((tall_slope, dh2))
    tall_sum = lax.psum_scatter(tall_slope, AXES, scatter_dimension=1, tiled=True).astype(F32)
    input_slope, memory_slope, dy2, dcq, dck, dcv, dy1, dq, dk, dv, early_slope, bias_slope = (
        attention_backward(
            flat_in, dh2, square_copy, vec, head_row,
            (q, k, v, p, o, h1, cq, ck, cv, pc, co),
        )
    )
    square_slope = jnp.stack(
        [
            weight_slope(left, right)
            for left, right in (
                (n1, dq), (n1, dk), (n1, dv), (m1, dy1),
                (n2, dcq), (flat_memory, dck), (flat_memory, dcv), (m2, dy2),
            )
        ]
    )
    vector_slope = jnp.concatenate([early_slope[:14], late_slope], axis=0)
    scale_slope = jnp.sum(early_slope[17].reshape(head_scale.shape[0], -1), axis=1)
    bias_slope = jnp.roll(bias_slope, 1, axis=1)
    small = [
        jnp.sum(lengths).astype(jnp.float32).reshape(1),
        scale_slope.reshape(-1),
        bias_slope.reshape(-1),
        vector_slope.reshape(-1),
        feed_slope.reshape(-1),
    ]
    sizes = [piece.shape[0] for piece in small]
    starts = [sum(sizes[:i]) for i in range(len(sizes) + 1)]
    if kernels:
        lines = -(-starts[-1] // 1024) * 8
        small.append(jnp.zeros((lines * 128 - starts[-1],), jnp.float32))
        square_sum, summed = reduce_scatter(
            [square_slope], jnp.concatenate(small).reshape(lines, 128), 1
        )
        summed = summed.reshape(-1)
    else:
        square_sum = lax.psum_scatter(
            square_slope, AXES, scatter_dimension=1, tiled=True
        ).astype(jnp.float32)
        summed = lax.psum(jnp.concatenate(small), AXES)
    total, scale_sum, bias_sum, vector_sum, feed_sum = (
        summed[starts[i] : starts[i + 1]] for i in range(len(sizes))
    )
    factor = inputs.shape[0] * count / total[0]
    bias_sum = bias_sum.reshape(bias_slope.shape)
    width = vector_slope.shape[1] // count
    vector_sum = lax.dynamic_slice_in_dim(
        vector_sum.reshape(vector_slope.shape), index * width, width, axis=1
    )
    width = feed_slope.shape[1] // count
    feed_sum = lax.dynamic_slice_in_dim(
        feed_sum.reshape(feed_slope.shape), index * width, width, axis=1
    )
    square_state = MOMENTUM_DECAY * square_momentum + factor * square_sum
    tall_state = MOMENTUM_DECAY * tall_momentum + factor * tall_sum
    rows_out = orthogonal_rows(to_owner_rows(square_state, tall_state, count), kernels)
    square, tall = from_owner_rows(
        rows_out, count, square_state.shape[1], tall_state.shape[1]
    )
    square, tall = square.astype(jnp.float32), tall.astype(jnp.float32)
    square_weight = square_master * (1.0 - LEARN_RATE * WEIGHT_DECAY) - LEARN_RATE * square
    tall_weight = (
        tall_master * (1.0 - LEARN_RATE * WEIGHT_DECAY)
        - LEARN_RATE * max(1.0, FF / D) ** 0.5 * tall
    )
    return (
        output.reshape(inputs.shape),
        input_slope.reshape(inputs.shape),
        memory_slope.reshape(memory.shape),
        square_state,
        tall_state,
        square_weight,
        tall_weight,
        factor * vector_sum,
        factor * feed_sum,
        factor * scale_sum,
        factor * bias_sum,
    )


def solution(mesh):
    count = mesh.devices.size
    grouped = Mesh(mesh.devices.reshape(4, 4, count // 16), AXES)
    placed = (
        P(AXES, None, None),
        P(AXES, None, None),
        P(AXES, None, None),
        P(AXES),
        P(AXES),
        P(None, AXES, None),
        P(None, AXES, None),
        P(None, AXES, None),
        P(None, AXES, None),
        P(),
        P(),
        P(),
        P(),
    )
    return jax.shard_map(
        local,
        mesh=grouped,
        in_specs=placed,
        out_specs=(
            P(AXES, None, None),
            P(AXES, None, None),
            P(AXES, None, None),
            P(None, AXES, None),
            P(None, AXES, None),
            P(None, AXES, None),
            P(None, AXES, None),
            P(None, AXES),
            P(None, AXES),
            P(),
            P(),
        ),
        check_vma=False,
    )
```

```python
import functools

import jax
import jax.numpy as jnp
from jax import lax
from jax.experimental import pallas as pl
from jax.experimental.pallas import tpu as pltpu
from jax.sharding import Mesh, PartitionSpec as P

D = 768
FF = 3072
ITERS = 5


NORM_EPSILON = 1e-05
FLOOR_EPSILON = 1e-07
FIRST_TERM = 3.4445
SECOND_TERM = -4.775
THIRD_TERM = 2.0315
MOMENTUM_DECAY = 0.95
LEARN_RATE = 0.8
WEIGHT_DECAY = 0.01
NEGATIVE_LARGE = -1e30


F32, BF16 = jnp.float32, jnp.bfloat16
TOKENS = 256
SLOTS = 512
LANES = 128


def times(left, right):
    return jnp.dot(left, right, preferred_element_type=F32)


def times_back(left, right):
    return lax.dot_general(left, right, (((1,), (1,)), ((), ())), preferred_element_type=F32)


def times_down(left, right):
    return lax.dot_general(left, right, (((0,), (0,)), ((), ())), preferred_element_type=F32)


def standard(values):
    center = values - jnp.mean(values, axis=-1, keepdims=True)
    scale = lax.rsqrt(jnp.mean(center * center, axis=-1, keepdims=True) + NORM_EPSILON)
    return center * scale, scale


def norm(values, gain, shift):
    return standard(values)[0] * gain + shift


def norm_back(values, slope, gain):
    hat, scale = standard(values)
    inner = slope * gain
    back = scale * (
        inner
        - jnp.mean(inner, axis=-1, keepdims=True)
        - hat * jnp.mean(inner * hat, axis=-1, keepdims=True)
    )
    return back, down(slope * hat), down(slope)


def down(values):
    return jnp.sum(values, axis=0, keepdims=True)


def head_masks():
    lane = lax.broadcasted_iota(jnp.int32, (1, LANES), 1)
    even = jnp.where(lane < LANES // 2, 1.0, 0.0)
    return even.astype(BF16), (1.0 - even).astype(BF16)


def stacked(pair, masks):
    return jnp.concatenate([pair * masks[0], pair * masks[1]], axis=0)


def side_by_side(rows):
    half = rows.shape[0] // 2
    return jnp.concatenate([rows[:half], rows[half:]], axis=1)


def soften(scores):
    weights = jnp.exp(scores - jnp.max(scores, axis=-1, keepdims=True))
    return (weights * (1.0 / jnp.sum(weights, axis=-1, keepdims=True))).astype(BF16)


def soften_back(weights, slope):
    weights = weights.astype(F32)
    product = weights * slope
    return (product - weights * jnp.sum(product, axis=-1, keepdims=True)).astype(BF16)


def attention_kernel(
    memory_len, x_in, memory, w, vec, hs, bias,
    left, q, k, v, p, o, h1, cq, ck, cv, pc, co, h2,
):
    step = pl.program_id(0)
    masks = head_masks()
    x = x_in[...].astype(F32)
    left[0] = norm(x, vec[0:1], vec[1:2]).astype(BF16)
    q[...] = ((times(left[0], w[0]) + vec[2:3]) * 0.125).astype(BF16)
    k[...] = times(left[0], w[1]).astype(BF16)
    v[...] = (times(left[0], w[2]) + vec[3:4]).astype(BF16)
    items = TOKENS // 128

    @pl.loop(0, 6, unroll=True)
    def _(pair):
        lanes = pl.ds(pl.multiple_of(pair * LANES, LANES), LANES)
        for item in range(items):
            rows = slice(item * 128, item * 128 + 128)
            scores = times_back(stacked(q[rows, lanes], masks), k[rows, lanes]) + bias[pair]
            weights = soften(scores)
            p[item, pair] = weights
            o[rows, lanes] = times(side_by_side(weights), stacked(v[rows, lanes], masks))

    left[1] = norm(o[...] * hs[...], vec[5:6], vec[6:7]).astype(BF16)
    h1[...] = x + (times(left[1], w[3]) + vec[4:5])
    left[2] = norm(h1[...], vec[7:8], vec[8:9]).astype(BF16)
    cq[...] = ((times(left[2], w[4]) + vec[9:10]) * 0.125).astype(BF16)
    ck[...] = times(memory[...], w[5]).astype(BF16)
    cv[...] = (times(memory[...], w[6]) + vec[10:11]).astype(BF16)
    slots = SLOTS // items
    column = lax.broadcasted_iota(jnp.int32, (1, slots), 1)

    @pl.loop(0, 6, unroll=True)
    def _(pair):
        lanes = pl.ds(pl.multiple_of(pair * LANES, LANES), LANES)
        for item in range(items):
            rows = slice(item * 128, item * 128 + 128)
            keys = slice(item * slots, item * slots + slots)
            limit = memory_len[step * items + item]
            scores = times_back(stacked(cq[rows, lanes], masks), ck[keys, lanes])
            weights = soften(jnp.where(column < limit, scores, NEGATIVE_LARGE))
            pc[item, pair] = weights
            co[rows, lanes] = times(side_by_side(weights), stacked(cv[keys, lanes], masks))

    left[3] = norm(co[...], vec[12:13], vec[13:14]).astype(BF16)
    h2[...] = h1[...] + (times(left[3], w[7]) + vec[11:12])


def whole(shape):
    return pl.BlockSpec(shape, lambda *_: (0,) * len(shape), pipeline_mode=pl.Buffered(1))


def by_rows(rows, width):
    return pl.BlockSpec((rows, width), lambda i: (i, 0))


def by_blocks(blocks, rows, width):
    return pl.BlockSpec((blocks, rows, width), lambda i: (0, i, 0))


def by_items(items, *rest):
    return pl.BlockSpec((items,) + rest, lambda i: (i,) + (0,) * len(rest))


def attention_forward(inputs, memory, memory_len, square, vectors, head_row, bias):
    tokens, width = inputs.shape
    slots = memory.shape[0]
    steps = tokens // TOKENS
    items = TOKENS // 128
    shapes = [
        (BF16, "l"), (BF16, "t"), (BF16, "t"), (BF16, "t"), (BF16, "p"), (F32, "t"), (F32, "t"),
        (BF16, "t"), (BF16, "m"), (BF16, "m"), (BF16, "c"), (F32, "t"), (F32, "t"),
    ]
    full = {"l": (4, tokens, width), "t": (tokens, width), "m": (slots, width), "p": (steps * items, 6, 256, 128), "c": (steps * items, 6, 256, SLOTS // items)}
    spec = {
        "l": by_blocks(4, TOKENS, width),
        "t": by_rows(TOKENS, width), "m": by_rows(SLOTS, width),
        "p": by_items(items, 6, 256, 128), "c": by_items(items, 6, 256, SLOTS // items),
    }
    return pl.pallas_call(
        attention_kernel,
        grid=(steps,),
        out_shape=tuple(jax.ShapeDtypeStruct(full[kind], kept) for kept, kind in shapes),
        in_specs=[
            pl.BlockSpec(memory_space=pltpu.SMEM),
            spec["t"], spec["m"], whole(square.shape), whole(vectors.shape), whole(head_row.shape), whole(bias.shape),
        ],
        out_specs=tuple(spec[kind] for _, kind in shapes),
        compiler_params=pltpu.CompilerParams(vmem_limit_bytes=60 << 20),
        cost_estimate=pl.CostEstimate(flops=14_000_000_000, bytes_accessed=60_000_000, transcendentals=5_000_000),
    )(memory_len, inputs, memory, square, vectors, head_row, bias)


ROOT_HALF = 0.7071067811865476
INVERSE_ROOT = 0.3989422804014327
CHUNK = 1024


def feed_kernel(
    lengths, h2_in, cot, tall, vec, feed,
    out, dh2, narrow, wide, dvec, dfeed,
    u, g, dr, total,
):
    step = pl.program_id(0)
    items = TOKENS // 128
    width = tall.shape[1]
    chunks = width // CHUNK

    @pl.when(step == 0)
    def _():
        dvec[...] = jnp.zeros_like(dvec)
        dfeed[...] = jnp.zeros_like(dfeed)

    h2 = h2_in[...]
    narrow[0] = norm(h2, vec[14:15], vec[15:16]).astype(BF16)

    def at(i):
        return pl.ds(pl.multiple_of(i * CHUNK, CHUNK), CHUNK)

    def first(i, total):
        some = at(i)
        inner = times_back(narrow[0], tall[0, some]) + feed[0:1, some]
        bell = 0.5 + 0.5 * lax.erf(inner * ROOT_HALF)
        active = inner * bell
        g[:, some] = active
        u[:, some] = bell + inner * (jnp.exp(-0.5 * inner * inner) * INVERSE_ROOT)
        return total + jnp.sum(active, axis=-1, keepdims=True)

    zero = jnp.zeros((TOKENS, 1), F32)
    mean = lax.fori_loop(0, chunks, first, zero, unroll=True) * (1.0 / width)

    def second(i, total):
        center = g[:, at(i)] - mean
        return total + jnp.sum(center * center, axis=-1, keepdims=True)

    spread = lax.fori_loop(0, chunks, second, zero, unroll=True) * (1.0 / width)
    scale = lax.rsqrt(spread + NORM_EPSILON)
    row = lax.broadcasted_iota(jnp.int32, (128, 1), 0)
    valid = jnp.concatenate(
        [jnp.where(row < lengths[step * items + item], 1.0, 0.0) for item in range(items)], axis=0
    )
    dy32 = cot[...].astype(F32) * valid
    narrow[1] = dy32.astype(BF16)
    total[...] = h2 + vec[16:17]

    def third(i, sums):
        some = at(i)
        hat = (g[:, some] - mean) * scale
        g[:, some] = hat
        gain = feed[1:2, some]
        active = (hat * gain + feed[2:3, some]).astype(BF16)
        wide[1, :, some] = active
        total[...] += times(active, tall[1, some])
        slope = times_back(narrow[1], tall[1, some])
        dfeed[1:2, some] += down(slope * hat)
        dfeed[2:3, some] += down(slope)
        inner = slope * gain
        dr[:, some] = inner
        return (
            sums[0] + jnp.sum(inner, axis=-1, keepdims=True),
            sums[1] + jnp.sum(inner * hat, axis=-1, keepdims=True),
        )

    one, two = lax.fori_loop(0, chunks, third, (zero, zero), unroll=True)
    out[...] = total[...].astype(BF16)
    one, two = one * (1.0 / width), two * (1.0 / width)
    dh2[...] = jnp.zeros_like(dh2)

    def fourth(i, carry):
        some = at(i)
        back = scale * (dr[:, some] - one - g[:, some] * two)
        slope = (back * u[:, some]).astype(BF16)
        wide[0, :, some] = slope
        dfeed[0:1, some] += down(slope.astype(F32))
        dh2[...] += times(slope, tall[0, some])
        return carry

    lax.fori_loop(0, chunks, fourth, 0, unroll=True)
    back, gain_sum, shift_sum = norm_back(h2, dh2[...], vec[14:15])
    dvec[0:1] += gain_sum
    dvec[1:2] += shift_sum
    dvec[2:3] += down(dy32)
    dh2[...] = dy32 + back


def feed_both(hidden, cotangent, lengths, tall, vectors, feed_vectors):
    tokens, width = hidden.shape
    wide = tall.shape[1]
    steps = tokens // TOKENS
    some = by_rows(TOKENS, width)
    return pl.pallas_call(
        feed_kernel,
        grid=(steps,),
        out_shape=(
            jax.ShapeDtypeStruct((tokens, width), BF16),
            jax.ShapeDtypeStruct((tokens, width), F32),
            jax.ShapeDtypeStruct((2, tokens, width), BF16),
            jax.ShapeDtypeStruct((2, tokens, wide), BF16),
            jax.ShapeDtypeStruct((3, width), F32),
            jax.ShapeDtypeStruct((3, wide), F32),
        ),
        in_specs=[
            pl.BlockSpec(memory_space=pltpu.SMEM),
            some, some, whole(tall.shape), whole(vectors.shape), whole(feed_vectors.shape),
        ],
        out_specs=(
            some, some, by_blocks(2, TOKENS, width), by_blocks(2, TOKENS, wide),
            pl.BlockSpec((3, width), lambda i: (0, 0)),
            pl.BlockSpec((3, wide), lambda i: (0, 0)),
        ),
        scratch_shapes=[pltpu.VMEM((TOKENS, wide), F32)] * 3 + [pltpu.VMEM((TOKENS, width), F32)],
        compiler_params=pltpu.CompilerParams(vmem_limit_bytes=60 << 20),
        cost_estimate=pl.CostEstimate(flops=20_000_000_000, bytes_accessed=40_000_000, transcendentals=7_000_000),
    )(lengths, hidden, cotangent, tall, vectors, feed_vectors)


def attention_back_kernel(
    x_in, dh2, w, vec, hs,
    q, k, v, p, o, h1, cq, ck, cv, pc, co,
    dx, dmem, right, far, dvec, drel,
    do, dh1, dbias,
):
    step = pl.program_id(0)
    masks = head_masks()
    items = TOKENS // 128
    slots = SLOTS // items

    @pl.when(step == 0)
    def _():
        dvec[...] = jnp.zeros_like(dvec)
        dbias[...] = jnp.zeros_like(dbias)

    def note(row, value):
        dvec[row : row + 1] += value

    right[5] = dh2[...].astype(BF16)
    note(11, down(right[5].astype(F32)))
    back, gain_sum, shift_sum = norm_back(co[...], times_back(right[5], w[7]), vec[12:13])
    note(12, gain_sum)
    note(13, shift_sum)
    do[...] = back.astype(BF16)

    def through(pair, item, keys, query, key, value, weights, dquery, dkey, dvalue, with_bias):
        lanes = pl.ds(pl.multiple_of(pair * LANES, LANES), LANES)
        rows = slice(item * 128, item * 128 + 128)
        kept = weights[item, pair]
        grad = stacked(do[rows, lanes], masks)
        dvalue[keys, lanes] = times_down(kept, grad).astype(BF16)
        slope = soften_back(kept, times_back(grad, value[keys, lanes]))
        dquery[rows, lanes] = (
            times(side_by_side(slope), stacked(key[keys, lanes], masks)).astype(BF16) * 0.125
        ).astype(BF16)
        dkey[keys, lanes] = times_down(slope, stacked(query[rows, lanes], masks)).astype(BF16)
        if with_bias:
            dbias[pair] += slope.astype(F32)

    @pl.loop(0, 6, unroll=True)
    def _(pair):
        for item in range(items):
            keys = slice(item * slots, item * slots + slots)
            through(pair, item, keys, cq, ck, cv, pc, right.at[4], far.at[0], far.at[1], False)

    note(9, down(right[4].astype(F32)))
    note(10, down(far[1].astype(F32)))
    dmem[...] = (times_back(far[0], w[5]) + times_back(far[1], w[6])).astype(BF16)
    back, gain_sum, shift_sum = norm_back(h1[...], times_back(right[4], w[4]), vec[7:8])
    note(7, gain_sum)
    note(8, shift_sum)
    dh1[...] = dh2[...] + back
    right[3] = dh1[...].astype(BF16)
    note(4, down(right[3].astype(F32)))
    back, gain_sum, shift_sum = norm_back(o[...] * hs[...], times_back(right[3], w[3]), vec[5:6])
    note(5, gain_sum)
    note(6, shift_sum)
    note(17, down(back * o[...]))
    do[...] = (back * hs[...]).astype(BF16)

    @pl.loop(0, 6, unroll=True)
    def _(pair):
        for item in range(items):
            rows = slice(item * 128, item * 128 + 128)
            through(pair, item, rows, q, k, v, p, right.at[0], right.at[1], right.at[2], True)

    note(2, down(right[0].astype(F32)))
    note(3, down(right[2].astype(F32)))
    slope = times_back(right[0], w[0]) + times_back(right[1], w[1]) + times_back(right[2], w[2])
    back, gain_sum, shift_sum = norm_back(x_in[...].astype(F32), slope, vec[0:1])
    note(0, gain_sum)
    note(1, shift_sum)
    dx[...] = (dh1[...] + back).astype(BF16)

    @pl.when(step == pl.num_programs(0) - 1)
    def _():
        row = lax.broadcasted_iota(jnp.int32, (128, 128), 0)
        column = lax.broadcasted_iota(jnp.int32, (128, 128), 1)
        mirror = jnp.where(row + column == 127, 1.0, 0.0).astype(BF16)
        for head in range(12):
            part = dbias[head // 2, (head % 2) * 128 : (head % 2) * 128 + 128]
            high = part.astype(BF16)
            rest = part - high.astype(F32)
            middle = rest.astype(BF16)
            low = (rest - middle.astype(F32)).astype(BF16)
            flipped = times(high, mirror) + times(middle, mirror) + times(low, mirror)
            drel[head : head + 1] = down(pltpu.roll(flipped, 0, 1, stride=1, stride_axis=0))


def attention_backward(inputs, dh2, square, vectors, head_row, kept):
    tokens, width = inputs.shape
    q, k, v, p, o, h1, cq, ck, cv, pc, co = kept
    steps = tokens // TOKENS
    items = TOKENS // 128
    slots = ck.shape[0]
    t, m = by_rows(TOKENS, width), by_rows(SLOTS, width)
    ps, cs = by_items(items, 6, 256, 128), by_items(items, 6, 256, SLOTS // items)
    token = jax.ShapeDtypeStruct((tokens, width), BF16)
    slot = jax.ShapeDtypeStruct((slots, width), BF16)
    return pl.pallas_call(
        attention_back_kernel,
        grid=(steps,),
        out_shape=(
            token, slot,
            jax.ShapeDtypeStruct((6, tokens, width), BF16),
            jax.ShapeDtypeStruct((2, slots, width), BF16),
            jax.ShapeDtypeStruct((18, width), F32),
            jax.ShapeDtypeStruct((12, 128), F32),
        ),
        in_specs=[
            t, t, whole(square.shape), whole(vectors.shape), whole(head_row.shape),
            t, t, t, ps, t, t, t, m, m, cs, t,
        ],
        out_specs=(
            t, m, by_blocks(6, TOKENS, width), by_blocks(2, SLOTS, width),
            pl.BlockSpec((18, width), lambda i: (0, 0)),
            pl.BlockSpec((12, 128), lambda i: (0, 0)),
        ),
        scratch_shapes=[
            pltpu.VMEM((TOKENS, width), BF16),
            pltpu.VMEM((TOKENS, width), F32),
            pltpu.VMEM((6, 256, 128), F32),
        ],
        compiler_params=pltpu.CompilerParams(vmem_limit_bytes=60 << 20),
        cost_estimate=pl.CostEstimate(flops=16_000_000_000, bytes_accessed=60_000_000, transcendentals=0),
    )(inputs, dh2, square, vectors, head_row, q, k, v, p, o, h1, cq, ck, cv, pc, co)


def slope_kernel(left, right, memory, far, out):
    step = pl.program_id(0)
    width = out.shape[1]

    def product(from_left, from_right):
        @pl.loop(0, width // 256)
        def _(tile):
            some = pl.ds(pl.multiple_of(tile * 256, 256), 256)
            out[0, some] = times_down(from_left[:, some], from_right[...]).astype(BF16)

    @pl.when(step < 6)
    def _():
        product(left.at[0], right.at[0])

    @pl.when(step >= 6)
    def _():
        product(memory, far.at[0])


def square_slopes(left, right, memory, far):
    _, tokens, width = left.shape
    slots = memory.shape[0]
    return pl.pallas_call(
        slope_kernel,
        grid=(8,),
        out_shape=jax.ShapeDtypeStruct((8, width, width), BF16),
        in_specs=[
            pl.BlockSpec((1, tokens, width), lambda g: (jnp.clip(g - 2, 0, 3), 0, 0)),
            pl.BlockSpec((1, tokens, width), lambda g: (jnp.minimum(g, 5), 0, 0)),
            whole(memory.shape),
            pl.BlockSpec((1, slots, width), lambda g: (jnp.maximum(g - 6, 0), 0, 0)),
        ],
        out_specs=pl.BlockSpec(
            (1, width, width),
            lambda g: (jnp.where(g < 5, g, jnp.where(g == 5, 7, g - 1)), 0, 0),
        ),
        compiler_params=pltpu.CompilerParams(vmem_limit_bytes=60 << 20),
        cost_estimate=pl.CostEstimate(flops=12_000_000_000, bytes_accessed=30_000_000, transcendentals=0),
    )(left, right, memory, far)


AXES = ("tall", "square", "row")
MESH = pl.DeviceIdType.MESH


def place():
    z, plane, core = lax.axis_index("tall"), lax.axis_index("square"), lax.axis_index("row")
    return z, lax.div(plane, 2), lax.rem(plane, 2), core


def device(z, y, x, core):
    return (z, y * 2 + x, core)


def greet(partners):
    barrier = pltpu.get_barrier_semaphore()
    for partner in partners:
        pl.semaphore_signal(barrier, inc=1, device_id=partner, device_id_type=MESH)
    pl.semaphore_wait(barrier, len(partners))


def reduce_kernel(groups, has_small, *refs):
    n = len(groups)
    ins, refs = refs[:n], refs[n:]
    if has_small:
        small, refs = refs[0], refs[1:]
    outs, refs = refs[:n], refs[n:]
    if has_small:
        small_out, refs = refs[0], refs[1:]
    z, y, x, core = place()
    other = 1 - core
    sibling = device(z, y, x, other)
    across = {"x": device(z, y, 1 - x, core), "y": device(z, 1 - y, x, core)}
    along = [device(lax.rem(z + k, 4), y, x, core) for k in (1, 2, 3)]
    greet([sibling, across["x"], across["y"]] + along)
    mine = core * 384
    theirs = other * 384

    if has_small:
        held, total, refs = refs[0], refs[1], refs[2:]
        small_send, small_recv, refs = refs[0], refs[1], refs[2:]

        def small_copies(stage):
            source = small if stage == 0 else total.at[stage - 1]
            if stage < 3:
                partner = (sibling, across["x"], across["y"])[stage]
                return [
                    pltpu.make_async_remote_copy(
                        source, held.at[stage], small_send.at[stage], small_recv.at[stage],
                        device_id=partner, device_id_type=MESH,
                    )
                ]
            return [
                pltpu.make_async_remote_copy(
                    source, held.at[3 + z], small_send.at[3 + k], small_recv.at[3 + k],
                    device_id=along[k], device_id_type=MESH,
                )
                for k in range(3)
            ]

        for copy in small_copies(0):
            copy.start()

        def small_step(stage):
            for copy in small_copies(stage):
                copy.wait_recv()
            if stage < 3:
                own = small if stage == 0 else total.at[stage - 1]
                total[stage] = own[...] + held[stage]
                if stage == 2:
                    held[3 + z] = total[2]
                for copy in small_copies(stage + 1):
                    copy.start()
            else:
                small_out[...] = ((held[3] + held[4]) + held[5]) + held[6]
    else:
        def small_step(stage):
            pass

    plans = []
    for g, (pieces, rows, width, parts) in enumerate(groups):
        r0, r1, r2, r3, f3, r4, send, recv = refs[8 * g : 8 * g + 8]
        plans.append((pieces, rows, width, parts, ins[g], outs[g], r0, r1, r2, r3, f3, r4, send, recv))

    def where(plan, order, i):
        pieces, parts, width = plan[0], plan[3], plan[2]
        j = i + order * (pieces // 2)
        return j, lax.div(j, parts), pl.multiple_of(lax.rem(j, parts) * width, 128)

    def copies(plan, stage, order, i):
        pieces, rows, width, parts, src, out, r0, r1, r2, r3, f3, r4, send, recv = plan
        j, matrix, column = where(plan, order, i)
        first = "xy"[order]

        def make(source, target, slot, partner):
            return pltpu.make_async_remote_copy(
                source, target, send.at[slot, j], recv.at[slot, j],
                device_id=partner, device_id_type=MESH,
            )

        if stage == 0:
            lanes = pl.ds(pl.multiple_of(theirs + column, 128), width)
            return [make(src.at[matrix, :, :, :, :, lanes], r0.at[j], 0, sibling)]
        if stage == 1:
            part = r0.at[j, :, :, 1 - x] if order == 0 else r0.at[j, :, 1 - y]
            return [make(part, r1.at[j], 1, across[first])]
        if stage == 2:
            part = r1.at[j, :, 1 - y] if order == 0 else r1.at[j, :, 1 - x]
            return [make(part, r2.at[j], 2, across["yx"[order]])]
        if stage == 3:
            return [
                make(r2.at[j, lax.rem(z + k + 1, 4)], r3.at[j, k], 3 + k, along[k])
                for k in range(3)
            ]
        share = rows // 2
        return [make(f3.at[j, pl.ds(pl.multiple_of(other * share, 8), share)], r4.at[j], 6, sibling)]

    f32 = jnp.float32

    def add(plan, stage, order, i):
        pieces, rows, width, parts, src, out, r0, r1, r2, r3, f3, r4, send, recv = plan
        j, matrix, column = where(plan, order, i)
        if stage == 0:
            lanes = pl.ds(pl.multiple_of(mine + column, 128), width)

            @pl.loop(0, 16)
            def _(block):
                a, b, d = lax.div(block, 4), lax.rem(lax.div(block, 2), 2), lax.rem(block, 2)
                r0[j, a, b, d] = (
                    r0[j, a, b, d].astype(f32) + src[matrix, a, b, d, :, lanes].astype(f32)
                ).astype(jnp.bfloat16)
        elif stage == 1:
            @pl.loop(0, 8)
            def _(block):
                a, b = lax.div(block, 2), lax.rem(block, 2)
                own = r0[j, a, b, x] if order == 0 else r0[j, a, y, b]
                r1[j, a, b] = (r1[j, a, b].astype(f32) + own.astype(f32)).astype(jnp.bfloat16)
        elif stage == 2:
            @pl.loop(0, 4)
            def _(a):
                own = r1[j, a, y] if order == 0 else r1[j, a, x]
                r2[j, a] = (r2[j, a].astype(f32) + own.astype(f32)).astype(jnp.bfloat16)
        elif stage == 3:
            f3[j] = (r3[j, 0].astype(f32) + r3[j, 1].astype(f32)) + (
                r3[j, 2].astype(f32) + r2[j, z].astype(f32)
            )
        else:
            share = rows // 2
            lanes = pl.ds(pl.multiple_of(mine + column, 128), width)
            out[matrix, :, lanes] = f3[j, pl.ds(pl.multiple_of(core * share, 8), share)]
            lanes = pl.ds(pl.multiple_of(theirs + column, 128), width)
            out[matrix, :, lanes] = r4[j]

    def each(plan, body):
        @pl.loop(0, plan[0] // 2)
        def _(i):
            for order in range(2):
                body(order, i)

    def start(plan, stage):
        def body(order, i):
            for copy in copies(plan, stage, order, i):
                copy.start()

        each(plan, body)

    def step(plan, stage, order, i):
        for copy in copies(plan, stage, order, i):
            copy.wait_recv()
        add(plan, stage, order, i)
        if stage < 4:
            for copy in copies(plan, stage + 1, order, i):
                copy.start()

    def finish(plan, stage):
        def body(order, i):
            for copy in copies(plan, stage, order, i):
                copy.wait_send()

        each(plan, body)

    for plan in plans:
        start(plan, 0)
    for plan in plans:
        turns = plan[0] // 2

        @pl.loop(0, turns + 4)
        def _(turn):
            for stage in range(5):
                @pl.when((turn >= stage) & (turn < turns + stage))
                def _():
                    for order in range(2):
                        step(plan, stage, order, turn - stage)

            if plan is plans[0]:
                for stage in range(4):
                    @pl.when(turn == stage)
                    def _():
                        small_step(stage)

    for stage in range(5):
        for plan in plans:
            finish(plan, stage)
    if has_small:
        for stage in range(4):
            for copy in small_copies(stage):
                copy.wait_send()


def reduce_scatter(arrays, small, collective_id, split=1):
    groups, views, outs, scratch = [], [], [], []
    bf16, f32 = jnp.bfloat16, jnp.float32
    if small is not None:
        scratch += [
            pltpu.VMEM((7,) + small.shape, f32),
            pltpu.VMEM((3,) + small.shape, f32),
            pltpu.SemaphoreType.DMA((6,)),
            pltpu.SemaphoreType.DMA((6,)),
        ]
    for array in arrays:
        matrices, height, width_all = array.shape
        rows = height // 16
        parts = 3 if matrices == 2 else split
        pieces, width = matrices * parts, 384 // parts
        groups.append((pieces, rows, width, parts))
        views.append(array.reshape(matrices, 4, 2, 2, rows, width_all))
        outs.append(jax.ShapeDtypeStruct((matrices, rows // 2, width_all), f32))
        scratch += [
            pltpu.VMEM((pieces, 4, 2, 2, rows, width), bf16),
            pltpu.VMEM((pieces, 4, 2, rows, width), bf16),
            pltpu.VMEM((pieces, 4, rows, width), bf16),
            pltpu.VMEM((pieces, 3, rows, width), bf16),
            pltpu.VMEM((pieces, rows, width), f32),
            pltpu.VMEM((pieces, rows // 2, width), f32),
            pltpu.SemaphoreType.DMA((7, pieces)),
            pltpu.SemaphoreType.DMA((7, pieces)),
        ]
    if small is not None:
        views.append(small)
        outs.append(jax.ShapeDtypeStruct(small.shape, f32))
    vmem = pl.BlockSpec(memory_space=pltpu.VMEM)
    return pl.pallas_call(
        functools.partial(reduce_kernel, tuple(groups), small is not None),
        out_shape=tuple(outs),
        in_specs=[vmem] * len(views),
        out_specs=tuple([vmem] * len(outs)),
        scratch_shapes=scratch,
        compiler_params=pltpu.CompilerParams(
            collective_id=collective_id, has_side_effects=True, vmem_limit_bytes=60 << 20
        ),
    )(*views)


def gather_kernel(split, own, full, theirs, send, recv):
    z, y, x, core = place()
    other = 1 - core
    sibling = device(z, y, x, other)
    across = {"x": device(z, y, 1 - x, core), "y": device(z, 1 - y, x, core)}
    along = [device(lax.rem(z + k, 4), y, x, core) for k in (1, 2, 3)]
    greet([sibling, across["x"], across["y"]] + along)
    matrices, share, width = own.shape
    half = width // 2
    pieces, thin = matrices * split, half // split

    def spot(j):
        column = lax.rem(j, split) * thin
        return (
            lax.div(j, split),
            pl.ds(pl.multiple_of(core * half + column, 128), thin),
            pl.ds(pl.multiple_of(other * half + column, 128), thin),
        )

    def make(source, target, slot, j, partner):
        return pltpu.make_async_remote_copy(
            source, target, send.at[slot, j], recv.at[slot, j], device_id=partner, device_id_type=MESH
        )

    def copies(stage, order, i):
        j = i + order * (pieces // 2)
        m, mine, rest = spot(j)
        first = "yx"[order]
        if stage == 0:
            return [make(own.at[m, :, rest], theirs.at[j], 0, j, sibling)]
        if stage == 1:
            part = full.at[m, z, y, x, :, mine]
            return [make(part, part, 1 + k, j, along[k]) for k in range(3)]
        if stage == 2:
            part = full.at[m, :, y, x, :, mine]
            return [make(part, part, 4, j, across[first])]
        if stage == 3:
            part = full.at[m, :, :, x, :, mine] if order == 0 else full.at[m, :, y, :, :, mine]
            return [make(part, part, 5, j, across["xy"[order]])]
        part = full.at[m, :, :, :, :, mine]
        return [make(part, part, 6, j, sibling)]

    def each(body):
        @pl.loop(0, pieces // 2)
        def _(i):
            for order in range(2):
                body(order, i)

    def start(stage):
        def body(order, i):
            for copy in copies(stage, order, i):
                copy.start()

        each(body)

    def step(stage, order, i):
        for copy in copies(stage, order, i):
            copy.wait_recv()
        if stage == 0:
            j = i + order * (pieces // 2)
            m, mine, _ = spot(j)

            @pl.when(core == 0)
            def _():
                full[m, z, y, x, :, mine] = jnp.concatenate(
                    [own[m, :, mine], theirs[j]], axis=0
                ).astype(jnp.bfloat16)

            @pl.when(core == 1)
            def _():
                full[m, z, y, x, :, mine] = jnp.concatenate(
                    [theirs[j], own[m, :, mine]], axis=0
                ).astype(jnp.bfloat16)
        if stage < 4:
            for copy in copies(stage + 1, order, i):
                copy.start()

    def finish(stage):
        def body(order, i):
            for copy in copies(stage, order, i):
                copy.wait_send()

        each(body)

    start(0)
    turns = pieces // 2

    @pl.loop(0, turns + 4)
    def _(turn):
        for stage in range(5):
            @pl.when((turn >= stage) & (turn < turns + stage))
            def _():
                for order in range(2):
                    step(stage, order, turn - stage)

    for stage in range(5):
        finish(stage)


def gather_rows(own, collective_id, split=1):
    matrices, share, width = own.shape
    pieces = matrices * split
    vmem = pl.BlockSpec(memory_space=pltpu.VMEM)
    full = pl.pallas_call(
        functools.partial(gather_kernel, split),
        out_shape=jax.ShapeDtypeStruct((matrices, 4, 2, 2, 2 * share, width), jnp.bfloat16),
        in_specs=[vmem],
        out_specs=vmem,
        scratch_shapes=[
            pltpu.VMEM((pieces, share, width // 2 // split), jnp.float32),
            pltpu.SemaphoreType.DMA((7, pieces)),
            pltpu.SemaphoreType.DMA((7, pieces)),
        ],
        compiler_params=pltpu.CompilerParams(
            collective_id=collective_id, has_side_effects=True, vmem_limit_bytes=32 << 20
        ),
    )(own)
    return full.reshape(matrices, 32 * share, width)


def gram_kernel(gram, out, other_sum, half_a, half_b, final, send, recv):
    z, y, x, core = place()
    sibling = device(z, y, x, 1 - core)
    x_side, y_side = device(z, y, 1 - x, core), device(z, 1 - y, x, core)
    greet([sibling, x_side, y_side])
    side = gram.shape[0] // 2
    rows = pl.ds(pl.multiple_of(core * side, 8), side)
    rest = pl.ds(pl.multiple_of((1 - core) * side, 8), side)

    def send_to(source, target, slot, partner):
        return pltpu.make_async_remote_copy(
            source, target, send.at[slot], recv.at[slot], device_id=partner, device_id_type=MESH
        )

    first = send_to(gram.at[rest], other_sum.at[rest], 0, sibling)
    second = send_to(gram.at[rows], other_sum.at[rows], 1, sibling)
    first.start()
    second.start()
    mine = send_to(gram.at[rows], other_sum.at[rows], 0, sibling)
    mine.wait_recv()
    out[rows] = gram[rows] + other_sum[rows]
    theirs = send_to(gram.at[rest], other_sum.at[rest], 1, sibling)
    theirs.wait_recv()

    @pl.when(z < 2)
    def _():
        out[rest] = gram[rest] + other_sum[rest]

    @pl.when(z >= 2)
    def _():
        def pair(one, two):
            step = send_to(out.at[rows], half_a, 2, one)
            step.start()
            step.wait_recv()
            step.wait_send()
            half_b[...] = out[rows] + half_a[...]
            step = send_to(half_b, final, 3, two)
            step.start()
            step.wait_recv()
            out[rows] = half_b[...] + final[...]
            step.wait_send()

        @pl.when(core == 0)
        def _():
            pair(x_side, y_side)

        @pl.when(core == 1)
        def _():
            pair(y_side, x_side)

        last = send_to(out.at[rows], out.at[rows], 4, sibling)
        last.start()
        arrive = send_to(out.at[rest], out.at[rest], 4, sibling)
        arrive.wait_recv()
        last.wait_send()

    first.wait_send()
    second.wait_send()


def gram_sum(gram, collective_id):
    f32 = jnp.float32
    side = gram.shape[0] // 2
    vmem = pl.BlockSpec(memory_space=pltpu.VMEM)
    return pl.pallas_call(
        gram_kernel,
        out_shape=jax.ShapeDtypeStruct(gram.shape, f32),
        in_specs=[vmem],
        out_specs=vmem,
        scratch_shapes=[
            pltpu.VMEM(gram.shape, f32),
            pltpu.VMEM((side, gram.shape[1]), f32),
            pltpu.VMEM((side, gram.shape[1]), f32),
            pltpu.VMEM((side, gram.shape[1]), f32),
            pltpu.SemaphoreType.DMA((5,)),
            pltpu.SemaphoreType.DMA((5,)),
        ],
        compiler_params=pltpu.CompilerParams(
            collective_id=collective_id, has_side_effects=True, vmem_limit_bytes=32 << 20
        ),
    )(gram)


def matmul3(left, right):
    return jnp.matmul(left, right, precision=lax.Precision.HIGH)


def to_owner_rows(square_state, tall_state, count):
    rows = square_state.shape[1]
    group = count // 16
    if rows % group == 0:
        piece = rows // group
        pieces = jnp.concatenate(
            [
                square_state.reshape(8 * group, piece, D),
                tall_state.reshape(8 * group, piece, D),
            ],
            axis=0,
        ).astype(jnp.bfloat16)
        return lax.all_to_all(pieces, AXES, 0, 0, tiled=True).reshape(count * piece, D)
    square_all = lax.all_gather(square_state.astype(jnp.bfloat16), AXES, axis=1, tiled=True)
    tall_all = lax.all_gather(tall_state.astype(jnp.bfloat16), AXES, axis=1, tiled=True)
    joined = jnp.concatenate([square_all.reshape(-1, D), tall_all.reshape(-1, D)], axis=0)
    own = joined.shape[0] // count
    return lax.dynamic_slice_in_dim(joined, lax.axis_index(AXES) * own, own, axis=0)


def from_owner_rows(rows_out, count, square_rows, tall_rows):
    group = count // 16
    rows_out = rows_out.astype(jnp.bfloat16)
    if square_rows % group == 0:
        piece = square_rows // group
        back = lax.all_to_all(rows_out.reshape(count, piece, D), AXES, 0, 0, tiled=True)
        return (
            back[: 8 * group].reshape(8, square_rows, D),
            back[8 * group :].reshape(2, tall_rows, D),
        )
    joined = lax.all_gather(rows_out, AXES, axis=0, tiled=True)
    square_all = joined[: 8 * square_rows * count].reshape(8, square_rows * count, D)
    tall_all = joined[8 * square_rows * count :].reshape(2, tall_rows * count, D)
    index = lax.axis_index(AXES)
    return (
        lax.dynamic_slice_in_dim(square_all, index * square_rows, square_rows, axis=1),
        lax.dynamic_slice_in_dim(tall_all, index * tall_rows, tall_rows, axis=1),
    )


def orthogonal_rows(rows_in, kernels):
    rows_in = rows_in.astype(jnp.float32)
    gram = jnp.einsum("rd,re->de", rows_in, rows_in, precision=lax.Precision.HIGHEST)
    if kernels:
        gram = gram_sum(gram, 2)
    else:
        gram = lax.psum(gram, "row")
        is_tall = lax.axis_index("tall") >= 2
        gram = jnp.where(is_tall, lax.psum(jnp.where(is_tall, gram, 0.0), "square"), gram)
    eye = (jnp.arange(D)[:, None] == jnp.arange(D)[None, :]).astype(jnp.float32)
    scale = 1.0 / (jnp.sqrt(jnp.sum(gram * eye)) + FLOOR_EPSILON)
    gram = gram * (scale * scale)
    current = rows_in * scale

    for sweep in range(ITERS):
        poly = FIRST_TERM * eye + SECOND_TERM * gram + THIRD_TERM * matmul3(gram, gram)
        current = matmul3(current, poly)
        if sweep < ITERS - 1:
            gram = matmul3(matmul3(gram, poly), poly)
    return current


def local(
    inputs,
    memory,
    cotangent,
    lengths,
    memory_len,
    square_master,
    tall_master,
    square_momentum,
    tall_momentum,
    vectors,
    feed_vectors,
    head_scale,
    relative,
):
    count = lax.axis_size(AXES)
    kernels = count == 32
    index = lax.axis_index(AXES)
    if kernels:
        square_copy = gather_rows(square_master, 3, 3)
    else:
        square_copy = lax.all_gather(
            square_master.astype(jnp.bfloat16), AXES, axis=1, tiled=True
        )
    tall_copy = lax.all_gather(tall_master.astype(jnp.bfloat16), AXES, axis=1, tiled=True)
    width = inputs.shape[2]
    vec, feed = vectors.astype(F32), feed_vectors.astype(F32)
    head_row = jnp.repeat(head_scale.astype(F32), width // head_scale.shape[0])[None]
    at = jnp.arange(inputs.shape[1])
    distance = at[:, None] - at[None, :]
    table = (jnp.maximum(distance, 0)[:, :, None] == at[None, None, :]).astype(BF16)
    bias = jnp.einsum("hd,qkd->hqk", relative, table, preferred_element_type=F32)
    bias = jnp.where(distance >= 0, bias, NEGATIVE_LARGE).reshape(6, 256, 128)
    flat_in, flat_memory = inputs.reshape(-1, width), memory.reshape(-1, width)
    left, q, k, v, p, o, h1, cq, ck, cv, pc, co, h2 = attention_forward(
        flat_in, flat_memory, memory_len, square_copy, vec, head_row, bias
    )
    output, dh2, narrow, wide, late_slope, feed_slope = feed_both(
        h2, cotangent.reshape(-1, width), lengths, tall_copy, vec, feed
    )

    tall_slope = jnp.einsum("btf,btd->bfd", wide, narrow, preferred_element_type=F32).astype(BF16)
    tall_slope, dh2 = lax.optimization_barrier((tall_slope, dh2))
    tall_sum = lax.psum_scatter(tall_slope, AXES, scatter_dimension=1, tiled=True).astype(F32)
    input_slope, memory_slope, right, far, early_slope, bias_slope = attention_backward(
        flat_in, dh2, square_copy, vec, head_row, (q, k, v, p, o, h1, cq, ck, cv, pc, co)
    )
    square_slope = square_slopes(left, right, flat_memory, far)
    vector_slope = jnp.concatenate([early_slope[:14], late_slope], axis=0)
    scale_slope = jnp.sum(early_slope[17].reshape(head_scale.shape[0], -1), axis=1)
    bias_slope = jnp.roll(bias_slope, 1, axis=1)
    small = [
        jnp.sum(lengths).astype(jnp.float32).reshape(1),
        scale_slope.reshape(-1),
        bias_slope.reshape(-1),
        vector_slope.reshape(-1),
        feed_slope.reshape(-1),
    ]
    sizes = [piece.shape[0] for piece in small]
    starts = [sum(sizes[:i]) for i in range(len(sizes) + 1)]
    if kernels:
        lines = -(-starts[-1] // 1024) * 8
        small.append(jnp.zeros((lines * 128 - starts[-1],), jnp.float32))
        square_sum, summed = reduce_scatter(
            [square_slope], jnp.concatenate(small).reshape(lines, 128), 1
        )
        summed = summed.reshape(-1)
    else:
        square_sum = lax.psum_scatter(
            square_slope, AXES, scatter_dimension=1, tiled=True
        ).astype(jnp.float32)
        summed = lax.psum(jnp.concatenate(small), AXES)
    total, scale_sum, bias_sum, vector_sum, feed_sum = (
        summed[starts[i] : starts[i + 1]] for i in range(len(sizes))
    )
    factor = inputs.shape[0] * count / total[0]
    bias_sum = bias_sum.reshape(bias_slope.shape)
    width = vector_slope.shape[1] // count
    vector_sum = lax.dynamic_slice_in_dim(
        vector_sum.reshape(vector_slope.shape), index * width, width, axis=1
    )
    width = feed_slope.shape[1] // count
    feed_sum = lax.dynamic_slice_in_dim(
        feed_sum.reshape(feed_slope.shape), index * width, width, axis=1
    )
    square_state = MOMENTUM_DECAY * square_momentum + factor * square_sum
    tall_state = MOMENTUM_DECAY * tall_momentum + factor * tall_sum
    rows_out = orthogonal_rows(to_owner_rows(square_state, tall_state, count), kernels)
    square, tall = from_owner_rows(
        rows_out, count, square_state.shape[1], tall_state.shape[1]
    )
    square, tall = square.astype(jnp.float32), tall.astype(jnp.float32)
    square_weight = square_master * (1.0 - LEARN_RATE * WEIGHT_DECAY) - LEARN_RATE * square
    tall_weight = (
        tall_master * (1.0 - LEARN_RATE * WEIGHT_DECAY)
        - LEARN_RATE * max(1.0, FF / D) ** 0.5 * tall
    )
    return (
        output.reshape(inputs.shape),
        input_slope.reshape(inputs.shape),
        memory_slope.reshape(memory.shape),
        square_state,
        tall_state,
        square_weight,
        tall_weight,
        factor * vector_sum,
        factor * feed_sum,
        factor * scale_sum,
        factor * bias_sum,
    )


def solution(mesh):
    count = mesh.devices.size
    grouped = Mesh(mesh.devices.reshape(4, 4, count // 16), AXES)
    placed = (
        P(AXES, None, None),
        P(AXES, None, None),
        P(AXES, None, None),
        P(AXES),
        P(AXES),
        P(None, AXES, None),
        P(None, AXES, None),
        P(None, AXES, None),
        P(None, AXES, None),
        P(),
        P(),
        P(),
        P(),
    )
    return jax.shard_map(
        local,
        mesh=grouped,
        in_specs=placed,
        out_specs=(
            P(AXES, None, None),
            P(AXES, None, None),
            P(AXES, None, None),
            P(None, AXES, None),
            P(None, AXES, None),
            P(None, AXES, None),
            P(None, AXES, None),
            P(None, AXES),
            P(None, AXES),
            P(),
            P(),
        ),
        check_vma=False,
    )
```

```python
import functools

import jax
import jax.numpy as jnp
from jax import lax
from jax.experimental import pallas as pl
from jax.experimental.pallas import tpu as pltpu
from jax.sharding import Mesh, PartitionSpec as P

D = 768
FF = 3072
ITERS = 5


NORM_EPSILON = 1e-05
FLOOR_EPSILON = 1e-07
FIRST_TERM = 3.4445
SECOND_TERM = -4.775
THIRD_TERM = 2.0315
MOMENTUM_DECAY = 0.95
LEARN_RATE = 0.8
WEIGHT_DECAY = 0.01
NEGATIVE_LARGE = -1e30


F32, BF16 = jnp.float32, jnp.bfloat16
TOKENS = 256
SLOTS = 512
LANES = 128


def times(left, right):
    return jnp.dot(left, right, preferred_element_type=F32)


def times_back(left, right):
    return lax.dot_general(left, right, (((1,), (1,)), ((), ())), preferred_element_type=F32)


def times_down(left, right):
    return lax.dot_general(left, right, (((0,), (0,)), ((), ())), preferred_element_type=F32)


def standard(values):
    center = values - jnp.mean(values, axis=-1, keepdims=True)
    scale = lax.rsqrt(jnp.mean(center * center, axis=-1, keepdims=True) + NORM_EPSILON)
    return center * scale, scale


def norm(values, gain, shift):
    return standard(values)[0] * gain + shift


def norm_back(values, slope, gain):
    hat, scale = standard(values)
    inner = slope * gain
    back = scale * (
        inner
        - jnp.mean(inner, axis=-1, keepdims=True)
        - hat * jnp.mean(inner * hat, axis=-1, keepdims=True)
    )
    return back, down(slope * hat), down(slope)


def down(values):
    return jnp.sum(values, axis=0, keepdims=True)


def head_masks():
    lane = lax.broadcasted_iota(jnp.int32, (1, LANES), 1)
    even = jnp.where(lane < LANES // 2, 1.0, 0.0)
    return even.astype(BF16), (1.0 - even).astype(BF16)


def stacked(pair, masks):
    return jnp.concatenate([pair * masks[0], pair * masks[1]], axis=0)


def side_by_side(rows):
    half = rows.shape[0] // 2
    return jnp.concatenate([rows[:half], rows[half:]], axis=1)


def soften(scores):
    weights = jnp.exp(scores - jnp.max(scores, axis=-1, keepdims=True))
    return (weights * (1.0 / jnp.sum(weights, axis=-1, keepdims=True))).astype(BF16)


def soften_back(weights, slope):
    weights = weights.astype(F32)
    product = weights * slope
    return (product - weights * jnp.sum(product, axis=-1, keepdims=True)).astype(BF16)


def attention_kernel(
    memory_len, x_in, memory, w, vec, hs, mirrored,
    left, q, k, v, p, o, h1, cq, ck, cv, pc, co, h2,
    bias,
):
    step = pl.program_id(0)
    masks = head_masks()

    @pl.when(step == 0)
    def _():
        row = lax.broadcasted_iota(jnp.int32, (128, 128), 0)
        column = lax.broadcasted_iota(jnp.int32, (128, 128), 1)
        for head in range(12):
            line = jnp.broadcast_to(mirrored[head : head + 1], (128, 128))
            line = pltpu.roll(line, 0, 1, stride=1, stride_axis=0)
            bias[head // 2, (head % 2) * 128 : (head % 2) * 128 + 128] = jnp.where(
                row >= column, line, NEGATIVE_LARGE
            )

    x = x_in[...].astype(F32)
    left[0] = norm(x, vec[0:1], vec[1:2]).astype(BF16)
    q[...] = ((times(left[0], w[0]) + vec[2:3]) * 0.125).astype(BF16)
    k[...] = times(left[0], w[1]).astype(BF16)
    v[...] = (times(left[0], w[2]) + vec[3:4]).astype(BF16)
    items = TOKENS // 128

    @pl.loop(0, 6, unroll=True)
    def _(pair):
        lanes = pl.ds(pl.multiple_of(pair * LANES, LANES), LANES)
        for item in range(items):
            rows = slice(item * 128, item * 128 + 128)
            scores = times_back(stacked(q[rows, lanes], masks), k[rows, lanes]) + bias[pair]
            weights = soften(scores)
            p[item, pair] = weights
            o[rows, lanes] = times(side_by_side(weights), stacked(v[rows, lanes], masks))

    left[1] = norm(o[...] * hs[...], vec[5:6], vec[6:7]).astype(BF16)
    h1[...] = x + (times(left[1], w[3]) + vec[4:5])
    left[2] = norm(h1[...], vec[7:8], vec[8:9]).astype(BF16)
    cq[...] = ((times(left[2], w[4]) + vec[9:10]) * 0.125).astype(BF16)
    ck[...] = times(memory[...], w[5]).astype(BF16)
    cv[...] = (times(memory[...], w[6]) + vec[10:11]).astype(BF16)
    slots = SLOTS // items
    column = lax.broadcasted_iota(jnp.int32, (1, slots), 1)

    @pl.loop(0, 6, unroll=True)
    def _(pair):
        lanes = pl.ds(pl.multiple_of(pair * LANES, LANES), LANES)
        for item in range(items):
            rows = slice(item * 128, item * 128 + 128)
            keys = slice(item * slots, item * slots + slots)
            limit = memory_len[step * items + item]
            scores = times_back(stacked(cq[rows, lanes], masks), ck[keys, lanes])
            weights = soften(jnp.where(column < limit, scores, NEGATIVE_LARGE))
            pc[item, pair] = weights
            co[rows, lanes] = times(side_by_side(weights), stacked(cv[keys, lanes], masks))

    left[3] = norm(co[...], vec[12:13], vec[13:14]).astype(BF16)
    h2[...] = h1[...] + (times(left[3], w[7]) + vec[11:12])


def whole(shape):
    return pl.BlockSpec(shape, lambda *_: (0,) * len(shape), pipeline_mode=pl.Buffered(1))


def by_rows(rows, width):
    return pl.BlockSpec((rows, width), lambda i: (i, 0))


def by_blocks(blocks, rows, width):
    return pl.BlockSpec((blocks, rows, width), lambda i: (0, i, 0))


def by_items(items, *rest):
    return pl.BlockSpec((items,) + rest, lambda i: (i,) + (0,) * len(rest))


def attention_forward(inputs, memory, memory_len, square, vectors, head_row, bias):
    tokens, width = inputs.shape
    slots = memory.shape[0]
    steps = tokens // TOKENS
    items = TOKENS // 128
    shapes = [
        (BF16, "l"), (BF16, "t"), (BF16, "t"), (BF16, "t"), (BF16, "p"), (F32, "t"), (F32, "t"),
        (BF16, "t"), (BF16, "m"), (BF16, "m"), (BF16, "c"), (F32, "t"), (F32, "t"),
    ]
    full = {"l": (4, tokens, width), "t": (tokens, width), "m": (slots, width), "p": (steps * items, 6, 256, 128), "c": (steps * items, 6, 256, SLOTS // items)}
    spec = {
        "l": by_blocks(4, TOKENS, width),
        "t": by_rows(TOKENS, width), "m": by_rows(SLOTS, width),
        "p": by_items(items, 6, 256, 128), "c": by_items(items, 6, 256, SLOTS // items),
    }
    return pl.pallas_call(
        attention_kernel,
        grid=(steps,),
        out_shape=tuple(jax.ShapeDtypeStruct(full[kind], kept) for kept, kind in shapes),
        in_specs=[
            pl.BlockSpec(memory_space=pltpu.SMEM),
            spec["t"], spec["m"], whole(square.shape), whole(vectors.shape), whole(head_row.shape), whole(bias.shape),
        ],
        out_specs=tuple(spec[kind] for _, kind in shapes),
        scratch_shapes=[pltpu.VMEM((6, 256, 128), F32)],
        compiler_params=pltpu.CompilerParams(vmem_limit_bytes=60 << 20),
        cost_estimate=pl.CostEstimate(flops=14_000_000_000, bytes_accessed=60_000_000, transcendentals=5_000_000),
    )(memory_len, inputs, memory, square, vectors, head_row, bias)


ROOT_HALF = 0.7071067811865476
INVERSE_ROOT = 0.3989422804014327
CHUNK = 1024


def feed_kernel(
    lengths, h2_in, cot, tall, vec, feed,
    out, dh2, narrow, wide, dvec, dfeed,
    u, g, dr, total,
):
    step = pl.program_id(0)
    items = TOKENS // 128
    width = tall.shape[1]
    chunks = width // CHUNK

    @pl.when(step == 0)
    def _():
        dvec[...] = jnp.zeros_like(dvec)
        dfeed[...] = jnp.zeros_like(dfeed)

    h2 = h2_in[...]
    narrow[0] = norm(h2, vec[14:15], vec[15:16]).astype(BF16)

    def at(i):
        return pl.ds(pl.multiple_of(i * CHUNK, CHUNK), CHUNK)

    def first(i, total):
        some = at(i)
        inner = times_back(narrow[0], tall[0, some]) + feed[0:1, some]
        bell = 0.5 + 0.5 * lax.erf(inner * ROOT_HALF)
        active = inner * bell
        g[:, some] = active
        u[:, some] = bell + inner * (jnp.exp(-0.5 * inner * inner) * INVERSE_ROOT)
        return total + jnp.sum(active, axis=-1, keepdims=True)

    zero = jnp.zeros((TOKENS, 1), F32)
    mean = lax.fori_loop(0, chunks, first, zero, unroll=True) * (1.0 / width)

    def second(i, total):
        center = g[:, at(i)] - mean
        return total + jnp.sum(center * center, axis=-1, keepdims=True)

    spread = lax.fori_loop(0, chunks, second, zero, unroll=True) * (1.0 / width)
    scale = lax.rsqrt(spread + NORM_EPSILON)
    row = lax.broadcasted_iota(jnp.int32, (128, 1), 0)
    valid = jnp.concatenate(
        [jnp.where(row < lengths[step * items + item], 1.0, 0.0) for item in range(items)], axis=0
    )
    dy32 = cot[...].astype(F32) * valid
    narrow[1] = dy32.astype(BF16)
    total[...] = h2 + vec[16:17]

    def third(i, sums):
        some = at(i)
        hat = (g[:, some] - mean) * scale
        g[:, some] = hat
        gain = feed[1:2, some]
        active = (hat * gain + feed[2:3, some]).astype(BF16)
        wide[1, :, some] = active
        total[...] += times(active, tall[1, some])
        slope = times_back(narrow[1], tall[1, some])
        dfeed[1:2, some] += down(slope * hat)
        dfeed[2:3, some] += down(slope)
        inner = slope * gain
        dr[:, some] = inner
        return (
            sums[0] + jnp.sum(inner, axis=-1, keepdims=True),
            sums[1] + jnp.sum(inner * hat, axis=-1, keepdims=True),
        )

    one, two = lax.fori_loop(0, chunks, third, (zero, zero), unroll=True)
    out[...] = total[...].astype(BF16)
    one, two = one * (1.0 / width), two * (1.0 / width)
    dh2[...] = jnp.zeros_like(dh2)

    def fourth(i, carry):
        some = at(i)
        back = scale * (dr[:, some] - one - g[:, some] * two)
        slope = (back * u[:, some]).astype(BF16)
        wide[0, :, some] = slope
        dfeed[0:1, some] += down(slope.astype(F32))
        dh2[...] += times(slope, tall[0, some])
        return carry

    lax.fori_loop(0, chunks, fourth, 0, unroll=True)
    back, gain_sum, shift_sum = norm_back(h2, dh2[...], vec[14:15])
    dvec[0:1] += gain_sum
    dvec[1:2] += shift_sum
    dvec[2:3] += down(dy32)
    dh2[...] = dy32 + back


def feed_both(hidden, cotangent, lengths, tall, vectors, feed_vectors):
    tokens, width = hidden.shape
    wide = tall.shape[1]
    steps = tokens // TOKENS
    some = by_rows(TOKENS, width)
    return pl.pallas_call(
        feed_kernel,
        grid=(steps,),
        out_shape=(
            jax.ShapeDtypeStruct((tokens, width), BF16),
            jax.ShapeDtypeStruct((tokens, width), F32),
            jax.ShapeDtypeStruct((2, tokens, width), BF16),
            jax.ShapeDtypeStruct((2, tokens, wide), BF16),
            jax.ShapeDtypeStruct((3, width), F32),
            jax.ShapeDtypeStruct((3, wide), F32),
        ),
        in_specs=[
            pl.BlockSpec(memory_space=pltpu.SMEM),
            some, some, whole(tall.shape), whole(vectors.shape), whole(feed_vectors.shape),
        ],
        out_specs=(
            some, some, by_blocks(2, TOKENS, width), by_blocks(2, TOKENS, wide),
            pl.BlockSpec((3, width), lambda i: (0, 0)),
            pl.BlockSpec((3, wide), lambda i: (0, 0)),
        ),
        scratch_shapes=[pltpu.VMEM((TOKENS, wide), F32)] * 3 + [pltpu.VMEM((TOKENS, width), F32)],
        compiler_params=pltpu.CompilerParams(vmem_limit_bytes=60 << 20),
        cost_estimate=pl.CostEstimate(flops=20_000_000_000, bytes_accessed=40_000_000, transcendentals=7_000_000),
    )(lengths, hidden, cotangent, tall, vectors, feed_vectors)


def attention_back_kernel(
    x_in, dh2, w, vec, hs,
    q, k, v, p, o, h1, cq, ck, cv, pc, co,
    dx, dmem, right, far, dvec, drel,
    do, dh1, dbias,
):
    step = pl.program_id(0)
    masks = head_masks()
    items = TOKENS // 128
    slots = SLOTS // items

    @pl.when(step == 0)
    def _():
        dvec[...] = jnp.zeros_like(dvec)
        dbias[...] = jnp.zeros_like(dbias)

    def note(row, value):
        dvec[row : row + 1] += value

    right[5] = dh2[...].astype(BF16)
    note(11, down(right[5].astype(F32)))
    back, gain_sum, shift_sum = norm_back(co[...], times_back(right[5], w[7]), vec[12:13])
    note(12, gain_sum)
    note(13, shift_sum)
    do[...] = back.astype(BF16)

    def through(pair, item, keys, query, key, value, weights, dquery, dkey, dvalue, with_bias):
        lanes = pl.ds(pl.multiple_of(pair * LANES, LANES), LANES)
        rows = slice(item * 128, item * 128 + 128)
        kept = weights[item, pair]
        grad = stacked(do[rows, lanes], masks)
        dvalue[keys, lanes] = times_down(kept, grad).astype(BF16)
        slope = soften_back(kept, times_back(grad, value[keys, lanes]))
        dquery[rows, lanes] = (
            times(side_by_side(slope), stacked(key[keys, lanes], masks)).astype(BF16) * 0.125
        ).astype(BF16)
        dkey[keys, lanes] = times_down(slope, stacked(query[rows, lanes], masks)).astype(BF16)
        if with_bias:
            dbias[pair] += slope.astype(F32)

    @pl.loop(0, 6, unroll=True)
    def _(pair):
        for item in range(items):
            keys = slice(item * slots, item * slots + slots)
            through(pair, item, keys, cq, ck, cv, pc, right.at[4], far.at[0], far.at[1], False)

    note(9, down(right[4].astype(F32)))
    note(10, down(far[1].astype(F32)))
    dmem[...] = (times_back(far[0], w[5]) + times_back(far[1], w[6])).astype(BF16)
    back, gain_sum, shift_sum = norm_back(h1[...], times_back(right[4], w[4]), vec[7:8])
    note(7, gain_sum)
    note(8, shift_sum)
    dh1[...] = dh2[...] + back
    right[3] = dh1[...].astype(BF16)
    note(4, down(right[3].astype(F32)))
    back, gain_sum, shift_sum = norm_back(o[...] * hs[...], times_back(right[3], w[3]), vec[5:6])
    note(5, gain_sum)
    note(6, shift_sum)
    note(17, down(back * o[...]))
    do[...] = (back * hs[...]).astype(BF16)

    @pl.loop(0, 6, unroll=True)
    def _(pair):
        for item in range(items):
            rows = slice(item * 128, item * 128 + 128)
            through(pair, item, rows, q, k, v, p, right.at[0], right.at[1], right.at[2], True)

    note(2, down(right[0].astype(F32)))
    note(3, down(right[2].astype(F32)))
    slope = times_back(right[0], w[0]) + times_back(right[1], w[1]) + times_back(right[2], w[2])
    back, gain_sum, shift_sum = norm_back(x_in[...].astype(F32), slope, vec[0:1])
    note(0, gain_sum)
    note(1, shift_sum)
    dx[...] = (dh1[...] + back).astype(BF16)

    @pl.when(step == pl.num_programs(0) - 1)
    def _():
        row = lax.broadcasted_iota(jnp.int32, (128, 128), 0)
        column = lax.broadcasted_iota(jnp.int32, (128, 128), 1)
        mirror = jnp.where(row + column == 127, 1.0, 0.0).astype(BF16)
        for head in range(12):
            part = dbias[head // 2, (head % 2) * 128 : (head % 2) * 128 + 128]
            high = part.astype(BF16)
            rest = part - high.astype(F32)
            middle = rest.astype(BF16)
            low = (rest - middle.astype(F32)).astype(BF16)
            flipped = times(high, mirror) + times(middle, mirror) + times(low, mirror)
            drel[head : head + 1] = down(pltpu.roll(flipped, 0, 1, stride=1, stride_axis=0))


def attention_backward(inputs, dh2, square, vectors, head_row, kept):
    tokens, width = inputs.shape
    q, k, v, p, o, h1, cq, ck, cv, pc, co = kept
    steps = tokens // TOKENS
    items = TOKENS // 128
    slots = ck.shape[0]
    t, m = by_rows(TOKENS, width), by_rows(SLOTS, width)
    ps, cs = by_items(items, 6, 256, 128), by_items(items, 6, 256, SLOTS // items)
    token = jax.ShapeDtypeStruct((tokens, width), BF16)
    slot = jax.ShapeDtypeStruct((slots, width), BF16)
    return pl.pallas_call(
        attention_back_kernel,
        grid=(steps,),
        out_shape=(
            token, slot,
            jax.ShapeDtypeStruct((6, tokens, width), BF16),
            jax.ShapeDtypeStruct((2, slots, width), BF16),
            jax.ShapeDtypeStruct((18, width), F32),
            jax.ShapeDtypeStruct((12, 128), F32),
        ),
        in_specs=[
            t, t, whole(square.shape), whole(vectors.shape), whole(head_row.shape),
            t, t, t, ps, t, t, t, m, m, cs, t,
        ],
        out_specs=(
            t, m, by_blocks(6, TOKENS, width), by_blocks(2, SLOTS, width),
            pl.BlockSpec((18, width), lambda i: (0, 0)),
            pl.BlockSpec((12, 128), lambda i: (0, 0)),
        ),
        scratch_shapes=[
            pltpu.VMEM((TOKENS, width), BF16),
            pltpu.VMEM((TOKENS, width), F32),
            pltpu.VMEM((6, 256, 128), F32),
        ],
        compiler_params=pltpu.CompilerParams(vmem_limit_bytes=60 << 20),
        cost_estimate=pl.CostEstimate(flops=16_000_000_000, bytes_accessed=60_000_000, transcendentals=0),
    )(inputs, dh2, square, vectors, head_row, q, k, v, p, o, h1, cq, ck, cv, pc, co)


def slope_kernel(left, right, memory, far, out):
    step = pl.program_id(0)
    width = out.shape[1]

    def product(from_left, from_right):
        @pl.loop(0, width // 256)
        def _(tile):
            some = pl.ds(pl.multiple_of(tile * 256, 256), 256)
            out[0, some] = times_down(from_left[:, some], from_right[...]).astype(BF16)

    @pl.when(step < 6)
    def _():
        product(left.at[0], right.at[0])

    @pl.when(step >= 6)
    def _():
        product(memory, far.at[0])


def square_slopes(left, right, memory, far):
    _, tokens, width = left.shape
    slots = memory.shape[0]
    return pl.pallas_call(
        slope_kernel,
        grid=(8,),
        out_shape=jax.ShapeDtypeStruct((8, width, width), BF16),
        in_specs=[
            pl.BlockSpec((1, tokens, width), lambda g: (jnp.clip(g - 2, 0, 3), 0, 0)),
            pl.BlockSpec((1, tokens, width), lambda g: (jnp.minimum(g, 5), 0, 0)),
            whole(memory.shape),
            pl.BlockSpec((1, slots, width), lambda g: (jnp.maximum(g - 6, 0), 0, 0)),
        ],
        out_specs=pl.BlockSpec(
            (1, width, width),
            lambda g: (jnp.where(g < 5, g, jnp.where(g == 5, 7, g - 1)), 0, 0),
        ),
        compiler_params=pltpu.CompilerParams(vmem_limit_bytes=60 << 20),
        cost_estimate=pl.CostEstimate(flops=12_000_000_000, bytes_accessed=30_000_000, transcendentals=0),
    )(left, right, memory, far)


AXES = ("tall", "square", "row")
MESH = pl.DeviceIdType.MESH


def place():
    z, plane, core = lax.axis_index("tall"), lax.axis_index("square"), lax.axis_index("row")
    return z, lax.div(plane, 2), lax.rem(plane, 2), core


def device(z, y, x, core):
    return (z, y * 2 + x, core)


def greet(partners):
    barrier = pltpu.get_barrier_semaphore()
    for partner in partners:
        pl.semaphore_signal(barrier, inc=1, device_id=partner, device_id_type=MESH)
    pl.semaphore_wait(barrier, len(partners))


def reduce_kernel(groups, has_small, *refs):
    n = len(groups)
    ins, refs = refs[:n], refs[n:]
    if has_small:
        small, refs = refs[0], refs[1:]
    outs, refs = refs[:n], refs[n:]
    if has_small:
        small_out, refs = refs[0], refs[1:]
    z, y, x, core = place()
    other = 1 - core
    sibling = device(z, y, x, other)
    across = {"x": device(z, y, 1 - x, core), "y": device(z, 1 - y, x, core)}
    along = [device(lax.rem(z + k, 4), y, x, core) for k in (1, 2, 3)]
    greet([sibling, across["x"], across["y"]] + along)
    mine = core * 384
    theirs = other * 384

    if has_small:
        held, total, refs = refs[0], refs[1], refs[2:]
        small_send, small_recv, refs = refs[0], refs[1], refs[2:]

        def small_copies(stage):
            source = small if stage == 0 else total.at[stage - 1]
            if stage < 3:
                partner = (sibling, across["x"], across["y"])[stage]
                return [
                    pltpu.make_async_remote_copy(
                        source, held.at[stage], small_send.at[stage], small_recv.at[stage],
                        device_id=partner, device_id_type=MESH,
                    )
                ]
            return [
                pltpu.make_async_remote_copy(
                    source, held.at[3 + z], small_send.at[3 + k], small_recv.at[3 + k],
                    device_id=along[k], device_id_type=MESH,
                )
                for k in range(3)
            ]

        for copy in small_copies(0):
            copy.start()

        def small_step(stage):
            for copy in small_copies(stage):
                copy.wait_recv()
            if stage < 3:
                own = small if stage == 0 else total.at[stage - 1]
                total[stage] = own[...] + held[stage]
                if stage == 2:
                    held[3 + z] = total[2]
                for copy in small_copies(stage + 1):
                    copy.start()
            else:
                small_out[...] = ((held[3] + held[4]) + held[5]) + held[6]
    else:
        def small_step(stage):
            pass

    plans = []
    for g, (pieces, rows, width, parts) in enumerate(groups):
        r0, r1, r2, r3, f3, r4, send, recv = refs[8 * g : 8 * g + 8]
        plans.append((pieces, rows, width, parts, ins[g], outs[g], r0, r1, r2, r3, f3, r4, send, recv))

    def where(plan, order, i):
        pieces, parts, width = plan[0], plan[3], plan[2]
        j = i + order * (pieces // 2)
        return j, lax.div(j, parts), pl.multiple_of(lax.rem(j, parts) * width, 128)

    def copies(plan, stage, order, i):
        pieces, rows, width, parts, src, out, r0, r1, r2, r3, f3, r4, send, recv = plan
        j, matrix, column = where(plan, order, i)
        first = "xy"[order]

        def make(source, target, slot, partner):
            return pltpu.make_async_remote_copy(
                source, target, send.at[slot, j], recv.at[slot, j],
                device_id=partner, device_id_type=MESH,
            )

        if stage == 0:
            lanes = pl.ds(pl.multiple_of(theirs + column, 128), width)
            return [make(src.at[matrix, :, :, :, :, lanes], r0.at[j], 0, sibling)]
        if stage == 1:
            part = r0.at[j, :, :, 1 - x] if order == 0 else r0.at[j, :, 1 - y]
            return [make(part, r1.at[j], 1, across[first])]
        if stage == 2:
            part = r1.at[j, :, 1 - y] if order == 0 else r1.at[j, :, 1 - x]
            return [make(part, r2.at[j], 2, across["yx"[order]])]
        if stage == 3:
            return [
                make(r2.at[j, lax.rem(z + k + 1, 4)], r3.at[j, k], 3 + k, along[k])
                for k in range(3)
            ]
        share = rows // 2
        return [make(f3.at[j, pl.ds(pl.multiple_of(other * share, 8), share)], r4.at[j], 6, sibling)]

    f32 = jnp.float32

    def add(plan, stage, order, i):
        pieces, rows, width, parts, src, out, r0, r1, r2, r3, f3, r4, send, recv = plan
        j, matrix, column = where(plan, order, i)
        if stage == 0:
            lanes = pl.ds(pl.multiple_of(mine + column, 128), width)

            @pl.loop(0, 16)
            def _(block):
                a, b, d = lax.div(block, 4), lax.rem(lax.div(block, 2), 2), lax.rem(block, 2)
                r0[j, a, b, d] = (
                    r0[j, a, b, d].astype(f32) + src[matrix, a, b, d, :, lanes].astype(f32)
                ).astype(jnp.bfloat16)
        elif stage == 1:
            @pl.loop(0, 8)
            def _(block):
                a, b = lax.div(block, 2), lax.rem(block, 2)
                own = r0[j, a, b, x] if order == 0 else r0[j, a, y, b]
                r1[j, a, b] = (r1[j, a, b].astype(f32) + own.astype(f32)).astype(jnp.bfloat16)
        elif stage == 2:
            @pl.loop(0, 4)
            def _(a):
                own = r1[j, a, y] if order == 0 else r1[j, a, x]
                r2[j, a] = (r2[j, a].astype(f32) + own.astype(f32)).astype(jnp.bfloat16)
        elif stage == 3:
            f3[j] = (r3[j, 0].astype(f32) + r3[j, 1].astype(f32)) + (
                r3[j, 2].astype(f32) + r2[j, z].astype(f32)
            )
        else:
            share = rows // 2
            lanes = pl.ds(pl.multiple_of(mine + column, 128), width)
            out[matrix, :, lanes] = f3[j, pl.ds(pl.multiple_of(core * share, 8), share)]
            lanes = pl.ds(pl.multiple_of(theirs + column, 128), width)
            out[matrix, :, lanes] = r4[j]

    def each(plan, body):
        @pl.loop(0, plan[0] // 2)
        def _(i):
            for order in range(2):
                body(order, i)

    def start(plan, stage):
        def body(order, i):
            for copy in copies(plan, stage, order, i):
                copy.start()

        each(plan, body)

    def step(plan, stage, order, i):
        for copy in copies(plan, stage, order, i):
            copy.wait_recv()
        add(plan, stage, order, i)
        if stage < 4:
            for copy in copies(plan, stage + 1, order, i):
                copy.start()

    def finish(plan, stage):
        def body(order, i):
            for copy in copies(plan, stage, order, i):
                copy.wait_send()

        each(plan, body)

    for plan in plans:
        start(plan, 0)
    for plan in plans:
        turns = plan[0] // 2

        @pl.loop(0, turns + 4)
        def _(turn):
            for stage in range(5):
                @pl.when((turn >= stage) & (turn < turns + stage))
                def _():
                    for order in range(2):
                        step(plan, stage, order, turn - stage)

            if plan is plans[0]:
                for stage in range(4):
                    @pl.when(turn == stage)
                    def _():
                        small_step(stage)

    for stage in range(5):
        for plan in plans:
            finish(plan, stage)
    if has_small:
        for stage in range(4):
            for copy in small_copies(stage):
                copy.wait_send()


def reduce_scatter(arrays, small, collective_id, split=1):
    groups, views, outs, scratch = [], [], [], []
    bf16, f32 = jnp.bfloat16, jnp.float32
    if small is not None:
        scratch += [
            pltpu.VMEM((7,) + small.shape, f32),
            pltpu.VMEM((3,) + small.shape, f32),
            pltpu.SemaphoreType.DMA((6,)),
            pltpu.SemaphoreType.DMA((6,)),
        ]
    for array in arrays:
        matrices, height, width_all = array.shape
        rows = height // 16
        parts = 3 if matrices == 2 else split
        pieces, width = matrices * parts, 384 // parts
        groups.append((pieces, rows, width, parts))
        views.append(array.reshape(matrices, 4, 2, 2, rows, width_all))
        outs.append(jax.ShapeDtypeStruct((matrices, rows // 2, width_all), f32))
        scratch += [
            pltpu.VMEM((pieces, 4, 2, 2, rows, width), bf16),
            pltpu.VMEM((pieces, 4, 2, rows, width), bf16),
            pltpu.VMEM((pieces, 4, rows, width), bf16),
            pltpu.VMEM((pieces, 3, rows, width), bf16),
            pltpu.VMEM((pieces, rows, width), f32),
            pltpu.VMEM((pieces, rows // 2, width), f32),
            pltpu.SemaphoreType.DMA((7, pieces)),
            pltpu.SemaphoreType.DMA((7, pieces)),
        ]
    if small is not None:
        views.append(small)
        outs.append(jax.ShapeDtypeStruct(small.shape, f32))
    vmem = pl.BlockSpec(memory_space=pltpu.VMEM)
    return pl.pallas_call(
        functools.partial(reduce_kernel, tuple(groups), small is not None),
        out_shape=tuple(outs),
        in_specs=[vmem] * len(views),
        out_specs=tuple([vmem] * len(outs)),
        scratch_shapes=scratch,
        compiler_params=pltpu.CompilerParams(
            collective_id=collective_id, has_side_effects=True, vmem_limit_bytes=60 << 20
        ),
    )(*views)


def gather_kernel(split, own, full, theirs, send, recv):
    z, y, x, core = place()
    other = 1 - core
    sibling = device(z, y, x, other)
    across = {"x": device(z, y, 1 - x, core), "y": device(z, 1 - y, x, core)}
    along = [device(lax.rem(z + k, 4), y, x, core) for k in (1, 2, 3)]
    greet([sibling, across["x"], across["y"]] + along)
    matrices, share, width = own.shape
    half = width // 2
    pieces, thin = matrices * split, half // split

    def spot(j):
        column = lax.rem(j, split) * thin
        return (
            lax.div(j, split),
            pl.ds(pl.multiple_of(core * half + column, 128), thin),
            pl.ds(pl.multiple_of(other * half + column, 128), thin),
        )

    def make(source, target, slot, j, partner):
        return pltpu.make_async_remote_copy(
            source, target, send.at[slot, j], recv.at[slot, j], device_id=partner, device_id_type=MESH
        )

    def copies(stage, order, i):
        j = i + order * (pieces // 2)
        m, mine, rest = spot(j)
        first = "yx"[order]
        if stage == 0:
            return [make(own.at[m, :, rest], theirs.at[j], 0, j, sibling)]
        if stage == 1:
            part = full.at[m, z, y, x, :, mine]
            return [make(part, part, 1 + k, j, along[k]) for k in range(3)]
        if stage == 2:
            part = full.at[m, :, y, x, :, mine]
            return [make(part, part, 4, j, across[first])]
        if stage == 3:
            part = full.at[m, :, :, x, :, mine] if order == 0 else full.at[m, :, y, :, :, mine]
            return [make(part, part, 5, j, across["xy"[order]])]
        part = full.at[m, :, :, :, :, mine]
        return [make(part, part, 6, j, sibling)]

    def each(body):
        @pl.loop(0, pieces // 2)
        def _(i):
            for order in range(2):
                body(order, i)

    def start(stage):
        def body(order, i):
            for copy in copies(stage, order, i):
                copy.start()

        each(body)

    def step(stage, order, i):
        for copy in copies(stage, order, i):
            copy.wait_recv()
        if stage == 0:
            j = i + order * (pieces // 2)
            m, mine, _ = spot(j)

            @pl.when(core == 0)
            def _():
                full[m, z, y, x, :, mine] = jnp.concatenate(
                    [own[m, :, mine], theirs[j]], axis=0
                ).astype(jnp.bfloat16)

            @pl.when(core == 1)
            def _():
                full[m, z, y, x, :, mine] = jnp.concatenate(
                    [theirs[j], own[m, :, mine]], axis=0
                ).astype(jnp.bfloat16)
        if stage < 4:
            for copy in copies(stage + 1, order, i):
                copy.start()

    def finish(stage):
        def body(order, i):
            for copy in copies(stage, order, i):
                copy.wait_send()

        each(body)

    start(0)
    turns = pieces // 2

    @pl.loop(0, turns + 4)
    def _(turn):
        for stage in range(5):
            @pl.when((turn >= stage) & (turn < turns + stage))
            def _():
                for order in range(2):
                    step(stage, order, turn - stage)

    for stage in range(5):
        finish(stage)


def gather_rows(own, collective_id, split=1):
    matrices, share, width = own.shape
    pieces = matrices * split
    vmem = pl.BlockSpec(memory_space=pltpu.VMEM)
    full = pl.pallas_call(
        functools.partial(gather_kernel, split),
        out_shape=jax.ShapeDtypeStruct((matrices, 4, 2, 2, 2 * share, width), jnp.bfloat16),
        in_specs=[vmem],
        out_specs=vmem,
        scratch_shapes=[
            pltpu.VMEM((pieces, share, width // 2 // split), jnp.float32),
            pltpu.SemaphoreType.DMA((7, pieces)),
            pltpu.SemaphoreType.DMA((7, pieces)),
        ],
        compiler_params=pltpu.CompilerParams(
            collective_id=collective_id, has_side_effects=True, vmem_limit_bytes=32 << 20
        ),
    )(own)
    return full.reshape(matrices, 32 * share, width)


def gram_kernel(gram, out, other_sum, half_a, half_b, final, send, recv):
    z, y, x, core = place()
    sibling = device(z, y, x, 1 - core)
    x_side, y_side = device(z, y, 1 - x, core), device(z, 1 - y, x, core)
    greet([sibling, x_side, y_side])
    side = gram.shape[0] // 2
    rows = pl.ds(pl.multiple_of(core * side, 8), side)
    rest = pl.ds(pl.multiple_of((1 - core) * side, 8), side)

    def send_to(source, target, slot, partner):
        return pltpu.make_async_remote_copy(
            source, target, send.at[slot], recv.at[slot], device_id=partner, device_id_type=MESH
        )

    first = send_to(gram.at[rest], other_sum.at[rest], 0, sibling)
    second = send_to(gram.at[rows], other_sum.at[rows], 1, sibling)
    first.start()
    second.start()
    mine = send_to(gram.at[rows], other_sum.at[rows], 0, sibling)
    mine.wait_recv()
    out[rows] = gram[rows] + other_sum[rows]
    theirs = send_to(gram.at[rest], other_sum.at[rest], 1, sibling)
    theirs.wait_recv()

    @pl.when(z < 2)
    def _():
        out[rest] = gram[rest] + other_sum[rest]

    @pl.when(z >= 2)
    def _():
        def pair(one, two):
            step = send_to(out.at[rows], half_a, 2, one)
            step.start()
            step.wait_recv()
            step.wait_send()
            half_b[...] = out[rows] + half_a[...]
            step = send_to(half_b, final, 3, two)
            step.start()
            step.wait_recv()
            out[rows] = half_b[...] + final[...]
            step.wait_send()

        @pl.when(core == 0)
        def _():
            pair(x_side, y_side)

        @pl.when(core == 1)
        def _():
            pair(y_side, x_side)

        last = send_to(out.at[rows], out.at[rows], 4, sibling)
        last.start()
        arrive = send_to(out.at[rest], out.at[rest], 4, sibling)
        arrive.wait_recv()
        last.wait_send()

    first.wait_send()
    second.wait_send()


def gram_sum(gram, collective_id):
    f32 = jnp.float32
    side = gram.shape[0] // 2
    vmem = pl.BlockSpec(memory_space=pltpu.VMEM)
    return pl.pallas_call(
        gram_kernel,
        out_shape=jax.ShapeDtypeStruct(gram.shape, f32),
        in_specs=[vmem],
        out_specs=vmem,
        scratch_shapes=[
            pltpu.VMEM(gram.shape, f32),
            pltpu.VMEM((side, gram.shape[1]), f32),
            pltpu.VMEM((side, gram.shape[1]), f32),
            pltpu.VMEM((side, gram.shape[1]), f32),
            pltpu.SemaphoreType.DMA((5,)),
            pltpu.SemaphoreType.DMA((5,)),
        ],
        compiler_params=pltpu.CompilerParams(
            collective_id=collective_id, has_side_effects=True, vmem_limit_bytes=32 << 20
        ),
    )(gram)


SIDE = 256


def sweep_kernel(packed, rows, out, gram, held, now, poly, step):
    blocks = gram.shape[0] // SIDE
    width = blocks * SIDE

    def put(target, a, values):
        for b in range(a, blocks):
            block = values[:, (b - a) * SIDE : (b - a) * SIDE + SIDE]
            for i, j, piece in ((a, b, block),) if a == b else ((a, b, block), (b, a, block.T)):
                columns = slice(j * SIDE, j * SIDE + SIDE)
                top = piece.astype(BF16)
                target[i * SIDE : i * SIDE + SIDE, columns] = top
                target[width + i * SIDE : width + i * SIDE + SIDE, columns] = (
                    piece - top.astype(F32)
                ).astype(BF16)
                target[2 * width + i * SIDE : 2 * width + i * SIDE + SIDE, columns] = top

    def exact(left, a, right):
        high = left[a * SIDE : a * SIDE + SIDE]
        low = left[width + a * SIDE : width + a * SIDE + SIDE]
        return times(jnp.concatenate([high, high, low], axis=1), right[:, a * SIDE :])

    index, trace = 0, jnp.zeros((1, 1), F32)
    row = lax.broadcasted_iota(jnp.int32, (SIDE, SIDE), 0)
    column = lax.broadcasted_iota(jnp.int32, (SIDE, SIDE), 1)
    unit = jnp.where(row == column, 1.0, 0.0)
    for a in range(blocks):
        for b in range(a, blocks):
            block = packed[index * SIDE : index * SIDE + SIDE]
            gram[a * SIDE : a * SIDE + SIDE, b * SIDE : b * SIDE + SIDE] = block
            if a == b:
                trace = trace + jnp.sum(
                    jnp.sum(block * unit, axis=1, keepdims=True), axis=0, keepdims=True
                )
            else:
                gram[b * SIDE : b * SIDE + SIDE, a * SIDE : a * SIDE + SIDE] = block.T
            index += 1
    scale = 1.0 / (jnp.sqrt(trace) + FLOOR_EPSILON)

    for a in range(blocks):
        put(now, a, gram[a * SIDE : a * SIDE + SIDE, a * SIDE :] * (scale * scale))
    count = rows.shape[0]

    def keep(some, rest, values):
        top = values.astype(BF16)
        held[some] = top
        held[rest] = (values - top.astype(F32)).astype(BF16)

    keep(slice(0, count), slice(count, 2 * count), rows[...].astype(F32) * scale)

    @pl.loop(0, ITERS)
    def _(sweep):
        for a in range(blocks):
            row = lax.broadcasted_iota(jnp.int32, (SIDE, width - a * SIDE), 0)
            column = lax.broadcasted_iota(jnp.int32, (SIDE, width - a * SIDE), 1)
            lines = slice(a * SIDE, a * SIDE + SIDE)
            below = slice(width + a * SIDE, width + a * SIDE + SIDE)
            values = exact(now, a, now) * THIRD_TERM + SECOND_TERM * (
                now[lines, a * SIDE :].astype(F32) + now[below, a * SIDE :].astype(F32)
            )
            put(poly, a, jnp.where(row == column, values + FIRST_TERM, values))

        @pl.loop(0, count // 128)
        def _(a):
            some = pl.ds(pl.multiple_of(a * 128, 128), 128)
            rest = pl.ds(pl.multiple_of(a * 128 + count, 128), 128)
            high, low = held[some], held[rest]
            keep(some, rest, times(jnp.concatenate([high, high, low], axis=1), poly[...]))

        @pl.when(sweep < ITERS - 1)
        def _():
            for a in range(blocks):
                put(step, a, exact(now, a, poly))
            for a in range(blocks):
                put(now, a, exact(step, a, poly))

    out[...] = held[0:count]


def sweeps(packed, rows):
    width = rows.shape[1]
    vmem = pl.BlockSpec(memory_space=pltpu.VMEM)
    part = pltpu.VMEM((3 * width, width), BF16)
    return pl.pallas_call(
        sweep_kernel,
        out_shape=jax.ShapeDtypeStruct(rows.shape, BF16),
        in_specs=[vmem, vmem],
        out_specs=vmem,
        scratch_shapes=[
            pltpu.VMEM((width, width), F32),
            pltpu.VMEM((2 * rows.shape[0], width), BF16),
        ]
        + [part] * 3,
        compiler_params=pltpu.CompilerParams(vmem_limit_bytes=48 << 20),
        cost_estimate=pl.CostEstimate(flops=40_000_000_000, bytes_accessed=5_000_000, transcendentals=0),
    )(packed, rows)


def upper_blocks(gram):
    blocks = gram.shape[0] // SIDE
    return jnp.concatenate(
        [
            gram[a * SIDE : a * SIDE + SIDE, b * SIDE : b * SIDE + SIDE]
            for a in range(blocks)
            for b in range(a, blocks)
        ],
        axis=0,
    )


def matmul3(left, right):
    return jnp.matmul(left, right, precision=lax.Precision.HIGH)


def to_owner_rows(square_state, tall_state, count):
    rows = square_state.shape[1]
    group = count // 16
    if rows % group == 0:
        piece = rows // group
        pieces = jnp.concatenate(
            [
                square_state.reshape(8 * group, piece, D),
                tall_state.reshape(8 * group, piece, D),
            ],
            axis=0,
        ).astype(jnp.bfloat16)
        return lax.all_to_all(pieces, AXES, 0, 0, tiled=True).reshape(count * piece, D)
    square_all = lax.all_gather(square_state.astype(jnp.bfloat16), AXES, axis=1, tiled=True)
    tall_all = lax.all_gather(tall_state.astype(jnp.bfloat16), AXES, axis=1, tiled=True)
    joined = jnp.concatenate([square_all.reshape(-1, D), tall_all.reshape(-1, D)], axis=0)
    own = joined.shape[0] // count
    return lax.dynamic_slice_in_dim(joined, lax.axis_index(AXES) * own, own, axis=0)


def from_owner_rows(rows_out, count, square_rows, tall_rows):
    group = count // 16
    rows_out = rows_out.astype(jnp.bfloat16)
    if square_rows % group == 0:
        piece = square_rows // group
        back = lax.all_to_all(rows_out.reshape(count, piece, D), AXES, 0, 0, tiled=True)
        return (
            back[: 8 * group].reshape(8, square_rows, D),
            back[8 * group :].reshape(2, tall_rows, D),
        )
    joined = lax.all_gather(rows_out, AXES, axis=0, tiled=True)
    square_all = joined[: 8 * square_rows * count].reshape(8, square_rows * count, D)
    tall_all = joined[8 * square_rows * count :].reshape(2, tall_rows * count, D)
    index = lax.axis_index(AXES)
    return (
        lax.dynamic_slice_in_dim(square_all, index * square_rows, square_rows, axis=1),
        lax.dynamic_slice_in_dim(tall_all, index * tall_rows, tall_rows, axis=1),
    )


def orthogonal_rows(rows_in, kernels):
    gram = lax.dot_general(
        rows_in, rows_in, (((0,), (0,)), ((), ())), preferred_element_type=jnp.float32
    )
    if kernels:
        return sweeps(gram_sum(upper_blocks(gram), 2), rows_in)
    rows_in = rows_in.astype(jnp.float32)
    gram = lax.psum(gram, "row")
    is_tall = lax.axis_index("tall") >= 2
    gram = jnp.where(is_tall, lax.psum(jnp.where(is_tall, gram, 0.0), "square"), gram)
    eye = (jnp.arange(D)[:, None] == jnp.arange(D)[None, :]).astype(jnp.float32)
    scale = 1.0 / (jnp.sqrt(jnp.sum(gram * eye)) + FLOOR_EPSILON)
    gram = gram * (scale * scale)
    current = rows_in * scale

    for sweep in range(ITERS):
        poly = FIRST_TERM * eye + SECOND_TERM * gram + THIRD_TERM * matmul3(gram, gram)
        current = matmul3(current, poly)
        if sweep < ITERS - 1:
            gram = matmul3(matmul3(gram, poly), poly)
    return current


def local(
    inputs,
    memory,
    cotangent,
    lengths,
    memory_len,
    square_master,
    tall_master,
    square_momentum,
    tall_momentum,
    vectors,
    feed_vectors,
    head_scale,
    relative,
):
    count = lax.axis_size(AXES)
    kernels = count == 32
    index = lax.axis_index(AXES)
    if kernels:
        square_copy = gather_rows(square_master, 3, 3)
    else:
        square_copy = lax.all_gather(
            square_master.astype(jnp.bfloat16), AXES, axis=1, tiled=True
        )
    tall_copy = lax.all_gather(tall_master.astype(jnp.bfloat16), AXES, axis=1, tiled=True)
    width = inputs.shape[2]
    vec, feed = vectors.astype(F32), feed_vectors.astype(F32)
    head_row = jnp.repeat(head_scale.astype(F32), width // head_scale.shape[0])[None]
    bias = jnp.roll(relative.astype(F32)[:, ::-1], 1, axis=1)
    flat_in, flat_memory = inputs.reshape(-1, width), memory.reshape(-1, width)
    left, q, k, v, p, o, h1, cq, ck, cv, pc, co, h2 = attention_forward(
        flat_in, flat_memory, memory_len, square_copy, vec, head_row, bias
    )
    output, dh2, narrow, wide, late_slope, feed_slope = feed_both(
        h2, cotangent.reshape(-1, width), lengths, tall_copy, vec, feed
    )

    tall_slope = jnp.einsum("btf,btd->bfd", wide, narrow, preferred_element_type=F32).astype(BF16)
    tall_slope, dh2 = lax.optimization_barrier((tall_slope, dh2))
    tall_sum = lax.psum_scatter(tall_slope, AXES, scatter_dimension=1, tiled=True).astype(F32)
    input_slope, memory_slope, right, far, early_slope, bias_slope = attention_backward(
        flat_in, dh2, square_copy, vec, head_row, (q, k, v, p, o, h1, cq, ck, cv, pc, co)
    )
    square_slope = square_slopes(left, right, flat_memory, far)
    vector_slope = jnp.concatenate([early_slope[:14], late_slope], axis=0)
    scale_slope = jnp.sum(early_slope[17].reshape(head_scale.shape[0], -1), axis=1)
    bias_slope = jnp.roll(bias_slope, 1, axis=1)
    small = [
        jnp.sum(lengths).astype(jnp.float32).reshape(1),
        scale_slope.reshape(-1),
        bias_slope.reshape(-1),
        vector_slope.reshape(-1),
        feed_slope.reshape(-1),
    ]
    sizes = [piece.shape[0] for piece in small]
    starts = [sum(sizes[:i]) for i in range(len(sizes) + 1)]
    if kernels:
        lines = -(-starts[-1] // 1024) * 8
        small.append(jnp.zeros((lines * 128 - starts[-1],), jnp.float32))
        square_sum, summed = reduce_scatter(
            [square_slope], jnp.concatenate(small).reshape(lines, 128), 1
        )
        summed = summed.reshape(-1)
    else:
        square_sum = lax.psum_scatter(
            square_slope, AXES, scatter_dimension=1, tiled=True
        ).astype(jnp.float32)
        summed = lax.psum(jnp.concatenate(small), AXES)
    total, scale_sum, bias_sum, vector_sum, feed_sum = (
        summed[starts[i] : starts[i + 1]] for i in range(len(sizes))
    )
    factor = inputs.shape[0] * count / total[0]
    bias_sum = bias_sum.reshape(bias_slope.shape)
    width = vector_slope.shape[1] // count
    vector_sum = lax.dynamic_slice_in_dim(
        vector_sum.reshape(vector_slope.shape), index * width, width, axis=1
    )
    width = feed_slope.shape[1] // count
    feed_sum = lax.dynamic_slice_in_dim(
        feed_sum.reshape(feed_slope.shape), index * width, width, axis=1
    )
    square_state = MOMENTUM_DECAY * square_momentum + factor * square_sum
    tall_state = MOMENTUM_DECAY * tall_momentum + factor * tall_sum
    rows_out = orthogonal_rows(to_owner_rows(square_state, tall_state, count), kernels)
    square, tall = from_owner_rows(
        rows_out, count, square_state.shape[1], tall_state.shape[1]
    )
    square, tall = square.astype(jnp.float32), tall.astype(jnp.float32)
    square_weight = square_master * (1.0 - LEARN_RATE * WEIGHT_DECAY) - LEARN_RATE * square
    tall_weight = (
        tall_master * (1.0 - LEARN_RATE * WEIGHT_DECAY)
        - LEARN_RATE * max(1.0, FF / D) ** 0.5 * tall
    )
    return (
        output.reshape(inputs.shape),
        input_slope.reshape(inputs.shape),
        memory_slope.reshape(memory.shape),
        square_state,
        tall_state,
        square_weight,
        tall_weight,
        factor * vector_sum,
        factor * feed_sum,
        factor * scale_sum,
        factor * bias_sum,
    )


def solution(mesh):
    count = mesh.devices.size
    grouped = Mesh(mesh.devices.reshape(4, 4, count // 16), AXES)
    placed = (
        P(AXES, None, None),
        P(AXES, None, None),
        P(AXES, None, None),
        P(AXES),
        P(AXES),
        P(None, AXES, None),
        P(None, AXES, None),
        P(None, AXES, None),
        P(None, AXES, None),
        P(),
        P(),
        P(),
        P(),
    )
    return jax.shard_map(
        local,
        mesh=grouped,
        in_specs=placed,
        out_specs=(
            P(AXES, None, None),
            P(AXES, None, None),
            P(AXES, None, None),
            P(None, AXES, None),
            P(None, AXES, None),
            P(None, AXES, None),
            P(None, AXES, None),
            P(None, AXES),
            P(None, AXES),
            P(),
            P(),
        ),
        check_vma=False,
    )
```

```python
import functools

import jax
import jax.numpy as jnp
from jax import lax
from jax.experimental import pallas as pl
from jax.experimental.pallas import tpu as pltpu
from jax.sharding import Mesh, PartitionSpec as P

D = 768
FF = 3072
ITERS = 5


NORM_EPSILON = 1e-05
FLOOR_EPSILON = 1e-07
FIRST_TERM = 3.4445
SECOND_TERM = -4.775
THIRD_TERM = 2.0315
MOMENTUM_DECAY = 0.95
LEARN_RATE = 0.8
WEIGHT_DECAY = 0.01
NEGATIVE_LARGE = -1e30


F32, BF16 = jnp.float32, jnp.bfloat16
TOKENS = 256
SLOTS = 512
LANES = 128


def times(left, right):
    return jnp.dot(left, right, preferred_element_type=F32)


def times_back(left, right):
    return lax.dot_general(left, right, (((1,), (1,)), ((), ())), preferred_element_type=F32)


def times_down(left, right):
    return lax.dot_general(left, right, (((0,), (0,)), ((), ())), preferred_element_type=F32)


def down_to_keys(weights, values):
    if weights.shape[1] > values.shape[1]:
        return times_down(values, weights).astype(BF16).T
    return times_down(weights, values).astype(BF16)


def standard(values):
    center = values - jnp.mean(values, axis=-1, keepdims=True)
    scale = lax.rsqrt(jnp.mean(center * center, axis=-1, keepdims=True) + NORM_EPSILON)
    return center * scale, scale


def norm(values, gain, shift):
    return standard(values)[0] * gain + shift


def norm_back(values, slope, gain):
    hat, scale = standard(values)
    inner = slope * gain
    back = scale * (
        inner
        - jnp.mean(inner, axis=-1, keepdims=True)
        - hat * jnp.mean(inner * hat, axis=-1, keepdims=True)
    )
    return back, down(slope * hat), down(slope)


def down(values):
    return jnp.sum(values, axis=0, keepdims=True)


def head_masks():
    lane = lax.broadcasted_iota(jnp.int32, (1, LANES), 1)
    even = jnp.where(lane < LANES // 2, 1.0, 0.0)
    return even.astype(BF16), (1.0 - even).astype(BF16)


def stacked(pair, masks):
    return jnp.concatenate([pair * masks[0], pair * masks[1]], axis=0)


def side_by_side(rows):
    half = rows.shape[0] // 2
    return jnp.concatenate([rows[:half], rows[half:]], axis=1)


def soften(scores):
    weights = jnp.exp(scores - jnp.max(scores, axis=-1, keepdims=True))
    return (weights * (1.0 / jnp.sum(weights, axis=-1, keepdims=True))).astype(BF16)


def soften_back(weights, slope):
    weights = weights.astype(F32)
    product = weights * slope
    return (product - weights * jnp.sum(product, axis=-1, keepdims=True)).astype(BF16)


def attention_kernel(
    memory_len, x_in, memory, w, vec_in, hs, mirrored,
    left, q, k, v, p, o, h1, cq, ck, cv, pc, co, h2,
    bias, vec,
):
    step = pl.program_id(0)
    masks = head_masks()

    @pl.when(step == 0)
    def _():
        vec[...] = vec_in[...].astype(F32)
        row = lax.broadcasted_iota(jnp.int32, (128, 128), 0)
        column = lax.broadcasted_iota(jnp.int32, (128, 128), 1)
        for head in range(12):
            line = jnp.broadcast_to(mirrored[head : head + 1], (128, 128))
            line = pltpu.roll(line, 0, 1, stride=1, stride_axis=0)
            bias[head // 2, (head % 2) * 128 : (head % 2) * 128 + 128] = jnp.where(
                row >= column, line, NEGATIVE_LARGE
            )

    x = x_in[...].astype(F32)
    left[0] = norm(x, vec[0:1], vec[1:2]).astype(BF16)
    q[...] = ((times(left[0], w[0]) + vec[2:3]) * 0.125).astype(BF16)
    k[...] = times(left[0], w[1]).astype(BF16)
    v[...] = (times(left[0], w[2]) + vec[3:4]).astype(BF16)
    items = TOKENS // 128

    @pl.loop(0, 6, unroll=True)
    def _(pair):
        lanes = pl.ds(pl.multiple_of(pair * LANES, LANES), LANES)
        for item in range(items):
            rows = slice(item * 128, item * 128 + 128)
            scores = times_back(stacked(q[rows, lanes], masks), k[rows, lanes]) + bias[pair]
            weights = soften(scores)
            p[item, pair] = weights
            o[rows, lanes] = times(side_by_side(weights), stacked(v[rows, lanes], masks))

    left[1] = norm(o[...] * hs[...], vec[5:6], vec[6:7]).astype(BF16)
    h1[...] = x + (times(left[1], w[3]) + vec[4:5])
    left[2] = norm(h1[...], vec[7:8], vec[8:9]).astype(BF16)
    cq[...] = ((times(left[2], w[4]) + vec[9:10]) * 0.125).astype(BF16)
    ck[...] = times(memory[...], w[5]).astype(BF16)
    cv[...] = (times(memory[...], w[6]) + vec[10:11]).astype(BF16)
    slots = SLOTS // items
    column = lax.broadcasted_iota(jnp.int32, (1, slots), 1)

    @pl.loop(0, 6, unroll=True)
    def _(pair):
        lanes = pl.ds(pl.multiple_of(pair * LANES, LANES), LANES)
        for item in range(items):
            rows = slice(item * 128, item * 128 + 128)
            keys = slice(item * slots, item * slots + slots)
            limit = memory_len[step * items + item]
            scores = times_back(stacked(cq[rows, lanes], masks), ck[keys, lanes])
            weights = soften(jnp.where(column < limit, scores, NEGATIVE_LARGE))
            pc[item, pair] = weights
            co[rows, lanes] = times(side_by_side(weights), stacked(cv[keys, lanes], masks))

    left[3] = norm(co[...], vec[12:13], vec[13:14]).astype(BF16)
    h2[...] = h1[...] + (times(left[3], w[7]) + vec[11:12])


def whole(shape):
    return pl.BlockSpec(shape, lambda *_: (0,) * len(shape), pipeline_mode=pl.Buffered(1))


def by_rows(rows, width):
    return pl.BlockSpec((rows, width), lambda i: (i, 0))


def by_blocks(blocks, rows, width):
    return pl.BlockSpec((blocks, rows, width), lambda i: (0, i, 0))


def by_items(items, *rest):
    return pl.BlockSpec((items,) + rest, lambda i: (i,) + (0,) * len(rest))


def attention_forward(inputs, memory, memory_len, square, vectors, head_row, bias):
    tokens, width = inputs.shape
    slots = memory.shape[0]
    steps = tokens // TOKENS
    items = TOKENS // 128
    shapes = [
        (BF16, "l"), (BF16, "t"), (BF16, "t"), (BF16, "t"), (BF16, "p"), (F32, "t"), (F32, "t"),
        (BF16, "t"), (BF16, "m"), (BF16, "m"), (BF16, "c"), (F32, "t"), (F32, "t"),
    ]
    full = {"l": (4, tokens, width), "t": (tokens, width), "m": (slots, width), "p": (steps * items, 6, 256, 128), "c": (steps * items, 6, 256, SLOTS // items)}
    spec = {
        "l": by_blocks(4, TOKENS, width),
        "t": by_rows(TOKENS, width), "m": by_rows(SLOTS, width),
        "p": by_items(items, 6, 256, 128), "c": by_items(items, 6, 256, SLOTS // items),
    }
    return pl.pallas_call(
        attention_kernel,
        grid=(steps,),
        out_shape=tuple(jax.ShapeDtypeStruct(full[kind], kept) for kept, kind in shapes),
        in_specs=[
            pl.BlockSpec(memory_space=pltpu.SMEM),
            spec["t"], spec["m"], whole(square.shape), whole(vectors.shape), whole(head_row.shape), whole(bias.shape),
        ],
        out_specs=tuple(spec[kind] for _, kind in shapes),
        scratch_shapes=[pltpu.VMEM((6, 256, 128), F32), pltpu.VMEM(vectors.shape, F32)],
        compiler_params=pltpu.CompilerParams(vmem_limit_bytes=60 << 20),
        cost_estimate=pl.CostEstimate(flops=14_000_000_000, bytes_accessed=60_000_000, transcendentals=5_000_000),
    )(memory_len, inputs, memory, square, vectors, head_row, bias)


ROOT_HALF = 0.7071067811865476
INVERSE_ROOT = 0.3989422804014327
CHUNK = 1024


def feed_kernel(
    lengths, h2_in, cot, tall, vec_in, feed_in,
    out, dh2, narrow, wide, dvec, dfeed,
    u, g, dr, total, vec, feed,
):
    step = pl.program_id(0)
    items = TOKENS // 128
    width = tall.shape[1]
    chunks = width // CHUNK

    @pl.when(step == 0)
    def _():
        vec[...] = vec_in[...].astype(F32)
        feed[...] = feed_in[...].astype(F32)
        dvec[...] = jnp.zeros_like(dvec)
        dfeed[...] = jnp.zeros_like(dfeed)

    h2 = h2_in[...]
    narrow[0] = norm(h2, vec[14:15], vec[15:16]).astype(BF16)

    def at(i):
        return pl.ds(pl.multiple_of(i * CHUNK, CHUNK), CHUNK)

    def first(i, total):
        some = at(i)
        inner = times_back(narrow[0], tall[0, some]) + feed[0:1, some]
        bell = 0.5 + 0.5 * lax.erf(inner * ROOT_HALF)
        active = inner * bell
        g[:, some] = active
        u[:, some] = bell + inner * (jnp.exp(-0.5 * inner * inner) * INVERSE_ROOT)
        return total + jnp.sum(active, axis=-1, keepdims=True)

    zero = jnp.zeros((TOKENS, 1), F32)
    mean = lax.fori_loop(0, chunks, first, zero, unroll=True) * (1.0 / width)

    def second(i, total):
        center = g[:, at(i)] - mean
        return total + jnp.sum(center * center, axis=-1, keepdims=True)

    spread = lax.fori_loop(0, chunks, second, zero, unroll=True) * (1.0 / width)
    scale = lax.rsqrt(spread + NORM_EPSILON)
    row = lax.broadcasted_iota(jnp.int32, (128, 1), 0)
    valid = jnp.concatenate(
        [jnp.where(row < lengths[step * items + item], 1.0, 0.0) for item in range(items)], axis=0
    )
    dy32 = cot[...].astype(F32) * valid
    narrow[1] = dy32.astype(BF16)
    total[...] = h2 + vec[16:17]

    def third(i, sums):
        some = at(i)
        hat = (g[:, some] - mean) * scale
        g[:, some] = hat
        gain = feed[1:2, some]
        active = (hat * gain + feed[2:3, some]).astype(BF16)
        wide[1, :, some] = active
        total[...] += times(active, tall[1, some])
        slope = times_back(narrow[1], tall[1, some])
        dfeed[1:2, some] += down(slope * hat)
        dfeed[2:3, some] += down(slope)
        inner = slope * gain
        dr[:, some] = inner
        return (
            sums[0] + jnp.sum(inner, axis=-1, keepdims=True),
            sums[1] + jnp.sum(inner * hat, axis=-1, keepdims=True),
        )

    one, two = lax.fori_loop(0, chunks, third, (zero, zero), unroll=True)
    out[...] = total[...].astype(BF16)
    one, two = one * (1.0 / width), two * (1.0 / width)
    dh2[...] = jnp.zeros_like(dh2)

    def fourth(i, carry):
        some = at(i)
        back = scale * (dr[:, some] - one - g[:, some] * two)
        slope = (back * u[:, some]).astype(BF16)
        wide[0, :, some] = slope
        dfeed[0:1, some] += down(slope.astype(F32))
        dh2[...] += times(slope, tall[0, some])
        return carry

    lax.fori_loop(0, chunks, fourth, 0, unroll=True)
    back, gain_sum, shift_sum = norm_back(h2, dh2[...], vec[14:15])
    dvec[0:1] += gain_sum
    dvec[1:2] += shift_sum
    dvec[2:3] += down(dy32)
    dh2[...] = dy32 + back


def feed_both(hidden, cotangent, lengths, tall, vectors, feed_vectors):
    tokens, width = hidden.shape
    wide = tall.shape[1]
    steps = tokens // TOKENS
    some = by_rows(TOKENS, width)
    return pl.pallas_call(
        feed_kernel,
        grid=(steps,),
        out_shape=(
            jax.ShapeDtypeStruct((tokens, width), BF16),
            jax.ShapeDtypeStruct((tokens, width), F32),
            jax.ShapeDtypeStruct((2, tokens, width), BF16),
            jax.ShapeDtypeStruct((2, tokens, wide), BF16),
            jax.ShapeDtypeStruct((3, width), F32),
            jax.ShapeDtypeStruct((3, wide), F32),
        ),
        in_specs=[
            pl.BlockSpec(memory_space=pltpu.SMEM),
            some, some, whole(tall.shape), whole(vectors.shape), whole(feed_vectors.shape),
        ],
        out_specs=(
            some, some, by_blocks(2, TOKENS, width), by_blocks(2, TOKENS, wide),
            pl.BlockSpec((3, width), lambda i: (0, 0)),
            pl.BlockSpec((3, wide), lambda i: (0, 0)),
        ),
        scratch_shapes=[pltpu.VMEM((TOKENS, wide), F32)] * 3
        + [
            pltpu.VMEM((TOKENS, width), F32),
            pltpu.VMEM(vectors.shape, F32),
            pltpu.VMEM(feed_vectors.shape, F32),
        ],
        compiler_params=pltpu.CompilerParams(vmem_limit_bytes=60 << 20),
        cost_estimate=pl.CostEstimate(flops=20_000_000_000, bytes_accessed=40_000_000, transcendentals=7_000_000),
    )(lengths, hidden, cotangent, tall, vectors, feed_vectors)


def attention_back_kernel(
    x_in, dh2, w, vec_in, hs,
    q, k, v, p, o, h1, cq, ck, cv, pc, co,
    dx, dmem, right, far, dvec, drel,
    do, dh1, dbias, vec,
):
    step = pl.program_id(0)
    masks = head_masks()
    items = TOKENS // 128
    slots = SLOTS // items

    @pl.when(step == 0)
    def _():
        vec[...] = vec_in[...].astype(F32)
        dvec[...] = jnp.zeros_like(dvec)
        dbias[...] = jnp.zeros_like(dbias)

    def note(row, value):
        dvec[row : row + 1] += value

    right[5] = dh2[...].astype(BF16)
    note(11, down(right[5].astype(F32)))
    back, gain_sum, shift_sum = norm_back(co[...], times_back(right[5], w[7]), vec[12:13])
    note(12, gain_sum)
    note(13, shift_sum)
    do[...] = back.astype(BF16)

    def through(pair, item, keys, query, key, value, weights, dquery, dkey, dvalue, with_bias):
        lanes = pl.ds(pl.multiple_of(pair * LANES, LANES), LANES)
        rows = slice(item * 128, item * 128 + 128)
        kept = weights[item, pair]
        grad = stacked(do[rows, lanes], masks)
        dvalue[keys, lanes] = down_to_keys(kept, grad)
        slope = soften_back(kept, times_back(grad, value[keys, lanes]))
        dquery[rows, lanes] = (
            times(side_by_side(slope), stacked(key[keys, lanes], masks)).astype(BF16) * 0.125
        ).astype(BF16)
        dkey[keys, lanes] = down_to_keys(slope, stacked(query[rows, lanes], masks))
        if with_bias:
            dbias[pair] += slope.astype(F32)

    @pl.loop(0, 6, unroll=True)
    def _(pair):
        for item in range(items):
            keys = slice(item * slots, item * slots + slots)
            through(pair, item, keys, cq, ck, cv, pc, right.at[4], far.at[0], far.at[1], False)

    note(9, down(right[4].astype(F32)))
    note(10, down(far[1].astype(F32)))
    dmem[...] = (times_back(far[0], w[5]) + times_back(far[1], w[6])).astype(BF16)
    back, gain_sum, shift_sum = norm_back(h1[...], times_back(right[4], w[4]), vec[7:8])
    note(7, gain_sum)
    note(8, shift_sum)
    dh1[...] = dh2[...] + back
    right[3] = dh1[...].astype(BF16)
    note(4, down(right[3].astype(F32)))
    back, gain_sum, shift_sum = norm_back(o[...] * hs[...], times_back(right[3], w[3]), vec[5:6])
    note(5, gain_sum)
    note(6, shift_sum)
    note(17, down(back * o[...]))
    do[...] = (back * hs[...]).astype(BF16)

    @pl.loop(0, 6, unroll=True)
    def _(pair):
        for item in range(items):
            rows = slice(item * 128, item * 128 + 128)
            through(pair, item, rows, q, k, v, p, right.at[0], right.at[1], right.at[2], True)

    note(2, down(right[0].astype(F32)))
    note(3, down(right[2].astype(F32)))
    slope = times_back(right[0], w[0]) + times_back(right[1], w[1]) + times_back(right[2], w[2])
    back, gain_sum, shift_sum = norm_back(x_in[...].astype(F32), slope, vec[0:1])
    note(0, gain_sum)
    note(1, shift_sum)
    dx[...] = (dh1[...] + back).astype(BF16)

    @pl.when(step == pl.num_programs(0) - 1)
    def _():
        row = lax.broadcasted_iota(jnp.int32, (128, 128), 0)
        column = lax.broadcasted_iota(jnp.int32, (128, 128), 1)
        mirror = jnp.where(row + column == 127, 1.0, 0.0).astype(BF16)
        for head in range(12):
            part = dbias[head // 2, (head % 2) * 128 : (head % 2) * 128 + 128]
            high = part.astype(BF16)
            rest = part - high.astype(F32)
            middle = rest.astype(BF16)
            low = (rest - middle.astype(F32)).astype(BF16)
            flipped = times(high, mirror) + times(middle, mirror) + times(low, mirror)
            drel[head : head + 1] = down(pltpu.roll(flipped, 0, 1, stride=1, stride_axis=0))


def attention_backward(inputs, dh2, square, vectors, head_row, kept):
    tokens, width = inputs.shape
    q, k, v, p, o, h1, cq, ck, cv, pc, co = kept
    steps = tokens // TOKENS
    items = TOKENS // 128
    slots = ck.shape[0]
    t, m = by_rows(TOKENS, width), by_rows(SLOTS, width)
    ps, cs = by_items(items, 6, 256, 128), by_items(items, 6, 256, SLOTS // items)
    token = jax.ShapeDtypeStruct((tokens, width), BF16)
    slot = jax.ShapeDtypeStruct((slots, width), BF16)
    return pl.pallas_call(
        attention_back_kernel,
        grid=(steps,),
        out_shape=(
            token, slot,
            jax.ShapeDtypeStruct((6, tokens, width), BF16),
            jax.ShapeDtypeStruct((2, slots, width), BF16),
            jax.ShapeDtypeStruct((18, width), F32),
            jax.ShapeDtypeStruct((12, 128), F32),
        ),
        in_specs=[
            t, t, whole(square.shape), whole(vectors.shape), whole(head_row.shape),
            t, t, t, ps, t, t, t, m, m, cs, t,
        ],
        out_specs=(
            t, m, by_blocks(6, TOKENS, width), by_blocks(2, SLOTS, width),
            pl.BlockSpec((18, width), lambda i: (0, 0)),
            pl.BlockSpec((12, 128), lambda i: (0, 0)),
        ),
        scratch_shapes=[
            pltpu.VMEM((TOKENS, width), BF16),
            pltpu.VMEM((TOKENS, width), F32),
            pltpu.VMEM((6, 256, 128), F32),
            pltpu.VMEM(vectors.shape, F32),
        ],
        compiler_params=pltpu.CompilerParams(vmem_limit_bytes=60 << 20),
        cost_estimate=pl.CostEstimate(flops=16_000_000_000, bytes_accessed=60_000_000, transcendentals=0),
    )(inputs, dh2, square, vectors, head_row, q, k, v, p, o, h1, cq, ck, cv, pc, co)


def slope_kernel(left, right, memory, far, out):
    step = pl.program_id(0)
    width = out.shape[1]

    def product(from_left, from_right):
        @pl.loop(0, width // 256)
        def _(tile):
            some = pl.ds(pl.multiple_of(tile * 256, 256), 256)
            out[0, some] = times_down(from_left[:, some], from_right[...]).astype(BF16)

    @pl.when(step < 6)
    def _():
        product(left.at[0], right.at[0])

    @pl.when(step >= 6)
    def _():
        product(memory, far.at[0])


def square_slopes(left, right, memory, far):
    _, tokens, width = left.shape
    slots = memory.shape[0]
    return pl.pallas_call(
        slope_kernel,
        grid=(8,),
        out_shape=jax.ShapeDtypeStruct((8, width, width), BF16),
        in_specs=[
            pl.BlockSpec((1, tokens, width), lambda g: (jnp.clip(g - 2, 0, 3), 0, 0)),
            pl.BlockSpec((1, tokens, width), lambda g: (jnp.minimum(g, 5), 0, 0)),
            whole(memory.shape),
            pl.BlockSpec((1, slots, width), lambda g: (jnp.maximum(g - 6, 0), 0, 0)),
        ],
        out_specs=pl.BlockSpec(
            (1, width, width),
            lambda g: (jnp.where(g < 5, g, jnp.where(g == 5, 7, g - 1)), 0, 0),
        ),
        compiler_params=pltpu.CompilerParams(vmem_limit_bytes=60 << 20),
        cost_estimate=pl.CostEstimate(flops=12_000_000_000, bytes_accessed=30_000_000, transcendentals=0),
    )(left, right, memory, far)


AXES = ("tall", "square", "row")
MESH = pl.DeviceIdType.MESH


def place():
    z, plane, core = lax.axis_index("tall"), lax.axis_index("square"), lax.axis_index("row")
    return z, lax.div(plane, 2), lax.rem(plane, 2), core


def device(z, y, x, core):
    return (z, y * 2 + x, core)


def greet(partners):
    barrier = pltpu.get_barrier_semaphore()
    for partner in partners:
        pl.semaphore_signal(barrier, inc=1, device_id=partner, device_id_type=MESH)
    pl.semaphore_wait(barrier, len(partners))


def reduce_kernel(groups, has_small, *refs):
    n = len(groups)
    ins, refs = refs[:n], refs[n:]
    if has_small:
        small, refs = refs[0], refs[1:]
    outs, refs = refs[:n], refs[n:]
    if has_small:
        small_out, refs = refs[0], refs[1:]
    z, y, x, core = place()
    other = 1 - core
    sibling = device(z, y, x, other)
    across = {"x": device(z, y, 1 - x, core), "y": device(z, 1 - y, x, core)}
    along = [device(lax.rem(z + k, 4), y, x, core) for k in (1, 2, 3)]
    greet([sibling, across["x"], across["y"]] + along)
    mine = core * 384
    theirs = other * 384

    if has_small:
        held, total, refs = refs[0], refs[1], refs[2:]
        small_send, small_recv, refs = refs[0], refs[1], refs[2:]

        def small_copies(stage):
            source = small if stage == 0 else total.at[stage - 1]
            if stage < 3:
                partner = (sibling, across["x"], across["y"])[stage]
                return [
                    pltpu.make_async_remote_copy(
                        source, held.at[stage], small_send.at[stage], small_recv.at[stage],
                        device_id=partner, device_id_type=MESH,
                    )
                ]
            return [
                pltpu.make_async_remote_copy(
                    source, held.at[3 + z], small_send.at[3 + k], small_recv.at[3 + k],
                    device_id=along[k], device_id_type=MESH,
                )
                for k in range(3)
            ]

        for copy in small_copies(0):
            copy.start()

        def small_step(stage):
            for copy in small_copies(stage):
                copy.wait_recv()
            if stage < 3:
                own = small if stage == 0 else total.at[stage - 1]
                total[stage] = own[...] + held[stage]
                if stage == 2:
                    held[3 + z] = total[2]
                for copy in small_copies(stage + 1):
                    copy.start()
            else:
                small_out[...] = ((held[3] + held[4]) + held[5]) + held[6]
    else:
        def small_step(stage):
            pass

    plans = []
    for g, (pieces, rows, width, parts) in enumerate(groups):
        r0, r1, r2, r3, f3, r4, send, recv = refs[8 * g : 8 * g + 8]
        plans.append((pieces, rows, width, parts, ins[g], outs[g], r0, r1, r2, r3, f3, r4, send, recv))

    def where(plan, order, i):
        pieces, parts, width = plan[0], plan[3], plan[2]
        j = i + order * (pieces // 2)
        return j, lax.div(j, parts), pl.multiple_of(lax.rem(j, parts) * width, 128)

    def copies(plan, stage, order, i):
        pieces, rows, width, parts, src, out, r0, r1, r2, r3, f3, r4, send, recv = plan
        j, matrix, column = where(plan, order, i)
        first = "xy"[order]

        def make(source, target, slot, partner):
            return pltpu.make_async_remote_copy(
                source, target, send.at[slot, j], recv.at[slot, j],
                device_id=partner, device_id_type=MESH,
            )

        if stage == 0:
            lanes = pl.ds(pl.multiple_of(theirs + column, 128), width)
            return [make(src.at[matrix, :, :, :, :, lanes], r0.at[j], 0, sibling)]
        if stage == 1:
            part = r0.at[j, :, :, 1 - x] if order == 0 else r0.at[j, :, 1 - y]
            return [make(part, r1.at[j], 1, across[first])]
        if stage == 2:
            part = r1.at[j, :, 1 - y] if order == 0 else r1.at[j, :, 1 - x]
            return [make(part, r2.at[j], 2, across["yx"[order]])]
        if stage == 3:
            return [
                make(r2.at[j, lax.rem(z + k + 1, 4)], r3.at[j, k], 3 + k, along[k])
                for k in range(3)
            ]
        share = rows // 2
        return [make(f3.at[j, pl.ds(pl.multiple_of(other * share, 8), share)], r4.at[j], 6, sibling)]

    f32 = jnp.float32

    def add(plan, stage, order, i):
        pieces, rows, width, parts, src, out, r0, r1, r2, r3, f3, r4, send, recv = plan
        j, matrix, column = where(plan, order, i)
        if stage == 0:
            lanes = pl.ds(pl.multiple_of(mine + column, 128), width)

            @pl.loop(0, 4)
            def _(a):
                r0[j, a] = (
                    r0[j, a].astype(f32) + src[matrix, a, :, :, :, lanes].astype(f32)
                ).astype(jnp.bfloat16)
        elif stage == 1:
            @pl.loop(0, 4)
            def _(a):
                own = r0[j, a, :, x] if order == 0 else r0[j, a, y]
                r1[j, a] = (r1[j, a].astype(f32) + own.astype(f32)).astype(jnp.bfloat16)
        elif stage == 2:
            @pl.loop(0, 4)
            def _(a):
                own = r1[j, a, y] if order == 0 else r1[j, a, x]
                r2[j, a] = (r2[j, a].astype(f32) + own.astype(f32)).astype(jnp.bfloat16)
        elif stage == 3:
            f3[j] = (r3[j, 0].astype(f32) + r3[j, 1].astype(f32)) + (
                r3[j, 2].astype(f32) + r2[j, z].astype(f32)
            )
        else:
            share = rows // 2
            lanes = pl.ds(pl.multiple_of(mine + column, 128), width)
            out[matrix, :, lanes] = f3[j, pl.ds(pl.multiple_of(core * share, 8), share)]
            lanes = pl.ds(pl.multiple_of(theirs + column, 128), width)
            out[matrix, :, lanes] = r4[j]

    def each(plan, body, turns):
        @pl.loop(0, turns)
        def _(i):
            for order in range(2):
                body(order, i)

    def start(plan, stage, turns):
        def body(order, i):
            for copy in copies(plan, stage, order, i):
                copy.start()

        each(plan, body, turns)

    def step(plan, stage, order, i):
        for copy in copies(plan, stage, order, i):
            copy.wait_recv()
        add(plan, stage, order, i)
        if stage < 4:
            for copy in copies(plan, stage + 1, order, i):
                copy.start()

    def finish(plan, stage):
        def body(order, i):
            for copy in copies(plan, stage, order, i):
                copy.wait_send()

        each(plan, body, plan[0] // 2)

    for plan in plans:
        start(plan, 0, 2)
    for plan in plans:
        turns = plan[0] // 2

        @pl.loop(0, turns + 4)
        def _(turn):
            @pl.when(turn < turns - 2)
            def _():
                for order in range(2):
                    for copy in copies(plan, 0, order, turn + 2):
                        copy.start()

            for stage in range(5):
                @pl.when((turn >= stage) & (turn < turns + stage))
                def _():
                    for order in range(2):
                        step(plan, stage, order, turn - stage)

            if plan is plans[0]:
                for stage in range(4):
                    @pl.when(turn == stage)
                    def _():
                        small_step(stage)

    for stage in range(5):
        for plan in plans:
            finish(plan, stage)
    if has_small:
        for stage in range(4):
            for copy in small_copies(stage):
                copy.wait_send()


def reduce_scatter(arrays, small, collective_id, split=1):
    groups, views, outs, scratch = [], [], [], []
    bf16, f32 = jnp.bfloat16, jnp.float32
    if small is not None:
        scratch += [
            pltpu.VMEM((7,) + small.shape, f32),
            pltpu.VMEM((3,) + small.shape, f32),
            pltpu.SemaphoreType.DMA((6,)),
            pltpu.SemaphoreType.DMA((6,)),
        ]
    for array in arrays:
        matrices, height, width_all = array.shape
        rows = height // 16
        parts = 3 if matrices == 2 else split
        pieces, width = matrices * parts, 384 // parts
        groups.append((pieces, rows, width, parts))
        views.append(array.reshape(matrices, 4, 2, 2, rows, width_all))
        outs.append(jax.ShapeDtypeStruct((matrices, rows // 2, width_all), f32))
        scratch += [
            pltpu.VMEM((pieces, 4, 2, 2, rows, width), bf16),
            pltpu.VMEM((pieces, 4, 2, rows, width), bf16),
            pltpu.VMEM((pieces, 4, rows, width), bf16),
            pltpu.VMEM((pieces, 3, rows, width), bf16),
            pltpu.VMEM((pieces, rows, width), f32),
            pltpu.VMEM((pieces, rows // 2, width), f32),
            pltpu.SemaphoreType.DMA((7, pieces)),
            pltpu.SemaphoreType.DMA((7, pieces)),
        ]
    if small is not None:
        views.append(small)
        outs.append(jax.ShapeDtypeStruct(small.shape, f32))
    vmem = pl.BlockSpec(memory_space=pltpu.VMEM)
    return pl.pallas_call(
        functools.partial(reduce_kernel, tuple(groups), small is not None),
        out_shape=tuple(outs),
        in_specs=[vmem] * len(views),
        out_specs=tuple([vmem] * len(outs)),
        scratch_shapes=scratch,
        compiler_params=pltpu.CompilerParams(
            collective_id=collective_id, has_side_effects=True, vmem_limit_bytes=60 << 20
        ),
    )(*views)


def gather_kernel(split, own, full, theirs, send, recv):
    z, y, x, core = place()
    other = 1 - core
    sibling = device(z, y, x, other)
    across = {"x": device(z, y, 1 - x, core), "y": device(z, 1 - y, x, core)}
    along = [device(lax.rem(z + k, 4), y, x, core) for k in (1, 2, 3)]
    greet([sibling, across["x"], across["y"]] + along)
    matrices, share, width = own.shape
    half = width // 2
    pieces, thin = matrices * split, half // split

    def spot(j):
        column = lax.rem(j, split) * thin
        return (
            lax.div(j, split),
            pl.ds(pl.multiple_of(core * half + column, 128), thin),
            pl.ds(pl.multiple_of(other * half + column, 128), thin),
        )

    def make(source, target, slot, j, partner):
        return pltpu.make_async_remote_copy(
            source, target, send.at[slot, j], recv.at[slot, j], device_id=partner, device_id_type=MESH
        )

    def copies(stage, order, i):
        j = i + order * (pieces // 2)
        m, mine, rest = spot(j)
        first = "yx"[order]
        if stage == 0:
            return [make(own.at[m, :, rest], theirs.at[j], 0, j, sibling)]
        if stage == 1:
            part = full.at[m, z, y, x, :, mine]
            return [make(part, part, 1 + k, j, along[k]) for k in range(3)]
        if stage == 2:
            part = full.at[m, :, y, x, :, mine]
            return [make(part, part, 4, j, across[first])]
        if stage == 3:
            part = full.at[m, :, :, x, :, mine] if order == 0 else full.at[m, :, y, :, :, mine]
            return [make(part, part, 5, j, across["xy"[order]])]
        part = full.at[m, :, :, :, :, mine]
        return [make(part, part, 6, j, sibling)]

    def each(body):
        @pl.loop(0, pieces // 2)
        def _(i):
            for order in range(2):
                body(order, i)

    def start(stage):
        def body(order, i):
            for copy in copies(stage, order, i):
                copy.start()

        each(body)

    def step(stage, order, i):
        for copy in copies(stage, order, i):
            copy.wait_recv()
        if stage == 0:
            j = i + order * (pieces // 2)
            m, mine, _ = spot(j)

            @pl.when(core == 0)
            def _():
                full[m, z, y, x, :, mine] = jnp.concatenate(
                    [own[m, :, mine], theirs[j]], axis=0
                ).astype(jnp.bfloat16)

            @pl.when(core == 1)
            def _():
                full[m, z, y, x, :, mine] = jnp.concatenate(
                    [theirs[j], own[m, :, mine]], axis=0
                ).astype(jnp.bfloat16)
        if stage < 4:
            for copy in copies(stage + 1, order, i):
                copy.start()

    def finish(stage):
        def body(order, i):
            for copy in copies(stage, order, i):
                copy.wait_send()

        each(body)

    start(0)
    turns = pieces // 2

    @pl.loop(0, turns + 4)
    def _(turn):
        for stage in range(5):
            @pl.when((turn >= stage) & (turn < turns + stage))
            def _():
                for order in range(2):
                    step(stage, order, turn - stage)

    for stage in range(5):
        finish(stage)


def gather_rows(own, collective_id, split=1):
    matrices, share, width = own.shape
    pieces = matrices * split
    vmem = pl.BlockSpec(memory_space=pltpu.VMEM)
    full = pl.pallas_call(
        functools.partial(gather_kernel, split),
        out_shape=jax.ShapeDtypeStruct((matrices, 4, 2, 2, 2 * share, width), jnp.bfloat16),
        in_specs=[vmem],
        out_specs=vmem,
        scratch_shapes=[
            pltpu.VMEM((pieces, share, width // 2 // split), jnp.float32),
            pltpu.SemaphoreType.DMA((7, pieces)),
            pltpu.SemaphoreType.DMA((7, pieces)),
        ],
        compiler_params=pltpu.CompilerParams(
            collective_id=collective_id, has_side_effects=True, vmem_limit_bytes=32 << 20
        ),
    )(own)
    return full.reshape(matrices, 32 * share, width)


def gram_kernel(gram, out, other_sum, half_a, half_b, final, send, recv):
    z, y, x, core = place()
    sibling = device(z, y, x, 1 - core)
    x_side, y_side = device(z, y, 1 - x, core), device(z, 1 - y, x, core)
    greet([sibling, x_side, y_side])
    side = gram.shape[0] // 2
    rows = pl.ds(pl.multiple_of(core * side, 8), side)
    rest = pl.ds(pl.multiple_of((1 - core) * side, 8), side)

    def send_to(source, target, slot, partner):
        return pltpu.make_async_remote_copy(
            source, target, send.at[slot], recv.at[slot], device_id=partner, device_id_type=MESH
        )

    first = send_to(gram.at[rest], other_sum.at[rest], 0, sibling)
    second = send_to(gram.at[rows], other_sum.at[rows], 1, sibling)
    first.start()
    second.start()
    mine = send_to(gram.at[rows], other_sum.at[rows], 0, sibling)
    mine.wait_recv()
    out[rows] = gram[rows] + other_sum[rows]
    theirs = send_to(gram.at[rest], other_sum.at[rest], 1, sibling)
    theirs.wait_recv()

    @pl.when(z < 2)
    def _():
        out[rest] = gram[rest] + other_sum[rest]

    @pl.when(z >= 2)
    def _():
        def pair(one, two):
            step = send_to(out.at[rows], half_a, 2, one)
            step.start()
            step.wait_recv()
            step.wait_send()
            half_b[...] = out[rows] + half_a[...]
            step = send_to(half_b, final, 3, two)
            step.start()
            step.wait_recv()
            out[rows] = half_b[...] + final[...]
            step.wait_send()

        @pl.when(core == 0)
        def _():
            pair(x_side, y_side)

        @pl.when(core == 1)
        def _():
            pair(y_side, x_side)

        last = send_to(out.at[rows], out.at[rows], 4, sibling)
        last.start()
        arrive = send_to(out.at[rest], out.at[rest], 4, sibling)
        arrive.wait_recv()
        last.wait_send()

    first.wait_send()
    second.wait_send()


def gram_sum(gram, collective_id):
    f32 = jnp.float32
    side = gram.shape[0] // 2
    vmem = pl.BlockSpec(memory_space=pltpu.VMEM)
    return pl.pallas_call(
        gram_kernel,
        out_shape=jax.ShapeDtypeStruct(gram.shape, f32),
        in_specs=[vmem],
        out_specs=vmem,
        scratch_shapes=[
            pltpu.VMEM(gram.shape, f32),
            pltpu.VMEM((side, gram.shape[1]), f32),
            pltpu.VMEM((side, gram.shape[1]), f32),
            pltpu.VMEM((side, gram.shape[1]), f32),
            pltpu.SemaphoreType.DMA((5,)),
            pltpu.SemaphoreType.DMA((5,)),
        ],
        compiler_params=pltpu.CompilerParams(
            collective_id=collective_id, has_side_effects=True, vmem_limit_bytes=32 << 20
        ),
    )(gram)


SIDE = 256


def sweep_kernel(packed, rows, out, gram, held, now, poly, step):
    blocks = gram.shape[0] // SIDE
    width = blocks * SIDE

    def put(target, a, values):
        for b in range(a, blocks):
            block = values[:, (b - a) * SIDE : (b - a) * SIDE + SIDE]
            for i, j, piece in ((a, b, block),) if a == b else ((a, b, block), (b, a, block.T)):
                columns = slice(j * SIDE, j * SIDE + SIDE)
                top = piece.astype(BF16)
                target[i * SIDE : i * SIDE + SIDE, columns] = top
                target[width + i * SIDE : width + i * SIDE + SIDE, columns] = (
                    piece - top.astype(F32)
                ).astype(BF16)
                target[2 * width + i * SIDE : 2 * width + i * SIDE + SIDE, columns] = top

    def exact(left, a, right):
        high = left[a * SIDE : a * SIDE + SIDE]
        low = left[width + a * SIDE : width + a * SIDE + SIDE]
        return times(jnp.concatenate([high, high, low], axis=1), right[:, a * SIDE :])

    index, trace = 0, jnp.zeros((1, 1), F32)
    row = lax.broadcasted_iota(jnp.int32, (SIDE, SIDE), 0)
    column = lax.broadcasted_iota(jnp.int32, (SIDE, SIDE), 1)
    unit = jnp.where(row == column, 1.0, 0.0)
    for a in range(blocks):
        for b in range(a, blocks):
            block = packed[index * SIDE : index * SIDE + SIDE]
            gram[a * SIDE : a * SIDE + SIDE, b * SIDE : b * SIDE + SIDE] = block
            if a == b:
                trace = trace + jnp.sum(
                    jnp.sum(block * unit, axis=1, keepdims=True), axis=0, keepdims=True
                )
            else:
                gram[b * SIDE : b * SIDE + SIDE, a * SIDE : a * SIDE + SIDE] = block.T
            index += 1
    scale = 1.0 / (jnp.sqrt(trace) + FLOOR_EPSILON)

    for a in range(blocks):
        put(now, a, gram[a * SIDE : a * SIDE + SIDE, a * SIDE :] * (scale * scale))
    count = rows.shape[0]

    def keep(some, rest, values):
        top = values.astype(BF16)
        held[some] = top
        held[rest] = (values - top.astype(F32)).astype(BF16)

    keep(slice(0, count), slice(count, 2 * count), rows[...].astype(F32) * scale)

    @pl.loop(0, ITERS)
    def _(sweep):
        for a in range(blocks):
            row = lax.broadcasted_iota(jnp.int32, (SIDE, width - a * SIDE), 0)
            column = lax.broadcasted_iota(jnp.int32, (SIDE, width - a * SIDE), 1)
            lines = slice(a * SIDE, a * SIDE + SIDE)
            below = slice(width + a * SIDE, width + a * SIDE + SIDE)
            values = exact(now, a, now) * THIRD_TERM + SECOND_TERM * (
                now[lines, a * SIDE :].astype(F32) + now[below, a * SIDE :].astype(F32)
            )
            put(poly, a, jnp.where(row == column, values + FIRST_TERM, values))

        @pl.loop(0, count // 128)
        def _(a):
            some = pl.ds(pl.multiple_of(a * 128, 128), 128)
            rest = pl.ds(pl.multiple_of(a * 128 + count, 128), 128)
            high, low = held[some], held[rest]
            keep(some, rest, times(jnp.concatenate([high, high, low], axis=1), poly[...]))

        @pl.when(sweep < ITERS - 1)
        def _():
            for a in range(blocks):
                put(step, a, exact(now, a, poly))
            for a in range(blocks):
                put(now, a, exact(step, a, poly))

    out[...] = held[0:count]


def sweeps(packed, rows):
    width = rows.shape[1]
    vmem = pl.BlockSpec(memory_space=pltpu.VMEM)
    part = pltpu.VMEM((3 * width, width), BF16)
    return pl.pallas_call(
        sweep_kernel,
        out_shape=jax.ShapeDtypeStruct(rows.shape, BF16),
        in_specs=[vmem, vmem],
        out_specs=vmem,
        scratch_shapes=[
            pltpu.VMEM((width, width), F32),
            pltpu.VMEM((2 * rows.shape[0], width), BF16),
        ]
        + [part] * 3,
        compiler_params=pltpu.CompilerParams(vmem_limit_bytes=48 << 20),
        cost_estimate=pl.CostEstimate(flops=40_000_000_000, bytes_accessed=5_000_000, transcendentals=0),
    )(packed, rows)


def upper_blocks(gram):
    blocks = gram.shape[0] // SIDE
    return jnp.concatenate(
        [
            gram[a * SIDE : a * SIDE + SIDE, b * SIDE : b * SIDE + SIDE]
            for a in range(blocks)
            for b in range(a, blocks)
        ],
        axis=0,
    )


def matmul3(left, right):
    return jnp.matmul(left, right, precision=lax.Precision.HIGH)


def to_owner_rows(square_state, tall_state, count):
    rows = square_state.shape[1]
    group = count // 16
    if rows % group == 0:
        piece = rows // group
        pieces = jnp.concatenate(
            [
                square_state.reshape(8 * group, piece, D),
                tall_state.reshape(8 * group, piece, D),
            ],
            axis=0,
        ).astype(jnp.bfloat16)
        return lax.all_to_all(pieces, AXES, 0, 0, tiled=True).reshape(count * piece, D)
    square_all = lax.all_gather(square_state.astype(jnp.bfloat16), AXES, axis=1, tiled=True)
    tall_all = lax.all_gather(tall_state.astype(jnp.bfloat16), AXES, axis=1, tiled=True)
    joined = jnp.concatenate([square_all.reshape(-1, D), tall_all.reshape(-1, D)], axis=0)
    own = joined.shape[0] // count
    return lax.dynamic_slice_in_dim(joined, lax.axis_index(AXES) * own, own, axis=0)


def from_owner_rows(rows_out, count, square_rows, tall_rows):
    group = count // 16
    rows_out = rows_out.astype(jnp.bfloat16)
    if square_rows % group == 0:
        piece = square_rows // group
        back = lax.all_to_all(rows_out.reshape(count, piece, D), AXES, 0, 0, tiled=True)
        return (
            back[: 8 * group].reshape(8, square_rows, D),
            back[8 * group :].reshape(2, tall_rows, D),
        )
    joined = lax.all_gather(rows_out, AXES, axis=0, tiled=True)
    square_all = joined[: 8 * square_rows * count].reshape(8, square_rows * count, D)
    tall_all = joined[8 * square_rows * count :].reshape(2, tall_rows * count, D)
    index = lax.axis_index(AXES)
    return (
        lax.dynamic_slice_in_dim(square_all, index * square_rows, square_rows, axis=1),
        lax.dynamic_slice_in_dim(tall_all, index * tall_rows, tall_rows, axis=1),
    )


def orthogonal_rows(rows_in, kernels):
    gram = lax.dot_general(
        rows_in, rows_in, (((0,), (0,)), ((), ())), preferred_element_type=jnp.float32
    )
    if kernels:
        return sweeps(gram_sum(upper_blocks(gram), 2), rows_in)
    rows_in = rows_in.astype(jnp.float32)
    gram = lax.psum(gram, "row")
    is_tall = lax.axis_index("tall") >= 2
    gram = jnp.where(is_tall, lax.psum(jnp.where(is_tall, gram, 0.0), "square"), gram)
    eye = (jnp.arange(D)[:, None] == jnp.arange(D)[None, :]).astype(jnp.float32)
    scale = 1.0 / (jnp.sqrt(jnp.sum(gram * eye)) + FLOOR_EPSILON)
    gram = gram * (scale * scale)
    current = rows_in * scale

    for sweep in range(ITERS):
        poly = FIRST_TERM * eye + SECOND_TERM * gram + THIRD_TERM * matmul3(gram, gram)
        current = matmul3(current, poly)
        if sweep < ITERS - 1:
            gram = matmul3(matmul3(gram, poly), poly)
    return current


def local(
    inputs,
    memory,
    cotangent,
    lengths,
    memory_len,
    square_master,
    tall_master,
    square_momentum,
    tall_momentum,
    vectors,
    feed_vectors,
    head_scale,
    relative,
):
    count = lax.axis_size(AXES)
    kernels = count == 32
    index = lax.axis_index(AXES)
    if kernels:
        square_copy = gather_rows(square_master, 3, 3)
    else:
        square_copy = lax.all_gather(
            square_master.astype(jnp.bfloat16), AXES, axis=1, tiled=True
        )
    tall_copy = lax.all_gather(tall_master.astype(jnp.bfloat16), AXES, axis=1, tiled=True)
    width = inputs.shape[2]
    head_row = jnp.repeat(head_scale.astype(F32), width // head_scale.shape[0])[None]
    bias = jnp.roll(relative.astype(F32)[:, ::-1], 1, axis=1)
    flat_in, flat_memory = inputs.reshape(-1, width), memory.reshape(-1, width)
    left, q, k, v, p, o, h1, cq, ck, cv, pc, co, h2 = attention_forward(
        flat_in, flat_memory, memory_len, square_copy, vectors, head_row, bias
    )
    output, dh2, narrow, wide, late_slope, feed_slope = feed_both(
        h2, cotangent.reshape(-1, width), lengths, tall_copy, vectors, feed_vectors
    )

    tall_slope = jnp.einsum("btf,btd->bfd", wide, narrow, preferred_element_type=F32).astype(BF16)
    tall_slope, dh2 = lax.optimization_barrier((tall_slope, dh2))
    tall_sum = lax.psum_scatter(tall_slope, AXES, scatter_dimension=1, tiled=True).astype(F32)
    input_slope, memory_slope, right, far, early_slope, bias_slope = attention_backward(
        flat_in, dh2, square_copy, vectors, head_row, (q, k, v, p, o, h1, cq, ck, cv, pc, co)
    )
    square_slope = square_slopes(left, right, flat_memory, far)
    vector_slope = jnp.concatenate([early_slope[:14], late_slope], axis=0)
    scale_slope = jnp.sum(early_slope[17].reshape(head_scale.shape[0], -1), axis=1)
    bias_slope = jnp.roll(bias_slope, 1, axis=1)
    small = [
        jnp.sum(lengths).astype(jnp.float32).reshape(1),
        scale_slope.reshape(-1),
        bias_slope.reshape(-1),
        vector_slope.reshape(-1),
        feed_slope.reshape(-1),
    ]
    sizes = [piece.shape[0] for piece in small]
    starts = [sum(sizes[:i]) for i in range(len(sizes) + 1)]
    if kernels:
        lines = -(-starts[-1] // 1024) * 8
        small.append(jnp.zeros((lines * 128 - starts[-1],), jnp.float32))
        square_sum, summed = reduce_scatter(
            [square_slope], jnp.concatenate(small).reshape(lines, 128), 1
        )
        summed = summed.reshape(-1)
    else:
        square_sum = lax.psum_scatter(
            square_slope, AXES, scatter_dimension=1, tiled=True
        ).astype(jnp.float32)
        summed = lax.psum(jnp.concatenate(small), AXES)
    total, scale_sum, bias_sum, vector_sum, feed_sum = (
        summed[starts[i] : starts[i + 1]] for i in range(len(sizes))
    )
    factor = inputs.shape[0] * count / total[0]
    bias_sum = bias_sum.reshape(bias_slope.shape)
    width = vector_slope.shape[1] // count
    vector_sum = lax.dynamic_slice_in_dim(
        vector_sum.reshape(vector_slope.shape), index * width, width, axis=1
    )
    width = feed_slope.shape[1] // count
    feed_sum = lax.dynamic_slice_in_dim(
        feed_sum.reshape(feed_slope.shape), index * width, width, axis=1
    )
    square_state = MOMENTUM_DECAY * square_momentum + factor * square_sum
    tall_state = MOMENTUM_DECAY * tall_momentum + factor * tall_sum
    rows_out = orthogonal_rows(to_owner_rows(square_state, tall_state, count), kernels)
    square, tall = from_owner_rows(
        rows_out, count, square_state.shape[1], tall_state.shape[1]
    )
    square, tall = square.astype(jnp.float32), tall.astype(jnp.float32)
    square_weight = square_master * (1.0 - LEARN_RATE * WEIGHT_DECAY) - LEARN_RATE * square
    tall_weight = (
        tall_master * (1.0 - LEARN_RATE * WEIGHT_DECAY)
        - LEARN_RATE * max(1.0, FF / D) ** 0.5 * tall
    )
    return (
        output.reshape(inputs.shape),
        input_slope.reshape(inputs.shape),
        memory_slope.reshape(memory.shape),
        square_state,
        tall_state,
        square_weight,
        tall_weight,
        factor * vector_sum,
        factor * feed_sum,
        factor * scale_sum,
        factor * bias_sum,
    )


def solution(mesh):
    count = mesh.devices.size
    grouped = Mesh(mesh.devices.reshape(4, 4, count // 16), AXES)
    placed = (
        P(AXES, None, None),
        P(AXES, None, None),
        P(AXES, None, None),
        P(AXES),
        P(AXES),
        P(None, AXES, None),
        P(None, AXES, None),
        P(None, AXES, None),
        P(None, AXES, None),
        P(),
        P(),
        P(),
        P(),
    )
    return jax.shard_map(
        local,
        mesh=grouped,
        in_specs=placed,
        out_specs=(
            P(AXES, None, None),
            P(AXES, None, None),
            P(AXES, None, None),
            P(None, AXES, None),
            P(None, AXES, None),
            P(None, AXES, None),
            P(None, AXES, None),
            P(None, AXES),
            P(None, AXES),
            P(),
            P(),
        ),
        check_vma=False,
    )
```

```python
import functools

import jax
import jax.numpy as jnp
from jax import lax
from jax.experimental import pallas as pl
from jax.experimental.pallas import tpu as pltpu
from jax.sharding import Mesh, PartitionSpec as P

D = 768
FF = 3072
ITERS = 5


NORM_EPSILON = 1e-05
FLOOR_EPSILON = 1e-07
FIRST_TERM = 3.4445
SECOND_TERM = -4.775
THIRD_TERM = 2.0315
MOMENTUM_DECAY = 0.95
LEARN_RATE = 0.8
WEIGHT_DECAY = 0.01
NEGATIVE_LARGE = -1e30


F32, BF16 = jnp.float32, jnp.bfloat16
TOKENS = 256
SLOTS = 512
LANES = 128


def times(left, right):
    return jnp.dot(left, right, preferred_element_type=F32)


def times_back(left, right):
    return lax.dot_general(left, right, (((1,), (1,)), ((), ())), preferred_element_type=F32)


def times_down(left, right):
    return lax.dot_general(left, right, (((0,), (0,)), ((), ())), preferred_element_type=F32)


def down_to_keys(weights, values):
    if weights.shape[1] > values.shape[1]:
        return times_down(values, weights).astype(BF16).T
    return times_down(weights, values).astype(BF16)


def standard(values):
    center = values - jnp.mean(values, axis=-1, keepdims=True)
    scale = lax.rsqrt(jnp.mean(center * center, axis=-1, keepdims=True) + NORM_EPSILON)
    return center * scale, scale


def norm(values, gain, shift):
    return standard(values)[0] * gain + shift


def norm_back(values, slope, gain):
    hat, scale = standard(values)
    inner = slope * gain
    back = scale * (
        inner
        - jnp.mean(inner, axis=-1, keepdims=True)
        - hat * jnp.mean(inner * hat, axis=-1, keepdims=True)
    )
    return back, down(slope * hat), down(slope)


def down(values):
    return jnp.sum(values, axis=0, keepdims=True)


def spread_heads(scales):
    heads, width = scales.shape[1], scales.shape[1] * LANES // 2
    row = lax.broadcasted_iota(jnp.int32, (heads, width), 0)
    column = lax.broadcasted_iota(jnp.int32, (heads, width), 1)
    own = (column >= row * (LANES // 2)) & (column < (row + 1) * (LANES // 2))
    return times(scales, jnp.where(own, 1.0, 0.0).astype(BF16))


def head_masks():
    lane = lax.broadcasted_iota(jnp.int32, (1, LANES), 1)
    even = jnp.where(lane < LANES // 2, 1.0, 0.0)
    return even.astype(BF16), (1.0 - even).astype(BF16)


def stacked(pair, masks):
    return jnp.concatenate([pair * masks[0], pair * masks[1]], axis=0)


def side_by_side(rows):
    half = rows.shape[0] // 2
    return jnp.concatenate([rows[:half], rows[half:]], axis=1)


def soften(scores):
    weights = jnp.exp(scores - jnp.max(scores, axis=-1, keepdims=True))
    return (weights * (1.0 / jnp.sum(weights, axis=-1, keepdims=True))).astype(BF16)


def soften_back(weights, slope):
    weights = weights.astype(F32)
    product = weights * slope
    return (product - weights * jnp.sum(product, axis=-1, keepdims=True)).astype(BF16)


def attention_kernel(
    memory_len, x_in, memory, w, vec_in, scales, relative,
    left, q, k, v, p, o, h1, cq, ck, cv, pc, co, h2,
    bias, vec, hs,
):
    step = pl.program_id(0)
    masks = head_masks()

    @pl.when(step == 0)
    def _():
        vec[...] = vec_in[...].astype(F32)
        row = lax.broadcasted_iota(jnp.int32, (128, 128), 0)
        column = lax.broadcasted_iota(jnp.int32, (128, 128), 1)
        turned = jnp.where((row + column == 128) | (row + column == 0), 1.0, 0.0).astype(BF16)
        mirrored = times(relative[...], turned)
        hs[...] = spread_heads(scales[...])
        for head in range(12):
            line = jnp.broadcast_to(mirrored[head : head + 1], (128, 128))
            line = pltpu.roll(line, 0, 1, stride=1, stride_axis=0)
            bias[head // 2, (head % 2) * 128 : (head % 2) * 128 + 128] = jnp.where(
                row >= column, line, NEGATIVE_LARGE
            )

    x = x_in[...].astype(F32)
    left[0] = norm(x, vec[0:1], vec[1:2]).astype(BF16)
    q[...] = ((times(left[0], w[0]) + vec[2:3]) * 0.125).astype(BF16)
    k[...] = times(left[0], w[1]).astype(BF16)
    v[...] = (times(left[0], w[2]) + vec[3:4]).astype(BF16)
    items = TOKENS // 128

    @pl.loop(0, 6, unroll=True)
    def _(pair):
        lanes = pl.ds(pl.multiple_of(pair * LANES, LANES), LANES)
        for item in range(items):
            rows = slice(item * 128, item * 128 + 128)
            scores = times_back(stacked(q[rows, lanes], masks), k[rows, lanes]) + bias[pair]
            weights = soften(scores)
            p[item, pair] = weights
            o[rows, lanes] = times(side_by_side(weights), stacked(v[rows, lanes], masks))

    left[1] = norm(o[...] * hs[...], vec[5:6], vec[6:7]).astype(BF16)
    h1[...] = x + (times(left[1], w[3]) + vec[4:5])
    left[2] = norm(h1[...], vec[7:8], vec[8:9]).astype(BF16)
    cq[...] = ((times(left[2], w[4]) + vec[9:10]) * 0.125).astype(BF16)
    ck[...] = times(memory[...], w[5]).astype(BF16)
    cv[...] = (times(memory[...], w[6]) + vec[10:11]).astype(BF16)
    slots = SLOTS // items
    column = lax.broadcasted_iota(jnp.int32, (1, slots), 1)

    @pl.loop(0, 6, unroll=True)
    def _(pair):
        lanes = pl.ds(pl.multiple_of(pair * LANES, LANES), LANES)
        for item in range(items):
            rows = slice(item * 128, item * 128 + 128)
            keys = slice(item * slots, item * slots + slots)
            limit = memory_len[step * items + item]
            scores = times_back(stacked(cq[rows, lanes], masks), ck[keys, lanes])
            weights = soften(jnp.where(column < limit, scores, NEGATIVE_LARGE))
            pc[item, pair] = weights
            co[rows, lanes] = times(side_by_side(weights), stacked(cv[keys, lanes], masks))

    left[3] = norm(co[...], vec[12:13], vec[13:14]).astype(BF16)
    h2[...] = h1[...] + (times(left[3], w[7]) + vec[11:12])


def whole(shape):
    return pl.BlockSpec(shape, lambda *_: (0,) * len(shape), pipeline_mode=pl.Buffered(1))


def by_rows(rows, width):
    return pl.BlockSpec((rows, width), lambda i: (i, 0))


def by_blocks(blocks, rows, width):
    return pl.BlockSpec((blocks, rows, width), lambda i: (0, i, 0))


def by_items(items, *rest):
    return pl.BlockSpec((items,) + rest, lambda i: (i,) + (0,) * len(rest))


def attention_forward(inputs, memory, memory_len, square, vectors, head_row, bias):
    tokens, width = inputs.shape
    slots = memory.shape[0]
    steps = tokens // TOKENS
    items = TOKENS // 128
    shapes = [
        (BF16, "l"), (BF16, "t"), (BF16, "t"), (BF16, "t"), (BF16, "p"), (F32, "t"), (F32, "t"),
        (BF16, "t"), (BF16, "m"), (BF16, "m"), (BF16, "c"), (F32, "t"), (F32, "t"),
    ]
    full = {"l": (4, tokens, width), "t": (tokens, width), "m": (slots, width), "p": (steps * items, 6, 256, 128), "c": (steps * items, 6, 256, SLOTS // items)}
    spec = {
        "l": by_blocks(4, TOKENS, width),
        "t": by_rows(TOKENS, width), "m": by_rows(SLOTS, width),
        "p": by_items(items, 6, 256, 128), "c": by_items(items, 6, 256, SLOTS // items),
    }
    return pl.pallas_call(
        attention_kernel,
        grid=(steps,),
        out_shape=tuple(jax.ShapeDtypeStruct(full[kind], kept) for kept, kind in shapes),
        in_specs=[
            pl.BlockSpec(memory_space=pltpu.SMEM),
            spec["t"], spec["m"], whole(square.shape), whole(vectors.shape), whole(head_row.shape), whole(bias.shape),
        ],
        out_specs=tuple(spec[kind] for _, kind in shapes),
        scratch_shapes=[
            pltpu.VMEM((6, 256, 128), F32),
            pltpu.VMEM(vectors.shape, F32),
            pltpu.VMEM((1, width), F32),
        ],
        compiler_params=pltpu.CompilerParams(vmem_limit_bytes=60 << 20),
        cost_estimate=pl.CostEstimate(flops=14_000_000_000, bytes_accessed=60_000_000, transcendentals=5_000_000),
    )(memory_len, inputs, memory, square, vectors, head_row, bias)


ROOT_HALF = 0.7071067811865476
INVERSE_ROOT = 0.3989422804014327
CHUNK = 1024


def feed_kernel(
    lengths, h2_in, cot, tall, vec_in, feed_in,
    out, dh2, narrow, wide, dvec, dfeed,
    u, g, dr, total, vec, feed,
):
    step = pl.program_id(0)
    items = TOKENS // 128
    width = tall.shape[1]
    chunks = width // CHUNK

    @pl.when(step == 0)
    def _():
        vec[...] = vec_in[...].astype(F32)
        feed[...] = feed_in[...].astype(F32)
        dvec[...] = jnp.zeros_like(dvec)
        dfeed[...] = jnp.zeros_like(dfeed)

    h2 = h2_in[...]
    narrow[0] = norm(h2, vec[14:15], vec[15:16]).astype(BF16)

    def at(i):
        return pl.ds(pl.multiple_of(i * CHUNK, CHUNK), CHUNK)

    def first(i, total):
        some = at(i)
        inner = times_back(narrow[0], tall[0, some]) + feed[0:1, some]
        bell = 0.5 + 0.5 * lax.erf(inner * ROOT_HALF)
        active = inner * bell
        g[:, some] = active
        u[:, some] = bell + inner * (jnp.exp(-0.5 * inner * inner) * INVERSE_ROOT)
        return total + jnp.sum(active, axis=-1, keepdims=True)

    zero = jnp.zeros((TOKENS, 1), F32)
    mean = lax.fori_loop(0, chunks, first, zero, unroll=True) * (1.0 / width)

    def second(i, total):
        center = g[:, at(i)] - mean
        return total + jnp.sum(center * center, axis=-1, keepdims=True)

    spread = lax.fori_loop(0, chunks, second, zero, unroll=True) * (1.0 / width)
    scale = lax.rsqrt(spread + NORM_EPSILON)
    row = lax.broadcasted_iota(jnp.int32, (128, 1), 0)
    valid = jnp.concatenate(
        [jnp.where(row < lengths[step * items + item], 1.0, 0.0) for item in range(items)], axis=0
    )
    dy32 = cot[...].astype(F32) * valid
    narrow[1] = dy32.astype(BF16)
    total[...] = h2 + vec[16:17]

    def third(i, sums):
        some = at(i)
        hat = (g[:, some] - mean) * scale
        g[:, some] = hat
        gain = feed[1:2, some]
        active = (hat * gain + feed[2:3, some]).astype(BF16)
        wide[1, :, some] = active
        total[...] += times(active, tall[1, some])
        slope = times_back(narrow[1], tall[1, some])
        dfeed[1:2, some] += down(slope * hat)
        dfeed[2:3, some] += down(slope)
        inner = slope * gain
        dr[:, some] = inner
        return (
            sums[0] + jnp.sum(inner, axis=-1, keepdims=True),
            sums[1] + jnp.sum(inner * hat, axis=-1, keepdims=True),
        )

    one, two = lax.fori_loop(0, chunks, third, (zero, zero), unroll=True)
    out[...] = total[...].astype(BF16)
    one, two = one * (1.0 / width), two * (1.0 / width)
    dh2[...] = jnp.zeros_like(dh2)

    def fourth(i, carry):
        some = at(i)
        back = scale * (dr[:, some] - one - g[:, some] * two)
        slope = (back * u[:, some]).astype(BF16)
        wide[0, :, some] = slope
        dfeed[0:1, some] += down(slope.astype(F32))
        dh2[...] += times(slope, tall[0, some])
        return carry

    lax.fori_loop(0, chunks, fourth, 0, unroll=True)
    back, gain_sum, shift_sum = norm_back(h2, dh2[...], vec[14:15])
    dvec[0:1] += gain_sum
    dvec[1:2] += shift_sum
    dvec[2:3] += down(dy32)
    dh2[...] = dy32 + back


def feed_both(hidden, cotangent, lengths, tall, vectors, feed_vectors):
    tokens, width = hidden.shape
    wide = tall.shape[1]
    steps = tokens // TOKENS
    some = by_rows(TOKENS, width)
    return pl.pallas_call(
        feed_kernel,
        grid=(steps,),
        out_shape=(
            jax.ShapeDtypeStruct((tokens, width), BF16),
            jax.ShapeDtypeStruct((tokens, width), F32),
            jax.ShapeDtypeStruct((2, tokens, width), BF16),
            jax.ShapeDtypeStruct((2, tokens, wide), BF16),
            jax.ShapeDtypeStruct((3, width), F32),
            jax.ShapeDtypeStruct((3, wide), F32),
        ),
        in_specs=[
            pl.BlockSpec(memory_space=pltpu.SMEM),
            some, some, whole(tall.shape), whole(vectors.shape), whole(feed_vectors.shape),
        ],
        out_specs=(
            some, some, by_blocks(2, TOKENS, width), by_blocks(2, TOKENS, wide),
            pl.BlockSpec((3, width), lambda i: (0, 0)),
            pl.BlockSpec((3, wide), lambda i: (0, 0)),
        ),
        scratch_shapes=[pltpu.VMEM((TOKENS, wide), F32)] * 3
        + [
            pltpu.VMEM((TOKENS, width), F32),
            pltpu.VMEM(vectors.shape, F32),
            pltpu.VMEM(feed_vectors.shape, F32),
        ],
        compiler_params=pltpu.CompilerParams(vmem_limit_bytes=60 << 20),
        cost_estimate=pl.CostEstimate(flops=20_000_000_000, bytes_accessed=40_000_000, transcendentals=7_000_000),
    )(lengths, hidden, cotangent, tall, vectors, feed_vectors)


def attention_back_kernel(
    x_in, dh2, w, vec_in, scales,
    q, k, v, p, o, h1, cq, ck, cv, pc, co,
    dx, dmem, right, far, dvec, drel,
    do, dh1, dbias, vec, hs,
):
    step = pl.program_id(0)
    masks = head_masks()
    items = TOKENS // 128
    slots = SLOTS // items

    @pl.when(step == 0)
    def _():
        vec[...] = vec_in[...].astype(F32)
        hs[...] = spread_heads(scales[...])
        dvec[...] = jnp.zeros_like(dvec)
        dbias[...] = jnp.zeros_like(dbias)

    def note(row, value):
        dvec[row : row + 1] += value

    right[5] = dh2[...].astype(BF16)
    note(11, down(right[5].astype(F32)))
    back, gain_sum, shift_sum = norm_back(co[...], times_back(right[5], w[7]), vec[12:13])
    note(12, gain_sum)
    note(13, shift_sum)
    do[...] = back.astype(BF16)

    def through(pair, item, keys, query, key, value, weights, dquery, dkey, dvalue, with_bias):
        lanes = pl.ds(pl.multiple_of(pair * LANES, LANES), LANES)
        rows = slice(item * 128, item * 128 + 128)
        kept = weights[item, pair]
        grad = stacked(do[rows, lanes], masks)
        dvalue[keys, lanes] = down_to_keys(kept, grad)
        slope = soften_back(kept, times_back(grad, value[keys, lanes]))
        dquery[rows, lanes] = (
            times(side_by_side(slope), stacked(key[keys, lanes], masks)).astype(BF16) * 0.125
        ).astype(BF16)
        dkey[keys, lanes] = down_to_keys(slope, stacked(query[rows, lanes], masks))
        if with_bias:
            dbias[pair] += slope.astype(F32)

    @pl.loop(0, 6, unroll=True)
    def _(pair):
        for item in range(items):
            keys = slice(item * slots, item * slots + slots)
            through(pair, item, keys, cq, ck, cv, pc, right.at[4], far.at[0], far.at[1], False)

    note(9, down(right[4].astype(F32)))
    note(10, down(far[1].astype(F32)))
    dmem[...] = (times_back(far[0], w[5]) + times_back(far[1], w[6])).astype(BF16)
    back, gain_sum, shift_sum = norm_back(h1[...], times_back(right[4], w[4]), vec[7:8])
    note(7, gain_sum)
    note(8, shift_sum)
    dh1[...] = dh2[...] + back
    right[3] = dh1[...].astype(BF16)
    note(4, down(right[3].astype(F32)))
    back, gain_sum, shift_sum = norm_back(o[...] * hs[...], times_back(right[3], w[3]), vec[5:6])
    note(5, gain_sum)
    note(6, shift_sum)
    note(17, down(back * o[...]))
    do[...] = (back * hs[...]).astype(BF16)

    @pl.loop(0, 6, unroll=True)
    def _(pair):
        for item in range(items):
            rows = slice(item * 128, item * 128 + 128)
            through(pair, item, rows, q, k, v, p, right.at[0], right.at[1], right.at[2], True)

    note(2, down(right[0].astype(F32)))
    note(3, down(right[2].astype(F32)))
    slope = times_back(right[0], w[0]) + times_back(right[1], w[1]) + times_back(right[2], w[2])
    back, gain_sum, shift_sum = norm_back(x_in[...].astype(F32), slope, vec[0:1])
    note(0, gain_sum)
    note(1, shift_sum)
    dx[...] = (dh1[...] + back).astype(BF16)

    @pl.when(step == pl.num_programs(0) - 1)
    def _():
        row = lax.broadcasted_iota(jnp.int32, (128, 128), 0)
        column = lax.broadcasted_iota(jnp.int32, (128, 128), 1)
        mirror = jnp.where(row + column == 127, 1.0, 0.0).astype(BF16)
        for head in range(12):
            part = dbias[head // 2, (head % 2) * 128 : (head % 2) * 128 + 128]
            high = part.astype(BF16)
            rest = part - high.astype(F32)
            middle = rest.astype(BF16)
            low = (rest - middle.astype(F32)).astype(BF16)
            flipped = times(high, mirror) + times(middle, mirror) + times(low, mirror)
            drel[head : head + 1] = down(pltpu.roll(flipped, 0, 1, stride=1, stride_axis=0))


def attention_backward(inputs, dh2, square, vectors, head_row, kept):
    tokens, width = inputs.shape
    q, k, v, p, o, h1, cq, ck, cv, pc, co = kept
    steps = tokens // TOKENS
    items = TOKENS // 128
    slots = ck.shape[0]
    t, m = by_rows(TOKENS, width), by_rows(SLOTS, width)
    ps, cs = by_items(items, 6, 256, 128), by_items(items, 6, 256, SLOTS // items)
    token = jax.ShapeDtypeStruct((tokens, width), BF16)
    slot = jax.ShapeDtypeStruct((slots, width), BF16)
    return pl.pallas_call(
        attention_back_kernel,
        grid=(steps,),
        out_shape=(
            token, slot,
            jax.ShapeDtypeStruct((6, tokens, width), BF16),
            jax.ShapeDtypeStruct((2, slots, width), BF16),
            jax.ShapeDtypeStruct((18, width), F32),
            jax.ShapeDtypeStruct((12, 128), F32),
        ),
        in_specs=[
            t, t, whole(square.shape), whole(vectors.shape), whole(head_row.shape),
            t, t, t, ps, t, t, t, m, m, cs, t,
        ],
        out_specs=(
            t, m, by_blocks(6, TOKENS, width), by_blocks(2, SLOTS, width),
            pl.BlockSpec((18, width), lambda i: (0, 0)),
            pl.BlockSpec((12, 128), lambda i: (0, 0)),
        ),
        scratch_shapes=[
            pltpu.VMEM((TOKENS, width), BF16),
            pltpu.VMEM((TOKENS, width), F32),
            pltpu.VMEM((6, 256, 128), F32),
            pltpu.VMEM(vectors.shape, F32),
            pltpu.VMEM((1, width), F32),
        ],
        compiler_params=pltpu.CompilerParams(vmem_limit_bytes=60 << 20),
        cost_estimate=pl.CostEstimate(flops=16_000_000_000, bytes_accessed=60_000_000, transcendentals=0),
    )(inputs, dh2, square, vectors, head_row, q, k, v, p, o, h1, cq, ck, cv, pc, co)


def slope_kernel(left, right, memory, far, out):
    step = pl.program_id(0)
    width = out.shape[1]

    def product(from_left, from_right):
        @pl.loop(0, width // 256)
        def _(tile):
            some = pl.ds(pl.multiple_of(tile * 256, 256), 256)
            out[0, some] = times_down(from_left[:, some], from_right[...]).astype(BF16)

    @pl.when(step < 6)
    def _():
        product(left.at[0], right.at[0])

    @pl.when(step >= 6)
    def _():
        product(memory, far.at[0])


def square_slopes(left, right, memory, far):
    _, tokens, width = left.shape
    slots = memory.shape[0]
    return pl.pallas_call(
        slope_kernel,
        grid=(8,),
        out_shape=jax.ShapeDtypeStruct((8, width, width), BF16),
        in_specs=[
            pl.BlockSpec((1, tokens, width), lambda g: (jnp.clip(g - 2, 0, 3), 0, 0)),
            pl.BlockSpec((1, tokens, width), lambda g: (jnp.minimum(g, 5), 0, 0)),
            whole(memory.shape),
            pl.BlockSpec((1, slots, width), lambda g: (jnp.maximum(g - 6, 0), 0, 0)),
        ],
        out_specs=pl.BlockSpec(
            (1, width, width),
            lambda g: (jnp.where(g < 5, g, jnp.where(g == 5, 7, g - 1)), 0, 0),
        ),
        compiler_params=pltpu.CompilerParams(vmem_limit_bytes=60 << 20),
        cost_estimate=pl.CostEstimate(flops=12_000_000_000, bytes_accessed=30_000_000, transcendentals=0),
    )(left, right, memory, far)


AXES = ("tall", "square", "row")
MESH = pl.DeviceIdType.MESH


def place():
    z, plane, core = lax.axis_index("tall"), lax.axis_index("square"), lax.axis_index("row")
    return z, lax.div(plane, 2), lax.rem(plane, 2), core


def device(z, y, x, core):
    return (z, y * 2 + x, core)


def greet(partners):
    barrier = pltpu.get_barrier_semaphore()
    for partner in partners:
        pl.semaphore_signal(barrier, inc=1, device_id=partner, device_id_type=MESH)
    pl.semaphore_wait(barrier, len(partners))


def small_tiles(arrays):
    places, at = [], 0
    for array in arrays:
        for tile in range(array.shape[1] // 128):
            places.append((array, at, tile))
            at += -(-array.shape[0] // 8) * 8
    return places


def reduce_kernel(groups, has_small, *refs):
    n = len(groups)
    ins, refs = refs[:n], refs[n:]
    small_in, refs = refs[:has_small], refs[has_small:]
    outs, refs = refs[:n], refs[n:]
    small_outs, refs = refs[:has_small], refs[has_small:]
    z, y, x, core = place()
    other = 1 - core
    sibling = device(z, y, x, other)
    across = {"x": device(z, y, 1 - x, core), "y": device(z, 1 - y, x, core)}
    along = [device(lax.rem(z + k, 4), y, x, core) for k in (1, 2, 3)]
    greet([sibling, across["x"], across["y"]] + along)
    mine = core * 384
    theirs = other * 384

    if has_small:
        small, held, total, refs = refs[0], refs[1], refs[2], refs[3:]
        small_send, small_recv, refs = refs[0], refs[1], refs[2:]

        def small_copies(stage):
            source = small if stage == 0 else total.at[stage - 1]
            if stage < 3:
                partner = (sibling, across["x"], across["y"])[stage]
                return [
                    pltpu.make_async_remote_copy(
                        source, held.at[stage], small_send.at[stage], small_recv.at[stage],
                        device_id=partner, device_id_type=MESH,
                    )
                ]
            return [
                pltpu.make_async_remote_copy(
                    source, held.at[3 + z], small_send.at[3 + k], small_recv.at[3 + k],
                    device_id=along[k], device_id_type=MESH,
                )
                for k in range(3)
            ]

        small[...] = jnp.zeros_like(small)
        for source, at, tile in small_tiles(small_in):
            small[at : at + source.shape[0]] = source[:, tile * 128 : tile * 128 + 128]
        for copy in small_copies(0):
            copy.start()

        def small_step(stage):
            for copy in small_copies(stage):
                copy.wait_recv()
            if stage < 3:
                own = small if stage == 0 else total.at[stage - 1]
                total[stage] = own[...] + held[stage]
                if stage == 2:
                    held[3 + z] = total[2]
                for copy in small_copies(stage + 1):
                    copy.start()
            else:
                total[3] = ((held[3] + held[4]) + held[5]) + held[6]
                for target, at, tile in small_tiles(small_outs):
                    target[:, tile * 128 : tile * 128 + 128] = total[3, at : at + target.shape[0]]
    else:
        def small_step(stage):
            pass

    plans = []
    for g, (pieces, rows, width, parts) in enumerate(groups):
        r0, r1, r2, r3, f3, r4, send, recv = refs[8 * g : 8 * g + 8]
        plans.append((pieces, rows, width, parts, ins[g], outs[g], r0, r1, r2, r3, f3, r4, send, recv))

    def where(plan, order, i):
        pieces, parts, width = plan[0], plan[3], plan[2]
        j = i + order * (pieces // 2)
        return j, lax.div(j, parts), pl.multiple_of(lax.rem(j, parts) * width, 128)

    def copies(plan, stage, order, i):
        pieces, rows, width, parts, src, out, r0, r1, r2, r3, f3, r4, send, recv = plan
        j, matrix, column = where(plan, order, i)
        first = "xy"[order]

        def make(source, target, slot, partner):
            return pltpu.make_async_remote_copy(
                source, target, send.at[slot, j], recv.at[slot, j],
                device_id=partner, device_id_type=MESH,
            )

        if stage == 0:
            lanes = pl.ds(pl.multiple_of(theirs + column, 128), width)
            return [make(src.at[matrix, :, :, :, :, lanes], r0.at[j], 0, sibling)]
        if stage == 1:
            part = r0.at[j, :, :, 1 - x] if order == 0 else r0.at[j, :, 1 - y]
            return [make(part, r1.at[j], 1, across[first])]
        if stage == 2:
            part = r1.at[j, :, 1 - y] if order == 0 else r1.at[j, :, 1 - x]
            return [make(part, r2.at[j], 2, across["yx"[order]])]
        if stage == 3:
            return [
                make(r2.at[j, lax.rem(z + k + 1, 4)], r3.at[j, k], 3 + k, along[k])
                for k in range(3)
            ]
        share = rows // 2
        return [make(f3.at[j, pl.ds(pl.multiple_of(other * share, 8), share)], r4.at[j], 6, sibling)]

    f32 = jnp.float32

    def add(plan, stage, order, i):
        pieces, rows, width, parts, src, out, r0, r1, r2, r3, f3, r4, send, recv = plan
        j, matrix, column = where(plan, order, i)
        if stage == 0:
            lanes = pl.ds(pl.multiple_of(mine + column, 128), width)

            @pl.loop(0, 4)
            def _(a):
                r0[j, a] = (
                    r0[j, a].astype(f32) + src[matrix, a, :, :, :, lanes].astype(f32)
                ).astype(jnp.bfloat16)
        elif stage == 1:
            @pl.loop(0, 4)
            def _(a):
                own = r0[j, a, :, x] if order == 0 else r0[j, a, y]
                r1[j, a] = (r1[j, a].astype(f32) + own.astype(f32)).astype(jnp.bfloat16)
        elif stage == 2:
            @pl.loop(0, 4)
            def _(a):
                own = r1[j, a, y] if order == 0 else r1[j, a, x]
                r2[j, a] = (r2[j, a].astype(f32) + own.astype(f32)).astype(jnp.bfloat16)
        elif stage == 3:
            f3[j] = (r3[j, 0].astype(f32) + r3[j, 1].astype(f32)) + (
                r3[j, 2].astype(f32) + r2[j, z].astype(f32)
            )
        else:
            share = rows // 2
            lanes = pl.ds(pl.multiple_of(mine + column, 128), width)
            out[matrix, :, lanes] = f3[j, pl.ds(pl.multiple_of(core * share, 8), share)]
            lanes = pl.ds(pl.multiple_of(theirs + column, 128), width)
            out[matrix, :, lanes] = r4[j]

    def each(plan, body, turns):
        @pl.loop(0, turns)
        def _(i):
            for order in range(2):
                body(order, i)

    def start(plan, stage, turns):
        def body(order, i):
            for copy in copies(plan, stage, order, i):
                copy.start()

        each(plan, body, turns)

    def step(plan, stage, order, i):
        for copy in copies(plan, stage, order, i):
            copy.wait_recv()
        add(plan, stage, order, i)
        if stage < 4:
            for copy in copies(plan, stage + 1, order, i):
                copy.start()

    def finish(plan, stage):
        def body(order, i):
            for copy in copies(plan, stage, order, i):
                copy.wait_send()

        each(plan, body, plan[0] // 2)

    for plan in plans:
        start(plan, 0, 2)
    for plan in plans:
        turns = plan[0] // 2

        @pl.loop(0, turns + 4)
        def _(turn):
            @pl.when(turn < turns - 2)
            def _():
                for order in range(2):
                    for copy in copies(plan, 0, order, turn + 2):
                        copy.start()

            for stage in range(5):
                @pl.when((turn >= stage) & (turn < turns + stage))
                def _():
                    for order in range(2):
                        step(plan, stage, order, turn - stage)

            if plan is plans[0]:
                for stage in range(4):
                    @pl.when(turn == stage)
                    def _():
                        small_step(stage)

    for stage in range(5):
        for plan in plans:
            finish(plan, stage)
    if has_small:
        for stage in range(4):
            for copy in small_copies(stage):
                copy.wait_send()


def reduce_scatter(arrays, small, collective_id, split=1):
    groups, views, outs, scratch = [], [], [], []
    bf16, f32 = jnp.bfloat16, jnp.float32
    if small:
        last = small_tiles(small)[-1]
        lines = last[1] + -(-last[0].shape[0] // 8) * 8
        scratch += [
            pltpu.VMEM((lines, 128), f32),
            pltpu.VMEM((7, lines, 128), f32),
            pltpu.VMEM((4, lines, 128), f32),
            pltpu.SemaphoreType.DMA((6,)),
            pltpu.SemaphoreType.DMA((6,)),
        ]
    for array in arrays:
        matrices, height, width_all = array.shape
        rows = height // 16
        parts = 3 if matrices == 2 else split
        pieces, width = matrices * parts, 384 // parts
        groups.append((pieces, rows, width, parts))
        views.append(array.reshape(matrices, 4, 2, 2, rows, width_all))
        outs.append(jax.ShapeDtypeStruct((matrices, rows // 2, width_all), f32))
        scratch += [
            pltpu.VMEM((pieces, 4, 2, 2, rows, width), bf16),
            pltpu.VMEM((pieces, 4, 2, rows, width), bf16),
            pltpu.VMEM((pieces, 4, rows, width), bf16),
            pltpu.VMEM((pieces, 3, rows, width), bf16),
            pltpu.VMEM((pieces, rows, width), f32),
            pltpu.VMEM((pieces, rows // 2, width), f32),
            pltpu.SemaphoreType.DMA((7, pieces)),
            pltpu.SemaphoreType.DMA((7, pieces)),
        ]
    for array in small:
        views.append(array)
        outs.append(jax.ShapeDtypeStruct(array.shape, f32))
    vmem = pl.BlockSpec(memory_space=pltpu.VMEM)
    return pl.pallas_call(
        functools.partial(reduce_kernel, tuple(groups), len(small)),
        out_shape=tuple(outs),
        in_specs=[vmem] * len(views),
        out_specs=tuple([vmem] * len(outs)),
        scratch_shapes=scratch,
        compiler_params=pltpu.CompilerParams(
            collective_id=collective_id, has_side_effects=True, vmem_limit_bytes=60 << 20
        ),
    )(*views)


def gather_kernel(split, own, full, theirs, send, recv):
    z, y, x, core = place()
    other = 1 - core
    sibling = device(z, y, x, other)
    across = {"x": device(z, y, 1 - x, core), "y": device(z, 1 - y, x, core)}
    along = [device(lax.rem(z + k, 4), y, x, core) for k in (1, 2, 3)]
    greet([sibling, across["x"], across["y"]] + along)
    matrices, share, width = own.shape
    half = width // 2
    pieces, thin = matrices * split, half // split

    def spot(j):
        column = lax.rem(j, split) * thin
        return (
            lax.div(j, split),
            pl.ds(pl.multiple_of(core * half + column, 128), thin),
            pl.ds(pl.multiple_of(other * half + column, 128), thin),
        )

    def make(source, target, slot, j, partner):
        return pltpu.make_async_remote_copy(
            source, target, send.at[slot, j], recv.at[slot, j], device_id=partner, device_id_type=MESH
        )

    def copies(stage, order, i):
        j = i + order * (pieces // 2)
        m, mine, rest = spot(j)
        first = "yx"[order]
        if stage == 0:
            return [make(own.at[m, :, rest], theirs.at[j], 0, j, sibling)]
        if stage == 1:
            part = full.at[m, z, y, x, :, mine]
            return [make(part, part, 1 + k, j, along[k]) for k in range(3)]
        if stage == 2:
            part = full.at[m, :, y, x, :, mine]
            return [make(part, part, 4, j, across[first])]
        if stage == 3:
            part = full.at[m, :, :, x, :, mine] if order == 0 else full.at[m, :, y, :, :, mine]
            return [make(part, part, 5, j, across["xy"[order]])]
        part = full.at[m, :, :, :, :, mine]
        return [make(part, part, 6, j, sibling)]

    def each(body):
        @pl.loop(0, pieces // 2)
        def _(i):
            for order in range(2):
                body(order, i)

    def start(stage):
        def body(order, i):
            for copy in copies(stage, order, i):
                copy.start()

        each(body)

    def step(stage, order, i):
        for copy in copies(stage, order, i):
            copy.wait_recv()
        if stage == 0:
            j = i + order * (pieces // 2)
            m, mine, _ = spot(j)

            @pl.when(core == 0)
            def _():
                full[m, z, y, x, :, mine] = jnp.concatenate(
                    [own[m, :, mine], theirs[j]], axis=0
                ).astype(jnp.bfloat16)

            @pl.when(core == 1)
            def _():
                full[m, z, y, x, :, mine] = jnp.concatenate(
                    [theirs[j], own[m, :, mine]], axis=0
                ).astype(jnp.bfloat16)
        if stage < 4:
            for copy in copies(stage + 1, order, i):
                copy.start()

    def finish(stage):
        def body(order, i):
            for copy in copies(stage, order, i):
                copy.wait_send()

        each(body)

    start(0)
    turns = pieces // 2

    @pl.loop(0, turns + 4)
    def _(turn):
        for stage in range(5):
            @pl.when((turn >= stage) & (turn < turns + stage))
            def _():
                for order in range(2):
                    step(stage, order, turn - stage)

    for stage in range(5):
        finish(stage)


def gather_rows(own, collective_id, split=1):
    matrices, share, width = own.shape
    pieces = matrices * split
    vmem = pl.BlockSpec(memory_space=pltpu.VMEM)
    full = pl.pallas_call(
        functools.partial(gather_kernel, split),
        out_shape=jax.ShapeDtypeStruct((matrices, 4, 2, 2, 2 * share, width), jnp.bfloat16),
        in_specs=[vmem],
        out_specs=vmem,
        scratch_shapes=[
            pltpu.VMEM((pieces, share, width // 2 // split), jnp.float32),
            pltpu.SemaphoreType.DMA((7, pieces)),
            pltpu.SemaphoreType.DMA((7, pieces)),
        ],
        compiler_params=pltpu.CompilerParams(
            collective_id=collective_id, has_side_effects=True, vmem_limit_bytes=32 << 20
        ),
    )(own)
    return full.reshape(matrices, 32 * share, width)


def gram_kernel(gram, out, other_sum, half_a, half_b, final, send, recv):
    z, y, x, core = place()
    sibling = device(z, y, x, 1 - core)
    x_side, y_side = device(z, y, 1 - x, core), device(z, 1 - y, x, core)
    greet([sibling, x_side, y_side])
    side = gram.shape[0] // 2
    rows = pl.ds(pl.multiple_of(core * side, 8), side)
    rest = pl.ds(pl.multiple_of((1 - core) * side, 8), side)

    def send_to(source, target, slot, partner):
        return pltpu.make_async_remote_copy(
            source, target, send.at[slot], recv.at[slot], device_id=partner, device_id_type=MESH
        )

    first = send_to(gram.at[rest], other_sum.at[rest], 0, sibling)
    second = send_to(gram.at[rows], other_sum.at[rows], 1, sibling)
    first.start()
    second.start()
    mine = send_to(gram.at[rows], other_sum.at[rows], 0, sibling)
    mine.wait_recv()
    out[rows] = gram[rows] + other_sum[rows]
    theirs = send_to(gram.at[rest], other_sum.at[rest], 1, sibling)
    theirs.wait_recv()

    @pl.when(z < 2)
    def _():
        out[rest] = gram[rest] + other_sum[rest]

    @pl.when(z >= 2)
    def _():
        def pair(one, two):
            step = send_to(out.at[rows], half_a, 2, one)
            step.start()
            step.wait_recv()
            step.wait_send()
            half_b[...] = out[rows] + half_a[...]
            step = send_to(half_b, final, 3, two)
            step.start()
            step.wait_recv()
            out[rows] = half_b[...] + final[...]
            step.wait_send()

        @pl.when(core == 0)
        def _():
            pair(x_side, y_side)

        @pl.when(core == 1)
        def _():
            pair(y_side, x_side)

        last = send_to(out.at[rows], out.at[rows], 4, sibling)
        last.start()
        arrive = send_to(out.at[rest], out.at[rest], 4, sibling)
        arrive.wait_recv()
        last.wait_send()

    first.wait_send()
    second.wait_send()


def gram_sum(gram, collective_id):
    f32 = jnp.float32
    side = gram.shape[0] // 2
    vmem = pl.BlockSpec(memory_space=pltpu.VMEM)
    return pl.pallas_call(
        gram_kernel,
        out_shape=jax.ShapeDtypeStruct(gram.shape, f32),
        in_specs=[vmem],
        out_specs=vmem,
        scratch_shapes=[
            pltpu.VMEM(gram.shape, f32),
            pltpu.VMEM((side, gram.shape[1]), f32),
            pltpu.VMEM((side, gram.shape[1]), f32),
            pltpu.VMEM((side, gram.shape[1]), f32),
            pltpu.SemaphoreType.DMA((5,)),
            pltpu.SemaphoreType.DMA((5,)),
        ],
        compiler_params=pltpu.CompilerParams(
            collective_id=collective_id, has_side_effects=True, vmem_limit_bytes=32 << 20
        ),
    )(gram)


SIDE = 256


def sweep_kernel(packed, rows, out, gram, held, now, poly, step):
    blocks = gram.shape[0] // SIDE
    width = blocks * SIDE

    def put(target, a, values):
        for b in range(a, blocks):
            block = values[:, (b - a) * SIDE : (b - a) * SIDE + SIDE]
            for i, j, piece in ((a, b, block),) if a == b else ((a, b, block), (b, a, block.T)):
                columns = slice(j * SIDE, j * SIDE + SIDE)
                top = piece.astype(BF16)
                target[i * SIDE : i * SIDE + SIDE, columns] = top
                target[width + i * SIDE : width + i * SIDE + SIDE, columns] = (
                    piece - top.astype(F32)
                ).astype(BF16)
                target[2 * width + i * SIDE : 2 * width + i * SIDE + SIDE, columns] = top

    def exact(left, a, right):
        high = left[a * SIDE : a * SIDE + SIDE]
        low = left[width + a * SIDE : width + a * SIDE + SIDE]
        return times(jnp.concatenate([high, high, low], axis=1), right[:, a * SIDE :])

    index, trace = 0, jnp.zeros((1, 1), F32)
    row = lax.broadcasted_iota(jnp.int32, (SIDE, SIDE), 0)
    column = lax.broadcasted_iota(jnp.int32, (SIDE, SIDE), 1)
    unit = jnp.where(row == column, 1.0, 0.0)
    for a in range(blocks):
        for b in range(a, blocks):
            block = packed[index * SIDE : index * SIDE + SIDE]
            gram[a * SIDE : a * SIDE + SIDE, b * SIDE : b * SIDE + SIDE] = block
            if a == b:
                trace = trace + jnp.sum(
                    jnp.sum(block * unit, axis=1, keepdims=True), axis=0, keepdims=True
                )
            else:
                gram[b * SIDE : b * SIDE + SIDE, a * SIDE : a * SIDE + SIDE] = block.T
            index += 1
    scale = 1.0 / (jnp.sqrt(trace) + FLOOR_EPSILON)

    for a in range(blocks):
        put(now, a, gram[a * SIDE : a * SIDE + SIDE, a * SIDE :] * (scale * scale))
    count = rows.shape[0]

    def keep(some, rest, values):
        top = values.astype(BF16)
        held[some] = top
        held[rest] = (values - top.astype(F32)).astype(BF16)

    keep(slice(0, count), slice(count, 2 * count), rows[...].astype(F32) * scale)

    @pl.loop(0, ITERS)
    def _(sweep):
        for a in range(blocks):
            row = lax.broadcasted_iota(jnp.int32, (SIDE, width - a * SIDE), 0)
            column = lax.broadcasted_iota(jnp.int32, (SIDE, width - a * SIDE), 1)
            lines = slice(a * SIDE, a * SIDE + SIDE)
            below = slice(width + a * SIDE, width + a * SIDE + SIDE)
            values = exact(now, a, now) * THIRD_TERM + SECOND_TERM * (
                now[lines, a * SIDE :].astype(F32) + now[below, a * SIDE :].astype(F32)
            )
            put(poly, a, jnp.where(row == column, values + FIRST_TERM, values))

        @pl.loop(0, count // 128)
        def _(a):
            some = pl.ds(pl.multiple_of(a * 128, 128), 128)
            rest = pl.ds(pl.multiple_of(a * 128 + count, 128), 128)
            high, low = held[some], held[rest]
            keep(some, rest, times(jnp.concatenate([high, high, low], axis=1), poly[...]))

        @pl.when(sweep < ITERS - 1)
        def _():
            for a in range(blocks):
                put(step, a, exact(now, a, poly))
            for a in range(blocks):
                put(now, a, exact(step, a, poly))

    out[...] = held[0:count]


def sweeps(packed, rows):
    width = rows.shape[1]
    vmem = pl.BlockSpec(memory_space=pltpu.VMEM)
    part = pltpu.VMEM((3 * width, width), BF16)
    return pl.pallas_call(
        sweep_kernel,
        out_shape=jax.ShapeDtypeStruct(rows.shape, BF16),
        in_specs=[vmem, vmem],
        out_specs=vmem,
        scratch_shapes=[
            pltpu.VMEM((width, width), F32),
            pltpu.VMEM((2 * rows.shape[0], width), BF16),
        ]
        + [part] * 3,
        compiler_params=pltpu.CompilerParams(vmem_limit_bytes=48 << 20),
        cost_estimate=pl.CostEstimate(flops=40_000_000_000, bytes_accessed=5_000_000, transcendentals=0),
    )(packed, rows)


def upper_blocks(gram):
    blocks = gram.shape[0] // SIDE
    return jnp.concatenate(
        [
            gram[a * SIDE : a * SIDE + SIDE, b * SIDE : b * SIDE + SIDE]
            for a in range(blocks)
            for b in range(a, blocks)
        ],
        axis=0,
    )


def matmul3(left, right):
    return jnp.matmul(left, right, precision=lax.Precision.HIGH)


def to_owner_rows(square_state, tall_state, count):
    rows = square_state.shape[1]
    group = count // 16
    if rows % group == 0:
        piece = rows // group
        pieces = jnp.concatenate(
            [
                square_state.reshape(8 * group, piece, D),
                tall_state.reshape(8 * group, piece, D),
            ],
            axis=0,
        ).astype(jnp.bfloat16)
        return lax.all_to_all(pieces, AXES, 0, 0, tiled=True).reshape(count * piece, D)
    square_all = lax.all_gather(square_state.astype(jnp.bfloat16), AXES, axis=1, tiled=True)
    tall_all = lax.all_gather(tall_state.astype(jnp.bfloat16), AXES, axis=1, tiled=True)
    joined = jnp.concatenate([square_all.reshape(-1, D), tall_all.reshape(-1, D)], axis=0)
    own = joined.shape[0] // count
    return lax.dynamic_slice_in_dim(joined, lax.axis_index(AXES) * own, own, axis=0)


def from_owner_rows(rows_out, count, square_rows, tall_rows):
    group = count // 16
    rows_out = rows_out.astype(jnp.bfloat16)
    if square_rows % group == 0:
        piece = square_rows // group
        back = lax.all_to_all(rows_out.reshape(count, piece, D), AXES, 0, 0, tiled=True)
        return (
            back[: 8 * group].reshape(8, square_rows, D),
            back[8 * group :].reshape(2, tall_rows, D),
        )
    joined = lax.all_gather(rows_out, AXES, axis=0, tiled=True)
    square_all = joined[: 8 * square_rows * count].reshape(8, square_rows * count, D)
    tall_all = joined[8 * square_rows * count :].reshape(2, tall_rows * count, D)
    index = lax.axis_index(AXES)
    return (
        lax.dynamic_slice_in_dim(square_all, index * square_rows, square_rows, axis=1),
        lax.dynamic_slice_in_dim(tall_all, index * tall_rows, tall_rows, axis=1),
    )


def orthogonal_rows(rows_in, kernels):
    gram = lax.dot_general(
        rows_in, rows_in, (((0,), (0,)), ((), ())), preferred_element_type=jnp.float32
    )
    if kernels:
        return sweeps(gram_sum(upper_blocks(gram), 2), rows_in)
    rows_in = rows_in.astype(jnp.float32)
    gram = lax.psum(gram, "row")
    is_tall = lax.axis_index("tall") >= 2
    gram = jnp.where(is_tall, lax.psum(jnp.where(is_tall, gram, 0.0), "square"), gram)
    eye = (jnp.arange(D)[:, None] == jnp.arange(D)[None, :]).astype(jnp.float32)
    scale = 1.0 / (jnp.sqrt(jnp.sum(gram * eye)) + FLOOR_EPSILON)
    gram = gram * (scale * scale)
    current = rows_in * scale

    for sweep in range(ITERS):
        poly = FIRST_TERM * eye + SECOND_TERM * gram + THIRD_TERM * matmul3(gram, gram)
        current = matmul3(current, poly)
        if sweep < ITERS - 1:
            gram = matmul3(matmul3(gram, poly), poly)
    return current


def local(
    inputs,
    memory,
    cotangent,
    lengths,
    memory_len,
    square_master,
    tall_master,
    square_momentum,
    tall_momentum,
    vectors,
    feed_vectors,
    head_scale,
    relative,
):
    count = lax.axis_size(AXES)
    kernels = count == 32
    index = lax.axis_index(AXES)
    if kernels:
        square_copy = gather_rows(square_master, 3, 3)
    else:
        square_copy = lax.all_gather(
            square_master.astype(jnp.bfloat16), AXES, axis=1, tiled=True
        )
    tall_copy = lax.all_gather(tall_master.astype(jnp.bfloat16), AXES, axis=1, tiled=True)
    width = inputs.shape[2]
    head_row = head_scale[None]
    flat_in, flat_memory = inputs.reshape(-1, width), memory.reshape(-1, width)
    left, q, k, v, p, o, h1, cq, ck, cv, pc, co, h2 = attention_forward(
        flat_in, flat_memory, memory_len, square_copy, vectors, head_row, relative
    )
    output, dh2, narrow, wide, late_slope, feed_slope = feed_both(
        h2, cotangent.reshape(-1, width), lengths, tall_copy, vectors, feed_vectors
    )

    tall_slope = jnp.einsum("btf,btd->bfd", wide, narrow, preferred_element_type=F32).astype(BF16)
    tall_slope, dh2 = lax.optimization_barrier((tall_slope, dh2))
    tall_sum = lax.psum_scatter(tall_slope, AXES, scatter_dimension=1, tiled=True).astype(F32)
    input_slope, memory_slope, right, far, early_slope, bias_slope = attention_backward(
        flat_in, dh2, square_copy, vectors, head_row, (q, k, v, p, o, h1, cq, ck, cv, pc, co)
    )
    square_slope = square_slopes(left, right, flat_memory, far)
    small = [
        jnp.full((8, 128), jnp.sum(lengths).astype(F32)),
        early_slope,
        late_slope,
        feed_slope,
        bias_slope,
    ]
    if kernels:
        square_sum, *small = reduce_scatter([square_slope], small, 1)
    else:
        square_sum = lax.psum_scatter(
            square_slope, AXES, scatter_dimension=1, tiled=True
        ).astype(jnp.float32)
        small = lax.psum(small, AXES)
    total, early_sum, late_sum, feed_sum, bias_sum = small
    total = total[0, :1]
    vector_sum = jnp.concatenate([early_sum[:14], late_sum], axis=0)
    scale_sum = jnp.sum(early_sum[17].reshape(head_scale.shape[0], -1), axis=1)
    bias_sum = jnp.roll(bias_sum, 1, axis=1)
    factor = inputs.shape[0] * count / total[0]
    width = vector_sum.shape[1] // count
    vector_sum = lax.dynamic_slice_in_dim(
        vector_sum, index * width, width, axis=1
    )
    width = feed_slope.shape[1] // count
    feed_sum = lax.dynamic_slice_in_dim(
        feed_sum, index * width, width, axis=1
    )
    square_state = MOMENTUM_DECAY * square_momentum + factor * square_sum
    tall_state = MOMENTUM_DECAY * tall_momentum + factor * tall_sum
    rows_out = orthogonal_rows(to_owner_rows(square_state, tall_state, count), kernels)
    square, tall = from_owner_rows(
        rows_out, count, square_state.shape[1], tall_state.shape[1]
    )
    square, tall = square.astype(jnp.float32), tall.astype(jnp.float32)
    square_weight = square_master * (1.0 - LEARN_RATE * WEIGHT_DECAY) - LEARN_RATE * square
    tall_weight = (
        tall_master * (1.0 - LEARN_RATE * WEIGHT_DECAY)
        - LEARN_RATE * max(1.0, FF / D) ** 0.5 * tall
    )
    return (
        output.reshape(inputs.shape),
        input_slope.reshape(inputs.shape),
        memory_slope.reshape(memory.shape),
        square_state,
        tall_state,
        square_weight,
        tall_weight,
        factor * vector_sum,
        factor * feed_sum,
        factor * scale_sum,
        factor * bias_sum,
    )


def solution(mesh):
    count = mesh.devices.size
    grouped = Mesh(mesh.devices.reshape(4, 4, count // 16), AXES)
    placed = (
        P(AXES, None, None),
        P(AXES, None, None),
        P(AXES, None, None),
        P(AXES),
        P(AXES),
        P(None, AXES, None),
        P(None, AXES, None),
        P(None, AXES, None),
        P(None, AXES, None),
        P(),
        P(),
        P(),
        P(),
    )
    return jax.shard_map(
        local,
        mesh=grouped,
        in_specs=placed,
        out_specs=(
            P(AXES, None, None),
            P(AXES, None, None),
            P(AXES, None, None),
            P(None, AXES, None),
            P(None, AXES, None),
            P(None, AXES, None),
            P(None, AXES, None),
            P(None, AXES),
            P(None, AXES),
            P(),
            P(),
        ),
        check_vma=False,
    )
```

```python
import functools

import jax
import jax.numpy as jnp
from jax import lax
from jax.experimental import pallas as pl
from jax.experimental.pallas import tpu as pltpu
from jax.sharding import Mesh, PartitionSpec as P

D = 768
FF = 3072
ITERS = 5


NORM_EPSILON = 1e-05
FLOOR_EPSILON = 1e-07
FIRST_TERM = 3.4445
SECOND_TERM = -4.775
THIRD_TERM = 2.0315
MOMENTUM_DECAY = 0.95
LEARN_RATE = 0.8
WEIGHT_DECAY = 0.01
NEGATIVE_LARGE = -1e30


F32, BF16 = jnp.float32, jnp.bfloat16
TOKENS = 256
SLOTS = 512
LANES = 128


def times(left, right):
    return jnp.dot(left, right, preferred_element_type=F32)


def times_back(left, right):
    return lax.dot_general(left, right, (((1,), (1,)), ((), ())), preferred_element_type=F32)


def times_down(left, right):
    return lax.dot_general(left, right, (((0,), (0,)), ((), ())), preferred_element_type=F32)


def down_to_keys(weights, values):
    if weights.shape[1] > values.shape[1]:
        return times_down(values, weights).astype(BF16).T
    return times_down(weights, values).astype(BF16)


def standard(values):
    center = values - jnp.mean(values, axis=-1, keepdims=True)
    scale = lax.rsqrt(jnp.mean(center * center, axis=-1, keepdims=True) + NORM_EPSILON)
    return center * scale, scale


def norm(values, gain, shift):
    return standard(values)[0] * gain + shift


def norm_back(values, slope, gain):
    hat, scale = standard(values)
    inner = slope * gain
    back = scale * (
        inner
        - jnp.mean(inner, axis=-1, keepdims=True)
        - hat * jnp.mean(inner * hat, axis=-1, keepdims=True)
    )
    return back, down(slope * hat), down(slope)


def down(values):
    return jnp.sum(values, axis=0, keepdims=True)


def spread_heads(scales):
    heads, width = scales.shape[1], scales.shape[1] * LANES // 2
    row = lax.broadcasted_iota(jnp.int32, (heads, width), 0)
    column = lax.broadcasted_iota(jnp.int32, (heads, width), 1)
    own = (column >= row * (LANES // 2)) & (column < (row + 1) * (LANES // 2))
    return times(scales, jnp.where(own, 1.0, 0.0).astype(BF16))


def head_masks():
    lane = lax.broadcasted_iota(jnp.int32, (1, LANES), 1)
    even = jnp.where(lane < LANES // 2, 1.0, 0.0)
    return even.astype(BF16), (1.0 - even).astype(BF16)


def stacked(pair, masks):
    return jnp.concatenate([pair * masks[0], pair * masks[1]], axis=0)


def side_by_side(rows):
    half = rows.shape[0] // 2
    return jnp.concatenate([rows[:half], rows[half:]], axis=1)


def soften(scores):
    weights = jnp.exp(scores - jnp.max(scores, axis=-1, keepdims=True))
    return (weights * (1.0 / jnp.sum(weights, axis=-1, keepdims=True))).astype(BF16)


def soften_back(weights, slope):
    weights = weights.astype(F32)
    product = weights * slope
    return (product - weights * jnp.sum(product, axis=-1, keepdims=True)).astype(BF16)


def attention_kernel(
    memory_len, x_in, memory, w, vec_in, scales, relative,
    left, q, k, v, p, o, h1, cq, ck, cv, pc, co, h2,
    bias, vec, hs,
):
    step = pl.program_id(0)
    masks = head_masks()

    @pl.when(step == 0)
    def _():
        vec[...] = vec_in[...].astype(F32)
        row = lax.broadcasted_iota(jnp.int32, (128, 128), 0)
        column = lax.broadcasted_iota(jnp.int32, (128, 128), 1)
        turned = jnp.where((row + column == 128) | (row + column == 0), 1.0, 0.0).astype(BF16)
        mirrored = times(relative[...], turned)
        hs[...] = spread_heads(scales[...])
        for head in range(12):
            line = jnp.broadcast_to(mirrored[head : head + 1], (128, 128))
            line = pltpu.roll(line, 0, 1, stride=1, stride_axis=0)
            bias[head // 2, (head % 2) * 128 : (head % 2) * 128 + 128] = jnp.where(
                row >= column, line, NEGATIVE_LARGE
            )

    x = x_in[...].astype(F32)
    left[0] = norm(x, vec[0:1], vec[1:2]).astype(BF16)
    q[...] = ((times(left[0], w[0]) + vec[2:3]) * 0.125).astype(BF16)
    k[...] = times(left[0], w[1]).astype(BF16)
    v[...] = (times(left[0], w[2]) + vec[3:4]).astype(BF16)
    items = TOKENS // 128

    @pl.loop(0, 6, unroll=True)
    def _(pair):
        lanes = pl.ds(pl.multiple_of(pair * LANES, LANES), LANES)
        for item in range(items):
            rows = slice(item * 128, item * 128 + 128)
            scores = times_back(stacked(q[rows, lanes], masks), k[rows, lanes]) + bias[pair]
            weights = soften(scores)
            p[item, pair] = weights
            o[rows, lanes] = times(side_by_side(weights), stacked(v[rows, lanes], masks))

    left[1] = norm(o[...] * hs[...], vec[5:6], vec[6:7]).astype(BF16)
    h1[...] = x + (times(left[1], w[3]) + vec[4:5])
    left[2] = norm(h1[...], vec[7:8], vec[8:9]).astype(BF16)
    cq[...] = ((times(left[2], w[4]) + vec[9:10]) * 0.125).astype(BF16)
    ck[...] = times(memory[...], w[5]).astype(BF16)
    cv[...] = (times(memory[...], w[6]) + vec[10:11]).astype(BF16)
    slots = SLOTS // items
    column = lax.broadcasted_iota(jnp.int32, (1, slots), 1)

    @pl.loop(0, 6, unroll=True)
    def _(pair):
        lanes = pl.ds(pl.multiple_of(pair * LANES, LANES), LANES)
        for item in range(items):
            rows = slice(item * 128, item * 128 + 128)
            keys = slice(item * slots, item * slots + slots)
            limit = memory_len[step * items + item]
            scores = times_back(stacked(cq[rows, lanes], masks), ck[keys, lanes])
            weights = soften(jnp.where(column < limit, scores, NEGATIVE_LARGE))
            pc[item, pair] = weights
            co[rows, lanes] = times(side_by_side(weights), stacked(cv[keys, lanes], masks))

    left[3] = norm(co[...], vec[12:13], vec[13:14]).astype(BF16)
    h2[...] = h1[...] + (times(left[3], w[7]) + vec[11:12])


def whole(shape):
    return pl.BlockSpec(shape, lambda *_: (0,) * len(shape), pipeline_mode=pl.Buffered(1))


def by_rows(rows, width):
    return pl.BlockSpec((rows, width), lambda i: (i, 0))


def by_blocks(blocks, rows, width):
    return pl.BlockSpec((blocks, rows, width), lambda i: (0, i, 0))


def by_items(items, *rest):
    return pl.BlockSpec((items,) + rest, lambda i: (i,) + (0,) * len(rest))


def attention_forward(inputs, memory, memory_len, square, vectors, head_row, bias):
    tokens, width = inputs.shape
    slots = memory.shape[0]
    steps = tokens // TOKENS
    items = TOKENS // 128
    shapes = [
        (BF16, "l"), (BF16, "t"), (BF16, "t"), (BF16, "t"), (BF16, "p"), (F32, "t"), (F32, "t"),
        (BF16, "t"), (BF16, "m"), (BF16, "m"), (BF16, "c"), (F32, "t"), (F32, "t"),
    ]
    full = {"l": (4, tokens, width), "t": (tokens, width), "m": (slots, width), "p": (steps * items, 6, 256, 128), "c": (steps * items, 6, 256, SLOTS // items)}
    spec = {
        "l": by_blocks(4, TOKENS, width),
        "t": by_rows(TOKENS, width), "m": by_rows(SLOTS, width),
        "p": by_items(items, 6, 256, 128), "c": by_items(items, 6, 256, SLOTS // items),
    }
    return pl.pallas_call(
        attention_kernel,
        grid=(steps,),
        out_shape=tuple(jax.ShapeDtypeStruct(full[kind], kept) for kept, kind in shapes),
        in_specs=[
            pl.BlockSpec(memory_space=pltpu.SMEM),
            spec["t"], spec["m"], whole(square.shape), whole(vectors.shape), whole(head_row.shape), whole(bias.shape),
        ],
        out_specs=tuple(spec[kind] for _, kind in shapes),
        scratch_shapes=[
            pltpu.VMEM((6, 256, 128), F32),
            pltpu.VMEM(vectors.shape, F32),
            pltpu.VMEM((1, width), F32),
        ],
        compiler_params=pltpu.CompilerParams(vmem_limit_bytes=60 << 20),
        cost_estimate=pl.CostEstimate(flops=14_000_000_000, bytes_accessed=60_000_000, transcendentals=5_000_000),
    )(memory_len, inputs, memory, square, vectors, head_row, bias)


ROOT_HALF = 0.7071067811865476
INVERSE_ROOT = 0.3989422804014327
CHUNK = 1024


def feed_kernel(
    lengths, h2_in, cot, tall, vec_in, feed_in,
    out, dh2, narrow, wide, dvec, dfeed,
    u, g, dr, total, vec, feed,
):
    step = pl.program_id(0)
    items = TOKENS // 128
    width = tall.shape[1]
    chunks = width // CHUNK

    @pl.when(step == 0)
    def _():
        vec[...] = vec_in[...].astype(F32)
        feed[...] = feed_in[...].astype(F32)
        dvec[...] = jnp.zeros_like(dvec)
        dfeed[...] = jnp.zeros_like(dfeed)

    h2 = h2_in[...]
    narrow[0] = norm(h2, vec[14:15], vec[15:16]).astype(BF16)

    def at(i):
        return pl.ds(pl.multiple_of(i * CHUNK, CHUNK), CHUNK)

    def first(i, total):
        some = at(i)
        inner = times_back(narrow[0], tall[0, some]) + feed[0:1, some]
        bell = 0.5 + 0.5 * lax.erf(inner * ROOT_HALF)
        active = inner * bell
        g[:, some] = active
        u[:, some] = bell + inner * (jnp.exp(-0.5 * inner * inner) * INVERSE_ROOT)
        return total + jnp.sum(active, axis=-1, keepdims=True)

    zero = jnp.zeros((TOKENS, 1), F32)
    mean = lax.fori_loop(0, chunks, first, zero, unroll=True) * (1.0 / width)

    def second(i, total):
        center = g[:, at(i)] - mean
        return total + jnp.sum(center * center, axis=-1, keepdims=True)

    spread = lax.fori_loop(0, chunks, second, zero, unroll=True) * (1.0 / width)
    scale = lax.rsqrt(spread + NORM_EPSILON)
    row = lax.broadcasted_iota(jnp.int32, (128, 1), 0)
    valid = jnp.concatenate(
        [jnp.where(row < lengths[step * items + item], 1.0, 0.0) for item in range(items)], axis=0
    )
    dy32 = cot[...].astype(F32) * valid
    narrow[1] = dy32.astype(BF16)
    total[...] = h2 + vec[16:17]

    def third(i, sums):
        some = at(i)
        hat = (g[:, some] - mean) * scale
        g[:, some] = hat
        gain = feed[1:2, some]
        active = (hat * gain + feed[2:3, some]).astype(BF16)
        wide[1, :, some] = active
        total[...] += times(active, tall[1, some])
        slope = times_back(narrow[1], tall[1, some])
        dfeed[1:2, some] += down(slope * hat)
        dfeed[2:3, some] += down(slope)
        inner = slope * gain
        dr[:, some] = inner
        return (
            sums[0] + jnp.sum(inner, axis=-1, keepdims=True),
            sums[1] + jnp.sum(inner * hat, axis=-1, keepdims=True),
        )

    one, two = lax.fori_loop(0, chunks, third, (zero, zero), unroll=True)
    out[...] = total[...].astype(BF16)
    one, two = one * (1.0 / width), two * (1.0 / width)
    dh2[...] = jnp.zeros_like(dh2)

    def fourth(i, carry):
        some = at(i)
        back = scale * (dr[:, some] - one - g[:, some] * two)
        slope = (back * u[:, some]).astype(BF16)
        wide[0, :, some] = slope
        dfeed[0:1, some] += down(slope.astype(F32))
        dh2[...] += times(slope, tall[0, some])
        return carry

    lax.fori_loop(0, chunks, fourth, 0, unroll=True)
    back, gain_sum, shift_sum = norm_back(h2, dh2[...], vec[14:15])
    dvec[0:1] += gain_sum
    dvec[1:2] += shift_sum
    dvec[2:3] += down(dy32)
    dh2[...] = dy32 + back


def feed_both(hidden, cotangent, lengths, tall, vectors, feed_vectors):
    tokens, width = hidden.shape
    wide = tall.shape[1]
    steps = tokens // TOKENS
    some = by_rows(TOKENS, width)
    return pl.pallas_call(
        feed_kernel,
        grid=(steps,),
        out_shape=(
            jax.ShapeDtypeStruct((tokens, width), BF16),
            jax.ShapeDtypeStruct((tokens, width), F32),
            jax.ShapeDtypeStruct((2, tokens, width), BF16),
            jax.ShapeDtypeStruct((2, tokens, wide), BF16),
            jax.ShapeDtypeStruct((3, width), F32),
            jax.ShapeDtypeStruct((3, wide), F32),
        ),
        in_specs=[
            pl.BlockSpec(memory_space=pltpu.SMEM),
            some, some, whole(tall.shape), whole(vectors.shape), whole(feed_vectors.shape),
        ],
        out_specs=(
            some, some, by_blocks(2, TOKENS, width), by_blocks(2, TOKENS, wide),
            pl.BlockSpec((3, width), lambda i: (0, 0)),
            pl.BlockSpec((3, wide), lambda i: (0, 0)),
        ),
        scratch_shapes=[pltpu.VMEM((TOKENS, wide), F32)] * 3
        + [
            pltpu.VMEM((TOKENS, width), F32),
            pltpu.VMEM(vectors.shape, F32),
            pltpu.VMEM(feed_vectors.shape, F32),
        ],
        compiler_params=pltpu.CompilerParams(vmem_limit_bytes=60 << 20),
        cost_estimate=pl.CostEstimate(flops=20_000_000_000, bytes_accessed=40_000_000, transcendentals=7_000_000),
    )(lengths, hidden, cotangent, tall, vectors, feed_vectors)


def attention_back_kernel(
    x_in, dh2, w, vec_in, scales,
    q, k, v, p, o, h1, cq, ck, cv, pc, co,
    dx, dmem, right, far, dvec, drel,
    do, dh1, dbias, vec, hs,
):
    step = pl.program_id(0)
    masks = head_masks()
    items = TOKENS // 128
    slots = SLOTS // items

    @pl.when(step == 0)
    def _():
        vec[...] = vec_in[...].astype(F32)
        hs[...] = spread_heads(scales[...])
        dvec[...] = jnp.zeros_like(dvec)
        dbias[...] = jnp.zeros_like(dbias)

    def note(row, value):
        dvec[row : row + 1] += value

    right[5] = dh2[...].astype(BF16)
    note(11, down(right[5].astype(F32)))
    back, gain_sum, shift_sum = norm_back(co[...], times_back(right[5], w[7]), vec[12:13])
    note(12, gain_sum)
    note(13, shift_sum)
    do[...] = back.astype(BF16)

    def through(pair, item, keys, query, key, value, weights, dquery, dkey, dvalue, with_bias):
        lanes = pl.ds(pl.multiple_of(pair * LANES, LANES), LANES)
        rows = slice(item * 128, item * 128 + 128)
        kept = weights[item, pair]
        grad = stacked(do[rows, lanes], masks)
        dvalue[keys, lanes] = down_to_keys(kept, grad)
        slope = soften_back(kept, times_back(grad, value[keys, lanes]))
        dquery[rows, lanes] = (
            times(side_by_side(slope), stacked(key[keys, lanes], masks)).astype(BF16) * 0.125
        ).astype(BF16)
        dkey[keys, lanes] = down_to_keys(slope, stacked(query[rows, lanes], masks))
        if with_bias:
            dbias[pair] += slope.astype(F32)

    @pl.loop(0, 6, unroll=True)
    def _(pair):
        for item in range(items):
            keys = slice(item * slots, item * slots + slots)
            through(pair, item, keys, cq, ck, cv, pc, right.at[4], far.at[0], far.at[1], False)

    note(9, down(right[4].astype(F32)))
    note(10, down(far[1].astype(F32)))
    dmem[...] = (times_back(far[0], w[5]) + times_back(far[1], w[6])).astype(BF16)
    back, gain_sum, shift_sum = norm_back(h1[...], times_back(right[4], w[4]), vec[7:8])
    note(7, gain_sum)
    note(8, shift_sum)
    dh1[...] = dh2[...] + back
    right[3] = dh1[...].astype(BF16)
    note(4, down(right[3].astype(F32)))
    back, gain_sum, shift_sum = norm_back(o[...] * hs[...], times_back(right[3], w[3]), vec[5:6])
    note(5, gain_sum)
    note(6, shift_sum)
    note(17, down(back * o[...]))
    do[...] = (back * hs[...]).astype(BF16)

    @pl.loop(0, 6, unroll=True)
    def _(pair):
        for item in range(items):
            rows = slice(item * 128, item * 128 + 128)
            through(pair, item, rows, q, k, v, p, right.at[0], right.at[1], right.at[2], True)

    note(2, down(right[0].astype(F32)))
    note(3, down(right[2].astype(F32)))
    slope = times_back(right[0], w[0]) + times_back(right[1], w[1]) + times_back(right[2], w[2])
    back, gain_sum, shift_sum = norm_back(x_in[...].astype(F32), slope, vec[0:1])
    note(0, gain_sum)
    note(1, shift_sum)
    dx[...] = (dh1[...] + back).astype(BF16)

    @pl.when(step == pl.num_programs(0) - 1)
    def _():
        row = lax.broadcasted_iota(jnp.int32, (128, 128), 0)
        column = lax.broadcasted_iota(jnp.int32, (128, 128), 1)
        mirror = jnp.where(row + column == 127, 1.0, 0.0).astype(BF16)
        for head in range(12):
            part = dbias[head // 2, (head % 2) * 128 : (head % 2) * 128 + 128]
            high = part.astype(BF16)
            rest = part - high.astype(F32)
            middle = rest.astype(BF16)
            low = (rest - middle.astype(F32)).astype(BF16)
            flipped = times(high, mirror) + times(middle, mirror) + times(low, mirror)
            drel[head : head + 1] = down(pltpu.roll(flipped, 0, 1, stride=1, stride_axis=0))


def attention_backward(inputs, dh2, square, vectors, head_row, kept):
    tokens, width = inputs.shape
    q, k, v, p, o, h1, cq, ck, cv, pc, co = kept
    steps = tokens // TOKENS
    items = TOKENS // 128
    slots = ck.shape[0]
    t, m = by_rows(TOKENS, width), by_rows(SLOTS, width)
    ps, cs = by_items(items, 6, 256, 128), by_items(items, 6, 256, SLOTS // items)
    token = jax.ShapeDtypeStruct((tokens, width), BF16)
    slot = jax.ShapeDtypeStruct((slots, width), BF16)
    return pl.pallas_call(
        attention_back_kernel,
        grid=(steps,),
        out_shape=(
            token, slot,
            jax.ShapeDtypeStruct((6, tokens, width), BF16),
            jax.ShapeDtypeStruct((2, slots, width), BF16),
            jax.ShapeDtypeStruct((18, width), F32),
            jax.ShapeDtypeStruct((12, 128), F32),
        ),
        in_specs=[
            t, t, whole(square.shape), whole(vectors.shape), whole(head_row.shape),
            t, t, t, ps, t, t, t, m, m, cs, t,
        ],
        out_specs=(
            t, m, by_blocks(6, TOKENS, width), by_blocks(2, SLOTS, width),
            pl.BlockSpec((18, width), lambda i: (0, 0)),
            pl.BlockSpec((12, 128), lambda i: (0, 0)),
        ),
        scratch_shapes=[
            pltpu.VMEM((TOKENS, width), BF16),
            pltpu.VMEM((TOKENS, width), F32),
            pltpu.VMEM((6, 256, 128), F32),
            pltpu.VMEM(vectors.shape, F32),
            pltpu.VMEM((1, width), F32),
        ],
        compiler_params=pltpu.CompilerParams(vmem_limit_bytes=60 << 20),
        cost_estimate=pl.CostEstimate(flops=16_000_000_000, bytes_accessed=60_000_000, transcendentals=0),
    )(inputs, dh2, square, vectors, head_row, q, k, v, p, o, h1, cq, ck, cv, pc, co)


def slope_kernel(left, right, memory, far, out):
    step = pl.program_id(0)
    width = out.shape[1]

    def product(from_left, from_right):
        @pl.loop(0, width // 256)
        def _(tile):
            some = pl.ds(pl.multiple_of(tile * 256, 256), 256)
            out[0, some] = times_down(from_left[:, some], from_right[...]).astype(BF16)

    @pl.when(step < 6)
    def _():
        product(left.at[0], right.at[0])

    @pl.when(step >= 6)
    def _():
        product(memory, far.at[0])


def square_slopes(left, right, memory, far):
    _, tokens, width = left.shape
    slots = memory.shape[0]
    return pl.pallas_call(
        slope_kernel,
        grid=(8,),
        out_shape=jax.ShapeDtypeStruct((8, width, width), BF16),
        in_specs=[
            pl.BlockSpec((1, tokens, width), lambda g: (jnp.clip(g - 2, 0, 3), 0, 0)),
            pl.BlockSpec((1, tokens, width), lambda g: (jnp.minimum(g, 5), 0, 0)),
            whole(memory.shape),
            pl.BlockSpec((1, slots, width), lambda g: (jnp.maximum(g - 6, 0), 0, 0)),
        ],
        out_specs=pl.BlockSpec(
            (1, width, width),
            lambda g: (jnp.where(g < 5, g, jnp.where(g == 5, 7, g - 1)), 0, 0),
        ),
        compiler_params=pltpu.CompilerParams(vmem_limit_bytes=60 << 20),
        cost_estimate=pl.CostEstimate(flops=12_000_000_000, bytes_accessed=30_000_000, transcendentals=0),
    )(left, right, memory, far)


AXES = ("tall", "square", "row")
MESH = pl.DeviceIdType.MESH


def place():
    z, plane, core = lax.axis_index("tall"), lax.axis_index("square"), lax.axis_index("row")
    return z, lax.div(plane, 2), lax.rem(plane, 2), core


def device(z, y, x, core):
    return (z, y * 2 + x, core)


def greet(partners):
    barrier = pltpu.get_barrier_semaphore()
    for partner in partners:
        pl.semaphore_signal(barrier, inc=1, device_id=partner, device_id_type=MESH)
    pl.semaphore_wait(barrier, len(partners))


def small_tiles(arrays):
    places, at = [], 0
    for array in arrays:
        for tile in range(array.shape[1] // 128):
            places.append((array, at, tile))
            at += array.shape[0]
    return places


def reduce_kernel(groups, has_small, *refs):
    n = len(groups)
    ins, refs = refs[:n], refs[n:]
    small_in, refs = refs[:has_small], refs[has_small:]
    outs, refs = refs[:n], refs[n:]
    small_outs, refs = refs[:has_small], refs[has_small:]
    z, y, x, core = place()
    other = 1 - core
    sibling = device(z, y, x, other)
    across = {"x": device(z, y, 1 - x, core), "y": device(z, 1 - y, x, core)}
    along = [device(lax.rem(z + k, 4), y, x, core) for k in (1, 2, 3)]
    greet([sibling, across["x"], across["y"]] + along)
    mine = core * 384
    theirs = other * 384

    if has_small:
        small, held, total, refs = refs[0], refs[1], refs[2], refs[3:]
        small_send, small_recv, refs = refs[0], refs[1], refs[2:]

        side = small.shape[0] // 2
        own_rows = pl.ds(pl.multiple_of(core * side, 8), side)

        def small_copies(stage):
            def make(source, target, slot, partner):
                return pltpu.make_async_remote_copy(
                    source, target, small_send.at[slot], small_recv.at[slot],
                    device_id=partner, device_id_type=MESH,
                )

            if stage == 0:
                return [make(small, held.at[0], 0, sibling)]
            if stage < 3:
                source = total.at[stage - 1, own_rows]
                partner = across["x"] if stage == 1 else across["y"]
                return [make(source, held.at[stage, own_rows], stage, partner)]
            if stage == 3:
                source = total.at[2, own_rows]
                return [make(source, held.at[3 + z, own_rows], 3 + k, along[k]) for k in range(3)]
            return [make(total.at[3, own_rows], held.at[7, own_rows], 6, sibling)]

        small[...] = jnp.zeros_like(small)
        for source, at, tile in small_tiles(small_in):
            small[at : at + source.shape[0]] = source[:, tile * 128 : tile * 128 + 128]
        for copy in small_copies(0):
            copy.start()

        def small_step(stage):
            if stage < 4:
                for copy in small_copies(stage):
                    copy.wait_recv()
            if stage == 0:
                total[0] = small[...] + held[0]
            elif stage < 3:
                total[stage, own_rows] = total[stage - 1, own_rows] + held[stage, own_rows]
                if stage == 2:
                    held[3 + z, own_rows] = total[2, own_rows]
            elif stage == 3:
                total[3, own_rows] = (
                    (held[3, own_rows] + held[4, own_rows]) + held[5, own_rows]
                ) + held[6, own_rows]
            else:
                rest = pl.ds(pl.multiple_of(other * side, 8), side)
                pltpu.make_async_remote_copy(
                    total.at[3, rest], held.at[7, rest], small_send.at[6], small_recv.at[6],
                    device_id=sibling, device_id_type=MESH,
                ).wait_recv()
                held[7, own_rows] = total[3, own_rows]
                for target, at, tile in small_tiles(small_outs):
                    target[:, tile * 128 : tile * 128 + 128] = held[7, at : at + target.shape[0]]
            if stage < 4:
                for copy in small_copies(stage + 1):
                    copy.start()

    else:
        def small_step(stage):
            pass

    plans = []
    for g, (pieces, rows, width, parts) in enumerate(groups):
        r0, r1, r2, r3, f3, r4, send, recv = refs[8 * g : 8 * g + 8]
        plans.append((pieces, rows, width, parts, ins[g], outs[g], r0, r1, r2, r3, f3, r4, send, recv))

    def where(plan, order, i):
        pieces, parts, width = plan[0], plan[3], plan[2]
        j = i + order * (pieces // 2)
        return j, lax.div(j, parts), pl.multiple_of(lax.rem(j, parts) * width, 128)

    def copies(plan, stage, order, i):
        pieces, rows, width, parts, src, out, r0, r1, r2, r3, f3, r4, send, recv = plan
        j, matrix, column = where(plan, order, i)
        first = "xy"[order]

        def make(source, target, slot, partner):
            return pltpu.make_async_remote_copy(
                source, target, send.at[slot, j], recv.at[slot, j],
                device_id=partner, device_id_type=MESH,
            )

        if stage == 0:
            lanes = pl.ds(pl.multiple_of(theirs + column, 128), width)
            return [make(src.at[matrix, :, :, :, :, lanes], r0.at[j], 0, sibling)]
        if stage == 1:
            part = r0.at[j, :, :, 1 - x] if order == 0 else r0.at[j, :, 1 - y]
            return [make(part, r1.at[j], 1, across[first])]
        if stage == 2:
            part = r1.at[j, :, 1 - y] if order == 0 else r1.at[j, :, 1 - x]
            return [make(part, r2.at[j], 2, across["yx"[order]])]
        if stage == 3:
            return [
                make(r2.at[j, lax.rem(z + k + 1, 4)], r3.at[j, k], 3 + k, along[k])
                for k in range(3)
            ]
        share = rows // 2
        return [make(f3.at[j, pl.ds(pl.multiple_of(other * share, 8), share)], r4.at[j], 6, sibling)]

    f32 = jnp.float32

    def add(plan, stage, order, i):
        pieces, rows, width, parts, src, out, r0, r1, r2, r3, f3, r4, send, recv = plan
        j, matrix, column = where(plan, order, i)
        if stage == 0:
            lanes = pl.ds(pl.multiple_of(mine + column, 128), width)

            @pl.loop(0, 4)
            def _(a):
                r0[j, a] = (
                    r0[j, a].astype(f32) + src[matrix, a, :, :, :, lanes].astype(f32)
                ).astype(jnp.bfloat16)
        elif stage == 1:
            @pl.loop(0, 4)
            def _(a):
                own = r0[j, a, :, x] if order == 0 else r0[j, a, y]
                r1[j, a] = (r1[j, a].astype(f32) + own.astype(f32)).astype(jnp.bfloat16)
        elif stage == 2:
            @pl.loop(0, 4)
            def _(a):
                own = r1[j, a, y] if order == 0 else r1[j, a, x]
                r2[j, a] = (r2[j, a].astype(f32) + own.astype(f32)).astype(jnp.bfloat16)
        elif stage == 3:
            f3[j] = (r3[j, 0].astype(f32) + r3[j, 1].astype(f32)) + (
                r3[j, 2].astype(f32) + r2[j, z].astype(f32)
            )
        else:
            share = rows // 2
            lanes = pl.ds(pl.multiple_of(mine + column, 128), width)
            out[matrix, :, lanes] = f3[j, pl.ds(pl.multiple_of(core * share, 8), share)]
            lanes = pl.ds(pl.multiple_of(theirs + column, 128), width)
            out[matrix, :, lanes] = r4[j]

    def each(plan, body, turns):
        @pl.loop(0, turns)
        def _(i):
            for order in range(2):
                body(order, i)

    def start(plan, stage, turns):
        def body(order, i):
            for copy in copies(plan, stage, order, i):
                copy.start()

        each(plan, body, turns)

    def step(plan, stage, order, i):
        for copy in copies(plan, stage, order, i):
            copy.wait_recv()
        add(plan, stage, order, i)
        if stage < 4:
            for copy in copies(plan, stage + 1, order, i):
                copy.start()

    def finish(plan, stage):
        def body(order, i):
            for copy in copies(plan, stage, order, i):
                copy.wait_send()

        each(plan, body, plan[0] // 2)

    for plan in plans:
        start(plan, 0, 2)
    for plan in plans:
        turns = plan[0] // 2

        @pl.loop(0, turns + 4)
        def _(turn):
            @pl.when(turn < turns - 2)
            def _():
                for order in range(2):
                    for copy in copies(plan, 0, order, turn + 2):
                        copy.start()

            for stage in range(5):
                @pl.when((turn >= stage) & (turn < turns + stage))
                def _():
                    for order in range(2):
                        step(plan, stage, order, turn - stage)

            if plan is plans[0]:
                for stage in range(5):
                    @pl.when(turn == stage)
                    def _():
                        small_step(stage)

    for stage in range(5):
        for plan in plans:
            finish(plan, stage)
    if has_small:
        for stage in range(5):
            for copy in small_copies(stage):
                copy.wait_send()


def reduce_scatter(arrays, small, collective_id, split=1):
    groups, views, outs, scratch = [], [], [], []
    bf16, f32 = jnp.bfloat16, jnp.float32
    if small:
        last = small_tiles(small)[-1]
        lines = -(-(last[1] + last[0].shape[0]) // 16) * 16
        scratch += [
            pltpu.VMEM((lines, 128), f32),
            pltpu.VMEM((8, lines, 128), f32),
            pltpu.VMEM((4, lines, 128), f32),
            pltpu.SemaphoreType.DMA((7,)),
            pltpu.SemaphoreType.DMA((7,)),
        ]
    for array in arrays:
        matrices, height, width_all = array.shape
        rows = height // 16
        parts = 3 if matrices == 2 else split
        pieces, width = matrices * parts, 384 // parts
        groups.append((pieces, rows, width, parts))
        views.append(array.reshape(matrices, 4, 2, 2, rows, width_all))
        outs.append(jax.ShapeDtypeStruct((matrices, rows // 2, width_all), f32))
        scratch += [
            pltpu.VMEM((pieces, 4, 2, 2, rows, width), bf16),
            pltpu.VMEM((pieces, 4, 2, rows, width), bf16),
            pltpu.VMEM((pieces, 4, rows, width), bf16),
            pltpu.VMEM((pieces, 3, rows, width), bf16),
            pltpu.VMEM((pieces, rows, width), f32),
            pltpu.VMEM((pieces, rows // 2, width), f32),
            pltpu.SemaphoreType.DMA((7, pieces)),
            pltpu.SemaphoreType.DMA((7, pieces)),
        ]
    for array in small:
        views.append(array)
        outs.append(jax.ShapeDtypeStruct(array.shape, f32))
    vmem = pl.BlockSpec(memory_space=pltpu.VMEM)
    return pl.pallas_call(
        functools.partial(reduce_kernel, tuple(groups), len(small)),
        out_shape=tuple(outs),
        in_specs=[vmem] * len(views),
        out_specs=tuple([vmem] * len(outs)),
        scratch_shapes=scratch,
        compiler_params=pltpu.CompilerParams(
            collective_id=collective_id, has_side_effects=True, vmem_limit_bytes=60 << 20
        ),
    )(*views)


def gather_kernel(split, own, full, theirs, send, recv):
    z, y, x, core = place()
    other = 1 - core
    sibling = device(z, y, x, other)
    across = {"x": device(z, y, 1 - x, core), "y": device(z, 1 - y, x, core)}
    along = [device(lax.rem(z + k, 4), y, x, core) for k in (1, 2, 3)]
    greet([sibling, across["x"], across["y"]] + along)
    matrices, share, width = own.shape
    half = width // 2
    pieces, thin = matrices * split, half // split

    def spot(j):
        column = lax.rem(j, split) * thin
        return (
            lax.div(j, split),
            pl.ds(pl.multiple_of(core * half + column, 128), thin),
            pl.ds(pl.multiple_of(other * half + column, 128), thin),
        )

    def make(source, target, slot, j, partner):
        return pltpu.make_async_remote_copy(
            source, target, send.at[slot, j], recv.at[slot, j], device_id=partner, device_id_type=MESH
        )

    def copies(stage, order, i):
        j = i + order * (pieces // 2)
        m, mine, rest = spot(j)
        first = "yx"[order]
        if stage == 0:
            return [make(own.at[m, :, rest], theirs.at[j], 0, j, sibling)]
        if stage == 1:
            part = full.at[m, z, y, x, :, mine]
            return [make(part, part, 1 + k, j, along[k]) for k in range(3)]
        if stage == 2:
            part = full.at[m, :, y, x, :, mine]
            return [make(part, part, 4, j, across[first])]
        if stage == 3:
            part = full.at[m, :, :, x, :, mine] if order == 0 else full.at[m, :, y, :, :, mine]
            return [make(part, part, 5, j, across["xy"[order]])]
        part = full.at[m, :, :, :, :, mine]
        return [make(part, part, 6, j, sibling)]

    def each(body):
        @pl.loop(0, pieces // 2)
        def _(i):
            for order in range(2):
                body(order, i)

    def start(stage):
        def body(order, i):
            for copy in copies(stage, order, i):
                copy.start()

        each(body)

    def step(stage, order, i):
        for copy in copies(stage, order, i):
            copy.wait_recv()
        if stage == 0:
            j = i + order * (pieces // 2)
            m, mine, _ = spot(j)

            @pl.when(core == 0)
            def _():
                full[m, z, y, x, :, mine] = jnp.concatenate(
                    [own[m, :, mine], theirs[j]], axis=0
                ).astype(jnp.bfloat16)

            @pl.when(core == 1)
            def _():
                full[m, z, y, x, :, mine] = jnp.concatenate(
                    [theirs[j], own[m, :, mine]], axis=0
                ).astype(jnp.bfloat16)
        if stage < 4:
            for copy in copies(stage + 1, order, i):
                copy.start()

    def finish(stage):
        def body(order, i):
            for copy in copies(stage, order, i):
                copy.wait_send()

        each(body)

    start(0)
    turns = pieces // 2

    @pl.loop(0, turns + 4)
    def _(turn):
        for stage in range(5):
            @pl.when((turn >= stage) & (turn < turns + stage))
            def _():
                for order in range(2):
                    step(stage, order, turn - stage)

    for stage in range(5):
        finish(stage)


def gather_rows(own, collective_id, split=1):
    matrices, share, width = own.shape
    pieces = matrices * split
    vmem = pl.BlockSpec(memory_space=pltpu.VMEM)
    full = pl.pallas_call(
        functools.partial(gather_kernel, split),
        out_shape=jax.ShapeDtypeStruct((matrices, 4, 2, 2, 2 * share, width), jnp.bfloat16),
        in_specs=[vmem],
        out_specs=vmem,
        scratch_shapes=[
            pltpu.VMEM((pieces, share, width // 2 // split), jnp.float32),
            pltpu.SemaphoreType.DMA((7, pieces)),
            pltpu.SemaphoreType.DMA((7, pieces)),
        ],
        compiler_params=pltpu.CompilerParams(
            collective_id=collective_id, has_side_effects=True, vmem_limit_bytes=32 << 20
        ),
    )(own)
    return full.reshape(matrices, 32 * share, width)


def gram_kernel(gram, out, other_sum, half_a, half_b, final, send, recv):
    z, y, x, core = place()
    sibling = device(z, y, x, 1 - core)
    x_side, y_side = device(z, y, 1 - x, core), device(z, 1 - y, x, core)
    greet([sibling, x_side, y_side])
    side = gram.shape[0] // 2
    rows = pl.ds(pl.multiple_of(core * side, 8), side)
    rest = pl.ds(pl.multiple_of((1 - core) * side, 8), side)

    def send_to(source, target, slot, partner):
        return pltpu.make_async_remote_copy(
            source, target, send.at[slot], recv.at[slot], device_id=partner, device_id_type=MESH
        )

    first = send_to(gram.at[rest], other_sum.at[rest], 0, sibling)
    second = send_to(gram.at[rows], other_sum.at[rows], 1, sibling)
    first.start()
    second.start()
    mine = send_to(gram.at[rows], other_sum.at[rows], 0, sibling)
    mine.wait_recv()
    out[rows] = gram[rows] + other_sum[rows]
    theirs = send_to(gram.at[rest], other_sum.at[rest], 1, sibling)
    theirs.wait_recv()

    @pl.when(z < 2)
    def _():
        out[rest] = gram[rest] + other_sum[rest]

    @pl.when(z >= 2)
    def _():
        def pair(one, two):
            step = send_to(out.at[rows], half_a, 2, one)
            step.start()
            step.wait_recv()
            step.wait_send()
            half_b[...] = out[rows] + half_a[...]
            step = send_to(half_b, final, 3, two)
            step.start()
            step.wait_recv()
            out[rows] = half_b[...] + final[...]
            step.wait_send()

        @pl.when(core == 0)
        def _():
            pair(x_side, y_side)

        @pl.when(core == 1)
        def _():
            pair(y_side, x_side)

        last = send_to(out.at[rows], out.at[rows], 4, sibling)
        last.start()
        arrive = send_to(out.at[rest], out.at[rest], 4, sibling)
        arrive.wait_recv()
        last.wait_send()

    first.wait_send()
    second.wait_send()


def gram_sum(gram, collective_id):
    f32 = jnp.float32
    side = gram.shape[0] // 2
    vmem = pl.BlockSpec(memory_space=pltpu.VMEM)
    return pl.pallas_call(
        gram_kernel,
        out_shape=jax.ShapeDtypeStruct(gram.shape, f32),
        in_specs=[vmem],
        out_specs=vmem,
        scratch_shapes=[
            pltpu.VMEM(gram.shape, f32),
            pltpu.VMEM((side, gram.shape[1]), f32),
            pltpu.VMEM((side, gram.shape[1]), f32),
            pltpu.VMEM((side, gram.shape[1]), f32),
            pltpu.SemaphoreType.DMA((5,)),
            pltpu.SemaphoreType.DMA((5,)),
        ],
        compiler_params=pltpu.CompilerParams(
            collective_id=collective_id, has_side_effects=True, vmem_limit_bytes=32 << 20
        ),
    )(gram)


SIDE = 256


def sweep_kernel(packed, rows, out, gram, held, now, poly, step):
    blocks = gram.shape[0] // SIDE
    width = blocks * SIDE

    def put(target, a, values):
        for b in range(a, blocks):
            block = values[:, (b - a) * SIDE : (b - a) * SIDE + SIDE]
            for i, j, piece in ((a, b, block),) if a == b else ((a, b, block), (b, a, block.T)):
                columns = slice(j * SIDE, j * SIDE + SIDE)
                top = piece.astype(BF16)
                target[i * SIDE : i * SIDE + SIDE, columns] = top
                target[width + i * SIDE : width + i * SIDE + SIDE, columns] = (
                    piece - top.astype(F32)
                ).astype(BF16)
                target[2 * width + i * SIDE : 2 * width + i * SIDE + SIDE, columns] = top

    def exact(left, a, right):
        high = left[a * SIDE : a * SIDE + SIDE]
        low = left[width + a * SIDE : width + a * SIDE + SIDE]
        return times(jnp.concatenate([high, high, low], axis=1), right[:, a * SIDE :])

    index, trace = 0, jnp.zeros((1, 1), F32)
    row = lax.broadcasted_iota(jnp.int32, (SIDE, SIDE), 0)
    column = lax.broadcasted_iota(jnp.int32, (SIDE, SIDE), 1)
    unit = jnp.where(row == column, 1.0, 0.0)
    for a in range(blocks):
        for b in range(a, blocks):
            block = packed[index * SIDE : index * SIDE + SIDE]
            gram[a * SIDE : a * SIDE + SIDE, b * SIDE : b * SIDE + SIDE] = block
            if a == b:
                trace = trace + jnp.sum(
                    jnp.sum(block * unit, axis=1, keepdims=True), axis=0, keepdims=True
                )
            else:
                gram[b * SIDE : b * SIDE + SIDE, a * SIDE : a * SIDE + SIDE] = block.T
            index += 1
    scale = 1.0 / (jnp.sqrt(trace) + FLOOR_EPSILON)

    for a in range(blocks):
        put(now, a, gram[a * SIDE : a * SIDE + SIDE, a * SIDE :] * (scale * scale))
    count = rows.shape[0]

    def keep(some, rest, values):
        top = values.astype(BF16)
        held[some] = top
        held[rest] = (values - top.astype(F32)).astype(BF16)

    keep(slice(0, count), slice(count, 2 * count), rows[...].astype(F32) * scale)

    @pl.loop(0, ITERS)
    def _(sweep):
        for a in range(blocks):
            row = lax.broadcasted_iota(jnp.int32, (SIDE, width - a * SIDE), 0)
            column = lax.broadcasted_iota(jnp.int32, (SIDE, width - a * SIDE), 1)
            lines = slice(a * SIDE, a * SIDE + SIDE)
            below = slice(width + a * SIDE, width + a * SIDE + SIDE)
            values = exact(now, a, now) * THIRD_TERM + SECOND_TERM * (
                now[lines, a * SIDE :].astype(F32) + now[below, a * SIDE :].astype(F32)
            )
            put(poly, a, jnp.where(row == column, values + FIRST_TERM, values))

        @pl.loop(0, count // 128)
        def _(a):
            some = pl.ds(pl.multiple_of(a * 128, 128), 128)
            rest = pl.ds(pl.multiple_of(a * 128 + count, 128), 128)
            high, low = held[some], held[rest]
            keep(some, rest, times(jnp.concatenate([high, high, low], axis=1), poly[...]))

        @pl.when(sweep < ITERS - 1)
        def _():
            for a in range(blocks):
                put(step, a, exact(now, a, poly))
            for a in range(blocks):
                put(now, a, exact(step, a, poly))

    out[...] = held[0:count]


def sweeps(packed, rows):
    width = rows.shape[1]
    vmem = pl.BlockSpec(memory_space=pltpu.VMEM)
    part = pltpu.VMEM((3 * width, width), BF16)
    return pl.pallas_call(
        sweep_kernel,
        out_shape=jax.ShapeDtypeStruct(rows.shape, BF16),
        in_specs=[vmem, vmem],
        out_specs=vmem,
        scratch_shapes=[
            pltpu.VMEM((width, width), F32),
            pltpu.VMEM((2 * rows.shape[0], width), BF16),
        ]
        + [part] * 3,
        compiler_params=pltpu.CompilerParams(vmem_limit_bytes=48 << 20),
        cost_estimate=pl.CostEstimate(flops=40_000_000_000, bytes_accessed=5_000_000, transcendentals=0),
    )(packed, rows)


def upper_blocks(gram):
    blocks = gram.shape[0] // SIDE
    return jnp.concatenate(
        [
            gram[a * SIDE : a * SIDE + SIDE, b * SIDE : b * SIDE + SIDE]
            for a in range(blocks)
            for b in range(a, blocks)
        ],
        axis=0,
    )


def matmul3(left, right):
    return jnp.matmul(left, right, precision=lax.Precision.HIGH)


def to_owner_rows(square_state, tall_state, count):
    rows = square_state.shape[1]
    group = count // 16
    if rows % group == 0:
        piece = rows // group
        pieces = jnp.concatenate(
            [
                square_state.reshape(8 * group, piece, D),
                tall_state.reshape(8 * group, piece, D),
            ],
            axis=0,
        ).astype(jnp.bfloat16)
        return lax.all_to_all(pieces, AXES, 0, 0, tiled=True).reshape(count * piece, D)
    square_all = lax.all_gather(square_state.astype(jnp.bfloat16), AXES, axis=1, tiled=True)
    tall_all = lax.all_gather(tall_state.astype(jnp.bfloat16), AXES, axis=1, tiled=True)
    joined = jnp.concatenate([square_all.reshape(-1, D), tall_all.reshape(-1, D)], axis=0)
    own = joined.shape[0] // count
    return lax.dynamic_slice_in_dim(joined, lax.axis_index(AXES) * own, own, axis=0)


def from_owner_rows(rows_out, count, square_rows, tall_rows):
    group = count // 16
    rows_out = rows_out.astype(jnp.bfloat16)
    if square_rows % group == 0:
        piece = square_rows // group
        back = lax.all_to_all(rows_out.reshape(count, piece, D), AXES, 0, 0, tiled=True)
        return (
            back[: 8 * group].reshape(8, square_rows, D),
            back[8 * group :].reshape(2, tall_rows, D),
        )
    joined = lax.all_gather(rows_out, AXES, axis=0, tiled=True)
    square_all = joined[: 8 * square_rows * count].reshape(8, square_rows * count, D)
    tall_all = joined[8 * square_rows * count :].reshape(2, tall_rows * count, D)
    index = lax.axis_index(AXES)
    return (
        lax.dynamic_slice_in_dim(square_all, index * square_rows, square_rows, axis=1),
        lax.dynamic_slice_in_dim(tall_all, index * tall_rows, tall_rows, axis=1),
    )


def orthogonal_rows(rows_in, kernels):
    gram = lax.dot_general(
        rows_in, rows_in, (((0,), (0,)), ((), ())), preferred_element_type=jnp.float32
    )
    if kernels:
        return sweeps(gram_sum(upper_blocks(gram), 2), rows_in)
    rows_in = rows_in.astype(jnp.float32)
    gram = lax.psum(gram, "row")
    is_tall = lax.axis_index("tall") >= 2
    gram = jnp.where(is_tall, lax.psum(jnp.where(is_tall, gram, 0.0), "square"), gram)
    eye = (jnp.arange(D)[:, None] == jnp.arange(D)[None, :]).astype(jnp.float32)
    scale = 1.0 / (jnp.sqrt(jnp.sum(gram * eye)) + FLOOR_EPSILON)
    gram = gram * (scale * scale)
    current = rows_in * scale

    for sweep in range(ITERS):
        poly = FIRST_TERM * eye + SECOND_TERM * gram + THIRD_TERM * matmul3(gram, gram)
        current = matmul3(current, poly)
        if sweep < ITERS - 1:
            gram = matmul3(matmul3(gram, poly), poly)
    return current


def local(
    inputs,
    memory,
    cotangent,
    lengths,
    memory_len,
    square_master,
    tall_master,
    square_momentum,
    tall_momentum,
    vectors,
    feed_vectors,
    head_scale,
    relative,
):
    count = lax.axis_size(AXES)
    kernels = count == 32
    index = lax.axis_index(AXES)
    if kernels:
        square_copy = gather_rows(square_master, 3, 3)
    else:
        square_copy = lax.all_gather(
            square_master.astype(jnp.bfloat16), AXES, axis=1, tiled=True
        )
    tall_copy = lax.all_gather(tall_master.astype(jnp.bfloat16), AXES, axis=1, tiled=True)
    width = inputs.shape[2]
    head_row = head_scale[None]
    flat_in, flat_memory = inputs.reshape(-1, width), memory.reshape(-1, width)
    left, q, k, v, p, o, h1, cq, ck, cv, pc, co, h2 = attention_forward(
        flat_in, flat_memory, memory_len, square_copy, vectors, head_row, relative
    )
    output, dh2, narrow, wide, late_slope, feed_slope = feed_both(
        h2, cotangent.reshape(-1, width), lengths, tall_copy, vectors, feed_vectors
    )

    tall_slope = jnp.einsum("btf,btd->bfd", wide, narrow, preferred_element_type=F32).astype(BF16)
    tall_slope, dh2 = lax.optimization_barrier((tall_slope, dh2))
    tall_sum = lax.psum_scatter(tall_slope, AXES, scatter_dimension=1, tiled=True).astype(F32)
    input_slope, memory_slope, right, far, early_slope, bias_slope = attention_backward(
        flat_in, dh2, square_copy, vectors, head_row, (q, k, v, p, o, h1, cq, ck, cv, pc, co)
    )
    square_slope = square_slopes(left, right, flat_memory, far)
    small = [
        jnp.full((1, 128), jnp.sum(lengths).astype(F32)),
        early_slope,
        late_slope,
        feed_slope,
        bias_slope,
    ]
    if kernels:
        square_sum, *small = reduce_scatter([square_slope], small, 1)
    else:
        square_sum = lax.psum_scatter(
            square_slope, AXES, scatter_dimension=1, tiled=True
        ).astype(jnp.float32)
        small = lax.psum(small, AXES)
    total, early_sum, late_sum, feed_sum, bias_sum = small
    total = total[0, :1]
    vector_sum = jnp.concatenate([early_sum[:14], late_sum], axis=0)
    scale_sum = jnp.sum(early_sum[17].reshape(head_scale.shape[0], -1), axis=1)
    bias_sum = jnp.roll(bias_sum, 1, axis=1)
    factor = inputs.shape[0] * count / total[0]
    width = vector_sum.shape[1] // count
    vector_sum = lax.dynamic_slice_in_dim(
        vector_sum, index * width, width, axis=1
    )
    width = feed_slope.shape[1] // count
    feed_sum = lax.dynamic_slice_in_dim(
        feed_sum, index * width, width, axis=1
    )
    square_state = MOMENTUM_DECAY * square_momentum + factor * square_sum
    tall_state = MOMENTUM_DECAY * tall_momentum + factor * tall_sum
    rows_out = orthogonal_rows(to_owner_rows(square_state, tall_state, count), kernels)
    square, tall = from_owner_rows(
        rows_out, count, square_state.shape[1], tall_state.shape[1]
    )
    square, tall = square.astype(jnp.float32), tall.astype(jnp.float32)
    square_weight = square_master * (1.0 - LEARN_RATE * WEIGHT_DECAY) - LEARN_RATE * square
    tall_weight = (
        tall_master * (1.0 - LEARN_RATE * WEIGHT_DECAY)
        - LEARN_RATE * max(1.0, FF / D) ** 0.5 * tall
    )
    return (
        output.reshape(inputs.shape),
        input_slope.reshape(inputs.shape),
        memory_slope.reshape(memory.shape),
        square_state,
        tall_state,
        square_weight,
        tall_weight,
        factor * vector_sum,
        factor * feed_sum,
        factor * scale_sum,
        factor * bias_sum,
    )


def solution(mesh):
    count = mesh.devices.size
    grouped = Mesh(mesh.devices.reshape(4, 4, count // 16), AXES)
    placed = (
        P(AXES, None, None),
        P(AXES, None, None),
        P(AXES, None, None),
        P(AXES),
        P(AXES),
        P(None, AXES, None),
        P(None, AXES, None),
        P(None, AXES, None),
        P(None, AXES, None),
        P(),
        P(),
        P(),
        P(),
    )
    return jax.shard_map(
        local,
        mesh=grouped,
        in_specs=placed,
        out_specs=(
            P(AXES, None, None),
            P(AXES, None, None),
            P(AXES, None, None),
            P(None, AXES, None),
            P(None, AXES, None),
            P(None, AXES, None),
            P(None, AXES, None),
            P(None, AXES),
            P(None, AXES),
            P(),
            P(),
        ),
        check_vma=False,
    )
```
